256 devices in a mesh: depth: 8 (over y, core), lat: 32 (over x, z).
Axes of the slice: x: 4, y: 4, z: 8, core: 2. Of those that a mesh axis runs over, the one named last changes fastest.
Arguments:
- volume: float32 [256, 512, 128], P('depth', 'lat'), may hold values from -6 to 6
Outputs:
- diffused: float32 [256, 512, 128], P('depth', 'lat')
The draws below stay inside these ranges and needn't reach their ends.
All inputs are finite; a program needn't handle non-finite values.
Results may differ from the reference program's by a relative error of at most 0.0003.
Values sent between devices are 32-bit elements; how exact they have to be, the bound alone decides.
No kernel may reach another device: no remote copies, remote signals or barrier semaphores. Data moves between devices by JAX's collectives and lax.ppermute only.
A program may use at most 64 MiB of HBM per device.

```python
import math
import jax
import jax.numpy as jnp
from jax import lax

NX = 128
NY = 512
NZ = 256


def draw_volume(key, part):
    key_freq, key_phase, key_noise = jax.random.split(key, 3)
    depth_pos = (jnp.arange(NZ, dtype=jnp.float32) / NZ)[:, None, None]
    row_pos = (jnp.arange(NY, dtype=jnp.float32) / NY)[None, :, None]
    column_pos = (jnp.arange(NX, dtype=jnp.float32) / NX)[None, None, :]
    frequencies = jax.random.uniform(key_freq, (3, 3), jnp.float32, 0.5, 2.5)
    phases = jax.random.uniform(key_phase, (3,), jnp.float32, 0.0, 2.0 * math.pi)
    smooth_part = jnp.zeros((NZ, NY, NX), jnp.float32)
    for index in range(3):
        angle_sum = frequencies[index, 0] * depth_pos + frequencies[index, 1] * row_pos + frequencies[index, 2] * column_pos
        smooth_part = smooth_part + 0.7 * jnp.cos(2.0 * math.pi * angle_sum + phases[index])
    noise = jnp.clip(jax.random.normal(key_noise, (NZ, NY, NX), jnp.float32), -6.0, 6.0) * 0.6
    return smooth_part + noise


def setup_inputs(seed: int = 0) -> dict:
    streams_of = jax.random.split(jax.random.key(seed), 2)
    volume = draw_volume(jax.random.fold_in(streams_of[1], 71), 0)
    return dict(volume=volume)


TAU = 300.0
LAMBDA = 0.5


def smooth_axis(field, axis):
    length = field.shape[axis]
    widths = [(0, 0)] * field.ndim
    widths[axis] = (1, 1)
    padded = jnp.pad(field, widths)
    before = lax.slice_in_dim(padded, 0, length, axis=axis)
    after = lax.slice_in_dim(padded, 2, length + 2, axis=axis)
    return 0.25 * (before + 2.0 * field + after)


def conductance(diff):
    ratio = diff / LAMBDA
    return 1.0 / (1.0 + ratio * ratio)


def forward_conductance(smoothed, axis):
    length = smoothed.shape[axis]
    diff = lax.slice_in_dim(smoothed, 1, length, axis=axis) - lax.slice_in_dim(smoothed, 0, length - 1, axis=axis)
    widths = [(0, 0)] * smoothed.ndim
    widths[axis] = (0, 1)
    return jnp.pad(conductance(diff), widths)


def thomas(forward, source):
    zero_row = jnp.zeros_like(forward[:1])
    lower = -3.0 * TAU * jnp.concatenate([zero_row, forward[:-1]], axis=0)
    upper = -3.0 * TAU * forward
    diag = 1.0 - lower - upper

    def sweep_down(carry, row):
        upper_prev, source_prev = carry
        low_val, diag_val, up_val, src_val = row
        pivot = diag_val - low_val * upper_prev
        upper_new = up_val / pivot
        source_new = (src_val - low_val * source_prev) / pivot
        return (upper_new, source_new), (upper_new, source_new)

    start = (jnp.zeros_like(source[0]), jnp.zeros_like(source[0]))
    _, (uppers, sources) = lax.scan(sweep_down, start, (lower, diag, upper, source))

    def sweep_up(later, row):
        up_val, src_val = row
        value = src_val - up_val * later
        return value, value

    _, values = lax.scan(sweep_up, jnp.zeros_like(source[0]), (uppers, sources), reverse=True)
    return values


def solve_columns(pair):
    forward, source = pair
    return thomas(forward.T, source.T).T


def solve_leading(pair):
    forward, source = pair
    return thomas(forward, source)


def reference(volume):
    smoothed = smooth_axis(smooth_axis(smooth_axis(volume, 2), 1), 0)
    cond_x = forward_conductance(smoothed, 2)
    cond_y = forward_conductance(smoothed, 1)
    cond_z = forward_conductance(smoothed, 0)
    solved_x = lax.map(solve_columns, (cond_x, volume))
    solved_y = lax.map(solve_leading, (cond_y, volume))
    moved = lax.map(solve_leading, (jnp.swapaxes(cond_z, 0, 1), jnp.swapaxes(volume, 0, 1)))
    solved_z = jnp.swapaxes(moved, 0, 1)
    return (solved_x + solved_y + solved_z) / 3.0
```

```python
import jax
import jax.numpy as jnp
from jax import lax
from jax.experimental import pallas as pl
from jax.experimental.pallas import tpu as pltpu
from jax.sharding import PartitionSpec as P

TAU3 = 900.0
INV_LAMBDA_SQ = 4.0
PLANES = 32
ROWS = 16
COLS = 128
BLOCKS = 32
F32 = jnp.float32


def resistance(diff):
    return (1.0 + INV_LAMBDA_SQ * (diff * diff)) * (1.0 / TAU3)


def smooth_lanes(field, first, last):
    before = jnp.where(first, 0.0, pltpu.roll(field, 1, field.ndim - 1))
    after = jnp.where(last, 0.0, pltpu.roll(field, COLS - 1, field.ndim - 1))
    return 0.25 * (before + 2.0 * field + after)


def eliminate(coupling, ground, source, near_ground, near_source, resist):
    factor = 1.0 / (1.0 + (coupling + ground) * resist)
    weight = factor * resist
    back = coupling * weight
    near_ground = near_ground + back * ground
    near_source = near_source + back * source
    saved = (factor, back, source * weight)
    return coupling * factor, ground * factor, source * factor, near_ground, near_source, saved


def eliminate_last(coupling, ground, source, near_ground, near_source, conduct):
    inverse = 1.0 / (coupling + ground + conduct)
    factor = conduct * inverse
    back = coupling * inverse
    near_ground = near_ground + back * ground
    near_source = near_source + back * source
    saved = (factor, back, source * inverse)
    return coupling * factor, ground * factor, source * factor, near_ground, near_source, saved


def join(left, right):
    lc, lg, lh, ls, lt = left
    rc, rg, rh, rs, rt = right
    ground = lh + rg
    source = lt + rs
    inverse = 1.0 / (lc + rc + ground)
    to_left = lc * inverse
    to_right = rc * inverse
    return (
        lc * to_right,
        lg + to_left * ground,
        rh + to_right * ground,
        ls + to_left * source,
        rt + to_right * source,
    ), (to_left, to_right, source * inverse)


def local_kernel(
    vol, low_plane, high_planes, low_row, high_rows,
    y_port, y_factor, y_back, y_rest, z_port, z_factor, z_back, z_rest, z_mid, x_conduct,
    mixed, deep, smooth, y_resist,
):
    depth_last = lax.axis_index("depth") == lax.axis_size("depth") - 1
    lat_last = lax.axis_index("lat") == lax.axis_size("lat") - 1
    z_open = jnp.where(depth_last, 0.0, TAU3).astype(F32)
    y_open = jnp.where(lat_last, 0.0, TAU3).astype(F32)
    lane = lax.broadcasted_iota(jnp.int32, (ROWS, COLS), 1)
    first, last = lane == 0, lane == COLS - 1
    for plane in range(PLANES):
        mixed[plane + 1, 8:24, :] = smooth_lanes(vol[plane * ROWS : (plane + 1) * ROWS, :], first, last)
    mixed[0, 8:24, :] = smooth_lanes(low_plane[...], first, last)
    mixed[PLANES + 1, 8:24, :] = smooth_lanes(high_planes[0:ROWS, :], first, last)
    mixed[PLANES + 2, 8:24, :] = smooth_lanes(high_planes[ROWS : 2 * ROWS, :], first, last)
    side_lane = lax.broadcasted_iota(jnp.int32, (PLANES + 3, COLS), 1)
    side_first, side_last = side_lane == 0, side_lane == COLS - 1
    mixed[:, 7, :] = smooth_lanes(low_row[...], side_first, side_last)
    mixed[:, 24, :] = smooth_lanes(high_rows[0], side_first, side_last)
    mixed[:, 25, :] = smooth_lanes(high_rows[1], side_first, side_last)
    for plane in range(PLANES + 1):
        deep[plane] = 0.25 * (mixed[plane] + 2.0 * mixed[plane + 1] + mixed[plane + 2])
    for plane in range(PLANES + 1):
        smooth[plane, 8:32, :] = 0.25 * (
            deep[plane, 7:31, :] + 2.0 * deep[plane, 8:32, :] + deep[plane, 9:33, :]
        )
    for plane in range(PLANES):
        here = smooth[plane, 8:24, :]
        span = slice(plane * ROWS, (plane + 1) * ROWS)
        y_resist[span, :] = resistance(smooth[plane, 9:25, :] - here)
        along = pltpu.roll(here, COLS - 1, 1) - here
        x_conduct[span, :] = jnp.where(last, 0.0, 1.0 / resistance(along))

    def y_row(ref, row):
        return ref[pl.ds(row, PLANES, stride=ROWS), :]

    half = PLANES // 2

    def z_resist(plane):
        return resistance(smooth[plane + 1, 8:24, :] - smooth[plane, 8:24, :])

    def z_cell(plane):
        return vol[plane * ROWS : (plane + 1) * ROWS, :]

    one_y = jnp.ones((PLANES, COLS), F32)
    one_z = jnp.ones((ROWS, COLS), F32)
    y_state = (1.0 / y_row(y_resist, 0), one_y, y_row(vol, 1), one_y, y_row(vol, 0))
    z_states = [
        (1.0 / z_resist(start), one_z, z_cell(start + 1), one_z, z_cell(start)) for start in (0, half)
    ]
    for step in range(1, ROWS):
        final = step == ROWS - 1
        if final:
            conduct = y_open / (TAU3 * y_row(y_resist, step))
            *y_state, saved = eliminate_last(*y_state, conduct)
        else:
            *y_state, saved = eliminate(*y_state, y_row(y_resist, step))
            y_state[1] = y_state[1] + 1.0
            y_state[2] = y_state[2] + y_row(vol, step + 1)
        y_factor[step], y_back[step], y_rest[step] = saved
        for part in range(2):
            plane = part * half + step
            span = slice(plane * ROWS, (plane + 1) * ROWS)
            resist = z_resist(plane)
            if final and part == 1:
                *state, saved = eliminate_last(*z_states[part], z_open / (TAU3 * resist))
            else:
                *state, saved = eliminate(*z_states[part], resist)
            if not final:
                state[1] = state[1] + 1.0
                state[2] = state[2] + z_cell(plane + 1)
            z_states[part] = state
            z_factor[span, :], z_back[span, :], z_rest[span, :] = saved
    coupling, far_ground, far_source, near_ground, near_source = y_state
    for place, value in enumerate((coupling, near_ground, far_ground, near_source, far_source)):
        y_port[pl.ds(place, PLANES, stride=8), :] = value
    for place in range(5, 8):
        y_port[pl.ds(place, PLANES, stride=8), :] = jnp.zeros((PLANES, COLS), F32)
    ports = [(c, ng, fg, ns, fs) for c, fg, fs, ng, ns in z_states]
    port, middle = join(*ports)
    for place, value in enumerate(port):
        z_port[place] = value
    for place, value in enumerate(middle):
        z_mid[place] = value


def lane_kernel(vol, conduct, out):
    def chunk(index, carry):
        start = pl.multiple_of(index * 64, 64)
        source = vol[pl.ds(start, 64), :]
        right = conduct[pl.ds(start, 64), :]
        ground = jnp.ones_like(source)
        step = 1
        while step < COLS:
            left = pltpu.roll(right, step, 1)
            inverse = 1.0 / (ground + left + right)
            ground_part = ground * inverse
            source_part = source * inverse
            ground = (
                ground
                + left * pltpu.roll(ground_part, step, 1)
                + right * pltpu.roll(ground_part, COLS - step, 1)
            )
            source = (
                source
                + left * pltpu.roll(source_part, step, 1)
                + right * pltpu.roll(source_part, COLS - step, 1)
            )
            right = right * pltpu.roll(right * inverse, COLS - step, 1)
            step *= 2
        out[pl.ds(start, 64), :] = source / ground
        return carry

    lax.fori_loop(0, PLANES * ROWS // 64, chunk, 0)


def row_reduced_kernel(ports, out):
    coupling, near_ground, far_ground, near_source, far_source = (
        ports[pl.ds(place, BLOCKS, stride=8), :] for place in range(5)
    )
    right = coupling
    ground = near_ground + pltpu.roll(far_ground, 1, 0)
    source = near_source + pltpu.roll(far_source, 1, 0)
    step = 1
    while step < BLOCKS:
        left = pltpu.roll(right, step, 0)
        inverse = 1.0 / (ground + left + right)
        ground_part = ground * inverse
        source_part = source * inverse
        ground = (
            ground
            + left * pltpu.roll(ground_part, step, 0)
            + right * pltpu.roll(ground_part, BLOCKS - step, 0)
        )
        source = (
            source
            + left * pltpu.roll(source_part, step, 0)
            + right * pltpu.roll(source_part, BLOCKS - step, 0)
        )
        right = right * pltpu.roll(right * inverse, BLOCKS - step, 0)
        step *= 2
    solved = source / ground
    out[:, 0, :] = solved
    out[:, 1, :] = pltpu.roll(solved, BLOCKS - 1, 0)


def pick(flag, there, here):
    return tuple(jnp.where(flag, a, b) for a, b in zip(there, here))


def join_kernel(bit, own, other, out):
    upper = (lax.axis_index("depth") & bit) != 0
    mine = tuple(own[place] for place in range(5))
    theirs = tuple(other[place] for place in range(5))
    port, _ = join(pick(upper, theirs, mine), pick(upper, mine, theirs))
    for place, value in enumerate(port):
        out[place] = value


def finish_kernel(
    ends_y, y_factor, y_back, y_rest, own, near, pair, quad, z_factor, z_back, z_rest, z_mid, solved_x,
    out, acc,
):
    index = lax.axis_index("depth")
    zero = jnp.zeros((ROWS, COLS), F32)
    left_ground, left_source, right_ground, right_source = zero, zero, zero, zero
    for bit, ref in ((4, quad), (2, pair), (1, near)):
        on_left = (index & bit) != 0
        c, ng, fg, ns, fs = (ref[place] for place in range(5))
        ground, source = ng + left_ground, ns + left_source
        share = c / (c + ground)
        left_ground = jnp.where(on_left, fg + share * ground, left_ground)
        left_source = jnp.where(on_left, fs + share * source, left_source)
        ground, source = fg + right_ground, fs + right_source
        total = c + ground
        share = jnp.where(total > 0.0, c / jnp.where(total > 0.0, total, 1.0), 0.0)
        right_ground = jnp.where(on_left, right_ground, ng + share * ground)
        right_source = jnp.where(on_left, right_source, ns + share * source)
    c, ng, fg, ns, fs = (own[place] for place in range(5))
    ground, source = fg + right_ground, fs + right_source
    total = c + ground
    inverse = jnp.where(total > 0.0, 1.0 / jnp.where(total > 0.0, total, 1.0), 0.0)
    share = c * inverse
    first = (left_source + ns + share * source) / (left_ground + ng + share * ground)
    after = share * first + source * inverse
    middle = z_mid[0] * first + z_mid[1] * after + z_mid[2]
    half = PLANES // 2
    y_first = ends_y[:, 0, :]
    y_after = ends_y[:, 1, :]
    acc[pl.ds(0, PLANES, stride=ROWS), :] = y_first
    value = y_after
    for row in range(ROWS - 1, 0, -1):
        value = y_factor[row] * value + (y_back[row] * y_first + y_rest[row])
        acc[pl.ds(row, PLANES, stride=ROWS), :] = value
    third = 1.0 / 3.0
    for start, near_value, far_value in ((0, first, middle), (half, middle, after)):
        value = far_value
        for plane in range(start + half - 1, start, -1):
            span = slice(plane * ROWS, (plane + 1) * ROWS)
            value = z_factor[span, :] * value + (z_back[span, :] * near_value + z_rest[span, :])
            out[span, :] = (solved_x[span, :] + acc[span, :] + value) * third
        span = slice(start * ROWS, (start + 1) * ROWS)
        out[span, :] = (solved_x[span, :] + acc[span, :] + near_value) * third


def call(kernel, outs, scratch=(), flops=1000000, moved=500000):
    return pl.pallas_call(
        kernel,
        out_shape=outs,
        scratch_shapes=scratch,
        compiler_params=pltpu.CompilerParams(vmem_limit_bytes=32 * 1024 * 1024),
        cost_estimate=pl.CostEstimate(flops=flops, bytes_accessed=moved, transcendentals=0),
    )


def shaped(*shape):
    return jax.ShapeDtypeStruct(shape, F32)


def line_perm(axis, step):
    count = lax.axis_size(axis)
    if step > 0:
        return [(i, i + 1) for i in range(count - 1)]
    return [(i + 1, i) for i in range(count - 1)]


def swap_perm(axis, bit):
    return [(i, i ^ bit) for i in range(lax.axis_size(axis))]


def shards(volume):
    flat = volume.reshape(PLANES * ROWS, COLS)
    low_plane = lax.ppermute(volume[PLANES - 1], "depth", line_perm("depth", 1))
    high_planes = lax.ppermute(volume[:2], "depth", line_perm("depth", -1))
    tall = jnp.concatenate([low_plane[None], volume, high_planes], axis=0)
    low_row = lax.ppermute(tall[:, ROWS - 1], "lat", line_perm("lat", 1))
    high_rows = lax.ppermute(jnp.stack([tall[:, 0], tall[:, 1]]), "lat", line_perm("lat", -1))
    lines = shaped(ROWS, PLANES, COLS)
    whole = shaped(PLANES * ROWS, COLS)
    (
        y_port, y_factor, y_back, y_rest, z_port, z_factor, z_back, z_rest, z_mid, x_conduct
    ) = call(
        local_kernel,
        (
            shaped(PLANES * 8, COLS), lines, lines, lines,
            shaped(5, ROWS, COLS), whole, whole, whole, shaped(3, ROWS, COLS), whole,
        ),
        (
            pltpu.VMEM((PLANES + 3, 40, COLS), F32),
            pltpu.VMEM((PLANES + 1, 40, COLS), F32),
            pltpu.VMEM((PLANES + 1, 32, COLS), F32),
            pltpu.VMEM((PLANES * ROWS, COLS), F32),
        ),
    )(flat, low_plane, high_planes.reshape(2 * ROWS, COLS), low_row, high_rows)
    near = lax.ppermute(z_port, "depth", swap_perm("depth", 1))
    pair_own = call(lambda *refs: join_kernel(1, *refs), shaped(5, ROWS, COLS))(z_port, near)
    y_port, pair_own = lax.optimization_barrier((y_port, pair_own))
    pair = lax.ppermute(pair_own, "depth", swap_perm("depth", 2))
    ports = lax.all_to_all(y_port, "lat", 0, 0, tiled=True)
    solved_x = call(lane_kernel, whole)(flat, x_conduct)
    ends = call(row_reduced_kernel, shaped(BLOCKS, 2, COLS))(ports)
    quad_own = call(lambda *refs: join_kernel(2, *refs), shaped(5, ROWS, COLS))(pair_own, pair)
    ends, quad_own = lax.optimization_barrier((ends, quad_own))
    quad = lax.ppermute(quad_own, "depth", swap_perm("depth", 4))
    ends_y = lax.all_to_all(ends, "lat", 0, 0, tiled=True)
    out = call(finish_kernel, whole, (pltpu.VMEM((PLANES * ROWS, COLS), F32),))(
        ends_y, y_factor, y_back, y_rest, z_port, near, pair, quad, z_factor, z_back, z_rest, z_mid, solved_x
    )
    return out.reshape(PLANES, ROWS, COLS)


def solution(mesh):
    placed = (P("depth", "lat", None),)
    return jax.shard_map(
        shards, mesh=mesh, in_specs=placed, out_specs=P("depth", "lat", None), check_vma=False
    )
```

```python
import jax
import jax.numpy as jnp
from jax import lax
from jax.experimental import pallas as pl
from jax.experimental.pallas import tpu as pltpu
from jax.sharding import PartitionSpec as P

TAU3 = 900.0
INV_LAMBDA_SQ = 4.0
PLANES = 32
ROWS = 16
COLS = 128
BLOCKS = 32
PORT = 16
F32 = jnp.float32


def resistance(diff):
    return (1.0 + INV_LAMBDA_SQ * (diff * diff)) * (1.0 / TAU3)


def smooth_lanes(field, first, last):
    before = jnp.where(first, 0.0, pltpu.roll(field, 1, field.ndim - 1))
    after = jnp.where(last, 0.0, pltpu.roll(field, COLS - 1, field.ndim - 1))
    return 0.25 * (before + 2.0 * field + after)


def eliminate(coupling, ground, source, near_ground, near_source, resist):
    factor = 1.0 / (1.0 + (coupling + ground) * resist)
    weight = factor * resist
    back = coupling * weight
    near_ground = near_ground + back * ground
    near_source = near_source + back * source
    saved = (factor, back, source * weight)
    return coupling * factor, ground * factor, source * factor, near_ground, near_source, saved


def eliminate_last(coupling, ground, source, near_ground, near_source, conduct):
    inverse = 1.0 / (coupling + ground + conduct)
    factor = conduct * inverse
    back = coupling * inverse
    near_ground = near_ground + back * ground
    near_source = near_source + back * source
    saved = (factor, back, source * inverse)
    return coupling * factor, ground * factor, source * factor, near_ground, near_source, saved


def join(left, right):
    lc, lg, lh, ls, lt = left
    rc, rg, rh, rs, rt = right
    ground = lh + rg
    source = lt + rs
    inverse = 1.0 / (lc + rc + ground)
    to_left = lc * inverse
    to_right = rc * inverse
    return (
        lc * to_right,
        lg + to_left * ground,
        rh + to_right * ground,
        ls + to_left * source,
        rt + to_right * source,
    ), (to_left, to_right, source * inverse)


def edge_kernel(vol, low_side, high_side, sems):
    copies = (
        pltpu.make_async_copy(vol.at[pl.ds((PLANES - 1) * ROWS, ROWS), :], high_side, sems.at[0]),
        pltpu.make_async_copy(vol.at[pl.ds(0, 2 * ROWS), :], low_side, sems.at[1]),
    )
    for copy in copies:
        copy.start()
    for copy in copies:
        copy.wait()


def strided(ref, row):
    return ref[pl.ds(row, 32, stride=16), :]


def row_kernel(vol, low_plane, high_planes, port, factor, back, rest, deep, low_side, high_side, mixed):
    lane = lax.broadcasted_iota(jnp.int32, (ROWS, COLS), 1)
    first, last = lane == 0, lane == COLS - 1
    mixed[0] = smooth_lanes(low_plane[...], first, last)
    for plane in range(PLANES):
        mixed[plane + 1] = smooth_lanes(vol[plane * ROWS : (plane + 1) * ROWS, :], first, last)
    mixed[PLANES + 1] = smooth_lanes(high_planes[0:ROWS, :], first, last)
    mixed[PLANES + 2] = smooth_lanes(high_planes[ROWS : 2 * ROWS, :], first, last)
    for plane in range(PLANES + 1):
        deep[plane * ROWS : (plane + 1) * ROWS, :] = 0.25 * (
            mixed[plane] + 2.0 * mixed[plane + 1] + mixed[plane + 2]
        )
    low_side[...] = deep[pl.ds(0, PLANES + 1, stride=ROWS), :]
    high_side[...] = deep[pl.ds(ROWS - 1, PLANES + 1, stride=ROWS), :]
    part = [strided(deep, row) for row in range(ROWS)]
    low_sum = 2.0 * part[0] + part[1]
    high_sum = part[ROWS - 2] + 2.0 * part[ROWS - 1]
    smooth = [None] + [0.25 * (part[r - 1] + 2.0 * part[r] + part[r + 1]) for r in range(1, ROWS - 1)]
    one = jnp.ones((PLANES, COLS), F32)
    state = (1.0 / resistance(smooth[2] - smooth[1]), one, strided(vol, 2), one, strided(vol, 1))
    for row in range(2, ROWS - 2):
        *state, saved = eliminate(*state, resistance(smooth[row + 1] - smooth[row]))
        state[1] = state[1] + 1.0
        state[2] = state[2] + strided(vol, row + 1)
        factor[row], back[row], rest[row] = saved
    coupling, far_ground, far_source, near_ground, near_source = state
    values = (
        coupling, near_ground, far_ground, near_source, far_source,
        part[0], part[ROWS - 1], low_sum, high_sum, smooth[1], smooth[ROWS - 2],
        strided(vol, 0), strided(vol, ROWS - 1),
    )
    for place, value in enumerate(values):
        port[pl.ds(place, PLANES, stride=PORT), :] = value
    for place in range(len(values), PORT):
        port[pl.ds(place, PLANES, stride=PORT), :] = jnp.zeros((PLANES, COLS), F32)


def chain_solve(coupling, near_ground, far_ground, near_source, far_source, count):
    size = coupling.shape[0]
    right = coupling
    ground = near_ground + pltpu.roll(far_ground, 1, 0)
    source = near_source + pltpu.roll(far_source, 1, 0)
    step = 1
    while step < count:
        left = pltpu.roll(right, step, 0)
        inverse = 1.0 / (ground + left + right)
        ground_part = ground * inverse
        source_part = source * inverse
        ground = (
            ground
            + left * pltpu.roll(ground_part, step, 0)
            + right * pltpu.roll(ground_part, size - step, 0)
        )
        source = (
            source
            + left * pltpu.roll(source_part, step, 0)
            + right * pltpu.roll(source_part, size - step, 0)
        )
        right = right * pltpu.roll(right * inverse, size - step, 0)
        step *= 2
    return source / ground


def plane_column_kernel(
    vol, deep, low_row, high_row,
    port, z_factor, z_back, z_rest, z_mid, solved_x,
    smooth, turned, turned_smooth, x_factor, x_back, x_rest,
):
    depth_last = lax.axis_index("depth") == lax.axis_size("depth") - 1
    z_open = jnp.where(depth_last, 0.0, TAU3).astype(F32)
    row_index = lax.broadcasted_iota(jnp.int32, (ROWS, COLS), 0)
    top, bottom = row_index == 0, row_index == ROWS - 1
    for plane in range(PLANES + 1):
        span = slice(plane * ROWS, (plane + 1) * ROWS)
        here = deep[span, :]
        above = jnp.where(top, low_row[plane : plane + 1, :], pltpu.roll(here, 1, 0))
        below = jnp.where(bottom, high_row[plane : plane + 1, :], pltpu.roll(here, ROWS - 1, 0))
        smooth[span, :] = 0.25 * (above + 2.0 * here + below)
    for group in range(4):
        span = slice(group * COLS, (group + 1) * COLS)
        turned[span, :] = vol[span, :].T
        turned_smooth[span, :] = smooth[span, :].T

    def z_cell(ref, plane):
        return ref[plane * ROWS : (plane + 1) * ROWS, :]

    def z_resist(plane):
        return resistance(z_cell(smooth, plane + 1) - z_cell(smooth, plane))

    def x_resist(step):
        if step < 15:
            return resistance(strided(turned_smooth, step + 1) - strided(turned_smooth, step))
        return resistance(pltpu.roll(strided(turned_smooth, 0), 31, 0) - strided(turned_smooth, 15))

    half = PLANES // 2
    chunk_last = (lax.broadcasted_iota(jnp.int32, (32, COLS), 0) & 7) == 7
    one_x = jnp.ones((32, COLS), F32)
    one_z = jnp.ones((ROWS, COLS), F32)
    x_state = (1.0 / x_resist(0), one_x, strided(turned, 1), one_x, strided(turned, 0))
    z_states = [
        (1.0 / z_resist(start), one_z, z_cell(vol, start + 1), one_z, z_cell(vol, start))
        for start in (0, half)
    ]
    for step in range(1, 16):
        final = step == 15
        if final:
            *x_state, saved = eliminate_last(*x_state, jnp.where(chunk_last, 0.0, 1.0 / x_resist(step)))
        else:
            *x_state, saved = eliminate(*x_state, x_resist(step))
            x_state[1] = x_state[1] + 1.0
            x_state[2] = x_state[2] + strided(turned, step + 1)
        x_factor[step], x_back[step], x_rest[step] = saved
        for part in range(2):
            plane = part * half + step
            span = slice(plane * ROWS, (plane + 1) * ROWS)
            resist = z_resist(plane)
            if final and part == 1:
                *state, saved = eliminate_last(*z_states[part], z_open / (TAU3 * resist))
            else:
                *state, saved = eliminate(*z_states[part], resist)
            if not final:
                state[1] = state[1] + 1.0
                state[2] = state[2] + z_cell(vol, plane + 1)
            z_states[part] = state
            z_factor[span, :], z_back[span, :], z_rest[span, :] = saved
    ports = [(c, ng, fg, ns, fs) for c, fg, fs, ng, ns in z_states]
    joined, middle = join(*ports)
    for place, value in enumerate(joined):
        port[place] = value
    for place, value in enumerate(middle):
        z_mid[place] = value
    coupling, far_ground, far_source, near_ground, near_source = x_state
    first = chain_solve(coupling, near_ground, far_ground, near_source, far_source, 8)
    turned[pl.ds(0, 32, stride=16), :] = first
    value = pltpu.roll(first, 31, 0)
    for step in range(15, 0, -1):
        value = x_factor[step] * value + (x_back[step] * first + x_rest[step])
        turned[pl.ds(step, 32, stride=16), :] = value
    for group in range(4):
        span = slice(group * COLS, (group + 1) * COLS)
        solved_x[span, :] = turned[span, :].T


def row_reduced_kernel(ports, out):
    (
        coupling, near_ground, far_ground, near_source, far_source,
        low, high, low_sum, high_sum, low_smooth, high_smooth, low_cell, high_cell,
    ) = (ports[pl.ds(place, BLOCKS, stride=PORT), :] for place in range(13))
    block = lax.broadcasted_iota(jnp.int32, (BLOCKS, COLS), 0)
    block_first, block_last = block == 0, block == BLOCKS - 1
    low_end = 0.25 * (jnp.where(block_first, 0.0, pltpu.roll(high, 1, 0)) + low_sum)
    high_end = 0.25 * (high_sum + jnp.where(block_last, 0.0, pltpu.roll(low, BLOCKS - 1, 0)))
    enter = 1.0 / resistance(low_smooth - low_end)
    leave = 1.0 / resistance(high_end - high_smooth)
    across = pltpu.roll(low_end, BLOCKS - 1, 0) - high_end
    across = jnp.where(block_last, 0.0, 1.0 / resistance(across))
    zero = jnp.zeros_like(coupling)
    one = jnp.ones_like(coupling)
    before, at_low = join(
        (enter, one, zero, low_cell, zero), (coupling, near_ground, far_ground, near_source, far_source)
    )
    after, at_high = join((leave, zero, one, zero, high_cell), (across, zero, zero, zero, zero))
    whole, between = join(before, after)
    first = chain_solve(*whole, BLOCKS)
    later = pltpu.roll(first, BLOCKS - 1, 0)

    def middle(weights, left, right):
        return weights[0] * left + weights[1] * right + weights[2]

    inner_high = middle(between, first, later)
    out[:, 0, :] = first
    out[:, 1, :] = middle(at_low, first, inner_high)
    out[:, 2, :] = inner_high
    out[:, 3, :] = middle(at_high, inner_high, later)


def pick(flag, there, here):
    return tuple(jnp.where(flag, a, b) for a, b in zip(there, here))


def join_kernel(bit, own, other, out):
    upper = (lax.axis_index("depth") & bit) != 0
    mine = tuple(own[place] for place in range(5))
    theirs = tuple(other[place] for place in range(5))
    port, _ = join(pick(upper, theirs, mine), pick(upper, mine, theirs))
    for place, value in enumerate(port):
        out[place] = value


def finish_kernel(
    ends_y, y_factor, y_back, y_rest, own, near, pair, across, skew, z_factor, z_back, z_rest, z_mid, solved_x,
    out, acc,
):
    index = lax.axis_index("depth")
    odd = (index & 2) != 0
    straight = tuple(across[place] for place in range(5))
    crossed = tuple(skew[place] for place in range(5))
    quad, _ = join(pick(odd, crossed, straight), pick(odd, straight, crossed))
    zero = jnp.zeros((ROWS, COLS), F32)
    left_ground, left_source, right_ground, right_source = zero, zero, zero, zero
    for bit, ref in ((4, quad), (2, pair), (1, near)):
        on_left = (index & bit) != 0
        c, ng, fg, ns, fs = (ref[place] for place in range(5))
        ground, source = ng + left_ground, ns + left_source
        share = c / (c + ground)
        left_ground = jnp.where(on_left, fg + share * ground, left_ground)
        left_source = jnp.where(on_left, fs + share * source, left_source)
        ground, source = fg + right_ground, fs + right_source
        total = c + ground
        share = jnp.where(total > 0.0, c / jnp.where(total > 0.0, total, 1.0), 0.0)
        right_ground = jnp.where(on_left, right_ground, ng + share * ground)
        right_source = jnp.where(on_left, right_source, ns + share * source)
    c, ng, fg, ns, fs = (own[place] for place in range(5))
    ground, source = fg + right_ground, fs + right_source
    total = c + ground
    inverse = jnp.where(total > 0.0, 1.0 / jnp.where(total > 0.0, total, 1.0), 0.0)
    share = c * inverse
    first = (left_source + ns + share * source) / (left_ground + ng + share * ground)
    after = share * first + source * inverse
    middle = z_mid[0] * first + z_mid[1] * after + z_mid[2]
    half = PLANES // 2
    for place, row in ((0, 0), (1, 1), (2, ROWS - 2), (3, ROWS - 1)):
        acc[pl.ds(row, PLANES, stride=ROWS), :] = ends_y[:, place, :]
    y_first = ends_y[:, 1, :]
    value = ends_y[:, 2, :]
    for row in range(ROWS - 3, 1, -1):
        value = y_factor[row] * value + (y_back[row] * y_first + y_rest[row])
        acc[pl.ds(row, PLANES, stride=ROWS), :] = value
    third = 1.0 / 3.0
    for start, near_value, far_value in ((0, first, middle), (half, middle, after)):
        value = far_value
        for plane in range(start + half - 1, start, -1):
            span = slice(plane * ROWS, (plane + 1) * ROWS)
            value = z_factor[span, :] * value + (z_back[span, :] * near_value + z_rest[span, :])
            out[span, :] = (solved_x[span, :] + acc[span, :] + value) * third
        span = slice(start * ROWS, (start + 1) * ROWS)
        out[span, :] = (solved_x[span, :] + acc[span, :] + near_value) * third


def call(kernel, outs, scratch=(), flops=1000000, moved=500000):
    return pl.pallas_call(
        kernel,
        out_shape=outs,
        scratch_shapes=scratch,
        compiler_params=pltpu.CompilerParams(vmem_limit_bytes=32 * 1024 * 1024),
        cost_estimate=pl.CostEstimate(flops=flops, bytes_accessed=moved, transcendentals=0),
    )


def shaped(*shape):
    return jax.ShapeDtypeStruct(shape, F32)


def line_perm(axis, step):
    count = lax.axis_size(axis)
    if step > 0:
        return [(i, i + 1) for i in range(count - 1)]
    return [(i + 1, i) for i in range(count - 1)]


def swap_perm(axis, bit):
    return [(i, i ^ bit) for i in range(lax.axis_size(axis))]


def shards(volume):
    flat = volume.reshape(PLANES * ROWS, COLS)
    lines = shaped(ROWS, PLANES, COLS)
    whole = shaped(PLANES * ROWS, COLS)
    port = shaped(5, ROWS, COLS)
    side = shaped(PLANES + 1, COLS)
    to_low, to_high = pl.pallas_call(
        edge_kernel,
        in_specs=[pl.BlockSpec(memory_space=pl.ANY)],
        out_shape=(shaped(2 * ROWS, COLS), shaped(ROWS, COLS)),
        scratch_shapes=[pltpu.SemaphoreType.DMA((2,))],
    )(flat)
    low_plane = lax.ppermute(to_high, "depth", line_perm("depth", 1))
    high_planes = lax.ppermute(to_low, "depth", line_perm("depth", -1))
    y_port, y_factor, y_back, y_rest, deep, row_low, row_high = call(
        row_kernel,
        (
            shaped(PLANES * PORT, COLS), lines, lines, lines,
            shaped((PLANES + 1) * ROWS, COLS), side, side,
        ),
        (pltpu.VMEM((PLANES + 3, ROWS, COLS), F32),),
    )(flat, low_plane, high_planes)
    ports = lax.all_to_all(y_port, "lat", 0, 0, tiled=True)
    low_row = lax.ppermute(row_high, "lat", line_perm("lat", 1))
    high_row = lax.ppermute(row_low, "lat", line_perm("lat", -1))
    z_port, z_factor, z_back, z_rest, z_mid, solved_x = call(
        plane_column_kernel,
        (port, whole, whole, whole, shaped(3, ROWS, COLS), whole),
        (
            pltpu.VMEM(((PLANES + 1) * ROWS, COLS), F32),
            pltpu.VMEM((512, COLS), F32),
            pltpu.VMEM((512, COLS), F32),
            pltpu.VMEM((16, 32, COLS), F32),
            pltpu.VMEM((16, 32, COLS), F32),
            pltpu.VMEM((16, 32, COLS), F32),
        ),
    )(flat, deep, low_row, high_row)
    near = lax.ppermute(z_port, "depth", swap_perm("depth", 1))
    pair_own = call(lambda *refs: join_kernel(1, *refs), port)(z_port, near)
    ends = call(row_reduced_kernel, shaped(BLOCKS, 4, COLS))(ports)
    ends, pair_own = lax.optimization_barrier((ends, pair_own))
    ends_y = lax.all_to_all(ends, "lat", 0, 0, tiled=True)
    pair, across, skew = (lax.ppermute(pair_own, "depth", swap_perm("depth", bits)) for bits in (2, 4, 6))
    out = call(finish_kernel, whole, (pltpu.VMEM((PLANES * ROWS, COLS), F32),))(
        ends_y, y_factor, y_back, y_rest, z_port, near, pair, across, skew,
        z_factor, z_back, z_rest, z_mid, solved_x,
    )
    return out.reshape(PLANES, ROWS, COLS)


def solution(mesh):
    placed = (P("depth", "lat", None),)
    return jax.shard_map(
        shards, mesh=mesh, in_specs=placed, out_specs=P("depth", "lat", None), check_vma=False
    )
```

```python
import jax
import jax.numpy as jnp
from jax import lax
from jax.experimental import pallas as pl
from jax.experimental.pallas import tpu as pltpu
from jax.sharding import PartitionSpec as P

TAU3 = 900.0
INV_LAMBDA_SQ = 4.0
PLANES = 32
ROWS = 16
COLS = 128
BLOCKS = 32
PORT = 8
F32 = jnp.float32


def resistance(diff):
    return (1.0 + INV_LAMBDA_SQ * (diff * diff)) * (1.0 / TAU3)


def smooth_lanes(field, first, last):
    before = jnp.where(first, 0.0, pltpu.roll(field, 1, field.ndim - 1))
    after = jnp.where(last, 0.0, pltpu.roll(field, COLS - 1, field.ndim - 1))
    return 0.25 * (before + 2.0 * field + after)


def eliminate(coupling, ground, source, near_ground, near_source, resist):
    factor = 1.0 / (1.0 + (coupling + ground) * resist)
    weight = factor * resist
    back = coupling * weight
    near_ground = near_ground + back * ground
    near_source = near_source + back * source
    saved = (factor, back, source * weight)
    return coupling * factor, ground * factor, source * factor, near_ground, near_source, saved


def eliminate_last(coupling, ground, source, near_ground, near_source, conduct):
    inverse = 1.0 / (coupling + ground + conduct)
    factor = conduct * inverse
    back = coupling * inverse
    near_ground = near_ground + back * ground
    near_source = near_source + back * source
    saved = (factor, back, source * inverse)
    return coupling * factor, ground * factor, source * factor, near_ground, near_source, saved


def join(left, right):
    lc, lg, lh, ls, lt = left
    rc, rg, rh, rs, rt = right
    ground = lh + rg
    source = lt + rs
    inverse = 1.0 / (lc + rc + ground)
    to_left = lc * inverse
    to_right = rc * inverse
    return (
        lc * to_right,
        lg + to_left * ground,
        rh + to_right * ground,
        ls + to_left * source,
        rt + to_right * source,
    ), (to_left, to_right, source * inverse)


def edge_kernel(vol, near_side, far_side, sems):
    odd = lax.axis_index("depth") & 1
    high = (PLANES - 2) * ROWS
    near_start = pl.multiple_of((1 - odd) * high, ROWS)
    far_start = pl.multiple_of(odd * high, ROWS)
    copies = (
        pltpu.make_async_copy(vol.at[pl.ds(near_start, 2 * ROWS), :], near_side, sems.at[0]),
        pltpu.make_async_copy(vol.at[pl.ds(far_start, 2 * ROWS), :], far_side, sems.at[1]),
    )
    for copy in copies:
        copy.start()
    for copy in copies:
        copy.wait()


def strided(ref, row):
    return ref[pl.ds(row, 32, stride=16), :]


def cells(ref, plane):
    return ref[plane * ROWS : (plane + 1) * ROWS, :]


def deep_kernel(vol, near_side, far_side, deep, low_side, high_side, mixed):
    odd = (lax.axis_index("depth") & 1) == 1
    lane = lax.broadcasted_iota(jnp.int32, (ROWS, COLS), 1)
    first, last = lane == 0, lane == COLS - 1
    mixed[0] = smooth_lanes(jnp.where(odd, cells(near_side, 1), cells(far_side, 1)), first, last)
    for plane in range(PLANES):
        mixed[plane + 1] = smooth_lanes(cells(vol, plane), first, last)
    for plane in range(2):
        mixed[PLANES + 1 + plane] = smooth_lanes(
            jnp.where(odd, cells(far_side, plane), cells(near_side, plane)), first, last
        )
    for plane in range(PLANES + 1):
        deep[plane * ROWS : (plane + 1) * ROWS, :] = 0.25 * (
            mixed[plane] + 2.0 * mixed[plane + 1] + mixed[plane + 2]
        )
    low_side[...] = deep[pl.ds(0, PLANES + 1, stride=ROWS), :]
    high_side[...] = deep[pl.ds(ROWS - 1, PLANES + 1, stride=ROWS), :]


def plane_kernel(vol, deep, low_row, high_row, port, factor, back, rest, mid, smooth):
    depth_last = lax.axis_index("depth") == lax.axis_size("depth") - 1
    z_open = jnp.where(depth_last, 0.0, TAU3).astype(F32)
    row_index = lax.broadcasted_iota(jnp.int32, (ROWS, COLS), 0)
    top, bottom = row_index == 0, row_index == ROWS - 1
    for plane in range(PLANES + 1):
        span = slice(plane * ROWS, (plane + 1) * ROWS)
        here = deep[span, :]
        above = jnp.where(top, low_row[plane : plane + 1, :], pltpu.roll(here, 1, 0))
        below = jnp.where(bottom, high_row[plane : plane + 1, :], pltpu.roll(here, ROWS - 1, 0))
        smooth[span, :] = 0.25 * (above + 2.0 * here + below)

    def resist(plane):
        return resistance(cells(smooth, plane + 1) - cells(smooth, plane))

    half = PLANES // 2
    one = jnp.ones((ROWS, COLS), F32)
    states = [
        (1.0 / resist(start), one, cells(vol, start + 1), one, cells(vol, start)) for start in (0, half)
    ]
    for step in range(1, half):
        final = step == half - 1
        for part in range(2):
            plane = part * half + step
            span = slice(plane * ROWS, (plane + 1) * ROWS)
            if final and part == 1:
                *state, saved = eliminate_last(*states[part], z_open / (TAU3 * resist(plane)))
            else:
                *state, saved = eliminate(*states[part], resist(plane))
            if not final:
                state[1] = state[1] + 1.0
                state[2] = state[2] + cells(vol, plane + 1)
            states[part] = state
            factor[span, :], back[span, :], rest[span, :] = saved
    joined, middle = join(*[(c, ng, fg, ns, fs) for c, fg, fs, ng, ns in states])
    for place, value in enumerate(joined):
        port[place] = value
    for place, value in enumerate(middle):
        mid[place] = value


def row_kernel(vol, smooth, port, factor, back, rest):
    def resist(row):
        return resistance(strided(smooth, row + 1) - strided(smooth, row))

    one = jnp.ones((PLANES, COLS), F32)
    state = (1.0 / resist(0), one, strided(vol, 1), one, strided(vol, 0))
    for row in range(1, ROWS - 1):
        *state, saved = eliminate(*state, resist(row))
        state[1] = state[1] + 1.0
        state[2] = state[2] + strided(vol, row + 1)
        factor[row], back[row], rest[row] = saved
    coupling, far_ground, far_source, near_ground, near_source = state
    values = (
        coupling, near_ground, far_ground, near_source, far_source,
        strided(smooth, 0), strided(smooth, ROWS - 1), jnp.zeros((PLANES, COLS), F32),
    )
    for place, value in enumerate(values):
        port[pl.ds(place, PLANES, stride=PORT), :] = value


def chain_solve(coupling, near_ground, far_ground, near_source, far_source, count):
    size = coupling.shape[0]
    right = coupling
    ground = near_ground + pltpu.roll(far_ground, 1, 0)
    source = near_source + pltpu.roll(far_source, 1, 0)
    step = 1
    while step < count:
        left = pltpu.roll(right, step, 0)
        inverse = 1.0 / (ground + left + right)
        ground_part = ground * inverse
        source_part = source * inverse
        ground = (
            ground
            + left * pltpu.roll(ground_part, step, 0)
            + right * pltpu.roll(ground_part, size - step, 0)
        )
        source = (
            source
            + left * pltpu.roll(source_part, step, 0)
            + right * pltpu.roll(source_part, size - step, 0)
        )
        right = right * pltpu.roll(right * inverse, size - step, 0)
        step *= 2
    return source / ground


def column_kernel(vol, smooth, solved_x, turned, turned_smooth, factor, back, rest):
    for group in range(4):
        span = slice(group * COLS, (group + 1) * COLS)
        turned[span, :] = vol[span, :].T
        turned_smooth[span, :] = smooth[span, :].T

    def resist(step):
        if step < 15:
            return resistance(strided(turned_smooth, step + 1) - strided(turned_smooth, step))
        return resistance(pltpu.roll(strided(turned_smooth, 0), 31, 0) - strided(turned_smooth, 15))

    chunk_last = (lax.broadcasted_iota(jnp.int32, (32, COLS), 0) & 7) == 7
    one = jnp.ones((32, COLS), F32)
    state = (1.0 / resist(0), one, strided(turned, 1), one, strided(turned, 0))
    for step in range(1, 16):
        if step == 15:
            *state, saved = eliminate_last(*state, jnp.where(chunk_last, 0.0, 1.0 / resist(step)))
        else:
            *state, saved = eliminate(*state, resist(step))
            state[1] = state[1] + 1.0
            state[2] = state[2] + strided(turned, step + 1)
        factor[step], back[step], rest[step] = saved
    coupling, far_ground, far_source, near_ground, near_source = state
    first = chain_solve(coupling, near_ground, far_ground, near_source, far_source, 8)
    turned[pl.ds(0, 32, stride=16), :] = first
    value = pltpu.roll(first, 31, 0)
    for step in range(15, 0, -1):
        value = factor[step] * value + (back[step] * first + rest[step])
        turned[pl.ds(step, 32, stride=16), :] = value
    for group in range(4):
        span = slice(group * COLS, (group + 1) * COLS)
        solved_x[span, :] = turned[span, :].T


def row_reduced_kernel(ports, out):
    coupling, near_ground, far_ground, near_source, far_source, low, high = (
        ports[pl.ds(place, BLOCKS, stride=PORT), :] for place in range(7)
    )
    block_last = lax.broadcasted_iota(jnp.int32, (BLOCKS, COLS), 0) == BLOCKS - 1
    across = pltpu.roll(low, BLOCKS - 1, 0) - high
    across = jnp.where(block_last, 0.0, 1.0 / resistance(across))
    zero = jnp.zeros_like(coupling)
    whole, at_high = join(
        (coupling, near_ground, far_ground, near_source, far_source), (across, zero, zero, zero, zero)
    )
    first = chain_solve(*whole, BLOCKS)
    out[:, 0, :] = first
    out[:, 1, :] = at_high[0] * first + at_high[1] * pltpu.roll(first, BLOCKS - 1, 0) + at_high[2]


def pick(flag, there, here):
    return tuple(jnp.where(flag, a, b) for a, b in zip(there, here))


def join_kernel(bit, own, other, out):
    upper = (lax.axis_index("depth") & bit) != 0
    mine = tuple(own[place] for place in range(5))
    theirs = tuple(other[place] for place in range(5))
    port, _ = join(pick(upper, theirs, mine), pick(upper, mine, theirs))
    for place, value in enumerate(port):
        out[place] = value


def finish_kernel(
    ends_y, y_factor, y_back, y_rest, own, near, pair, quad, z_factor, z_back, z_rest, z_mid, solved_x,
    out, acc,
):
    index = lax.axis_index("depth")
    zero = jnp.zeros((ROWS, COLS), F32)
    left_ground, left_source, right_ground, right_source = zero, zero, zero, zero
    for bit, ref in ((4, quad), (2, pair), (1, near)):
        on_left = (index & bit) != 0
        c, ng, fg, ns, fs = (ref[place] for place in range(5))
        ground, source = ng + left_ground, ns + left_source
        share = c / (c + ground)
        left_ground = jnp.where(on_left, fg + share * ground, left_ground)
        left_source = jnp.where(on_left, fs + share * source, left_source)
        ground, source = fg + right_ground, fs + right_source
        total = c + ground
        share = jnp.where(total > 0.0, c / jnp.where(total > 0.0, total, 1.0), 0.0)
        right_ground = jnp.where(on_left, right_ground, ng + share * ground)
        right_source = jnp.where(on_left, right_source, ns + share * source)
    c, ng, fg, ns, fs = (own[place] for place in range(5))
    ground, source = fg + right_ground, fs + right_source
    total = c + ground
    inverse = jnp.where(total > 0.0, 1.0 / jnp.where(total > 0.0, total, 1.0), 0.0)
    share = c * inverse
    first = (left_source + ns + share * source) / (left_ground + ng + share * ground)
    after = share * first + source * inverse
    middle = z_mid[0] * first + z_mid[1] * after + z_mid[2]
    half = PLANES // 2
    y_first = ends_y[:, 0, :]
    value = ends_y[:, 1, :]
    acc[pl.ds(0, PLANES, stride=ROWS), :] = y_first
    acc[pl.ds(ROWS - 1, PLANES, stride=ROWS), :] = value
    for row in range(ROWS - 2, 0, -1):
        value = y_factor[row] * value + (y_back[row] * y_first + y_rest[row])
        acc[pl.ds(row, PLANES, stride=ROWS), :] = value
    third = 1.0 / 3.0
    for start, near_value, far_value in ((0, first, middle), (half, middle, after)):
        value = far_value
        for plane in range(start + half - 1, start, -1):
            span = slice(plane * ROWS, (plane + 1) * ROWS)
            value = z_factor[span, :] * value + (z_back[span, :] * near_value + z_rest[span, :])
            out[span, :] = (solved_x[span, :] + acc[span, :] + value) * third
        span = slice(start * ROWS, (start + 1) * ROWS)
        out[span, :] = (solved_x[span, :] + acc[span, :] + near_value) * third


def call(kernel, outs, scratch=(), flops=1000000, moved=500000, **options):
    return pl.pallas_call(
        kernel,
        out_shape=outs,
        scratch_shapes=scratch,
        compiler_params=pltpu.CompilerParams(vmem_limit_bytes=16 * 1024 * 1024),
        cost_estimate=pl.CostEstimate(flops=flops, bytes_accessed=moved, transcendentals=0),
        **options,
    )


def shaped(*shape):
    return jax.ShapeDtypeStruct(shape, F32)


def line_perm(axis, step):
    count = lax.axis_size(axis)
    if step > 0:
        return [(i, i + 1) for i in range(count - 1)]
    return [(i + 1, i) for i in range(count - 1)]


def swap_perm(axis, bit):
    return [(i, i ^ bit) for i in range(lax.axis_size(axis))]


def next_perm(axis):
    pairs = []
    for i in range(1, lax.axis_size(axis) - 1, 2):
        pairs += [(i, i + 1), (i + 1, i)]
    return pairs


def shards(volume):
    flat = volume.reshape(PLANES * ROWS, COLS)
    lines = shaped(ROWS, PLANES, COLS)
    whole = shaped(PLANES * ROWS, COLS)
    tall = shaped((PLANES + 1) * ROWS, COLS)
    port = shaped(5, ROWS, COLS)
    side = shaped(PLANES + 1, COLS)
    to_near, to_far = call(
        edge_kernel,
        (shaped(2 * ROWS, COLS), shaped(2 * ROWS, COLS)),
        (pltpu.SemaphoreType.DMA((2,)),),
        in_specs=[pl.BlockSpec(memory_space=pl.ANY)],
    )(flat)
    far_side = lax.ppermute(to_far, "depth", next_perm("depth"))
    near_side = lax.ppermute(to_near, "depth", swap_perm("depth", 1))
    deep, row_low, row_high = call(
        deep_kernel, (tall, side, side), (pltpu.VMEM((PLANES + 3, ROWS, COLS), F32),)
    )(flat, near_side, far_side)
    low_row = lax.ppermute(row_high, "lat", line_perm("lat", 1))
    high_row = lax.ppermute(row_low, "lat", line_perm("lat", -1))
    z_port, z_factor, z_back, z_rest, z_mid, smooth = call(
        plane_kernel, (port, whole, whole, whole, shaped(3, ROWS, COLS), tall)
    )(flat, deep, low_row, high_row)
    near = lax.ppermute(z_port, "depth", swap_perm("depth", 1))
    y_port, y_factor, y_back, y_rest = call(row_kernel, (shaped(PLANES * PORT, COLS), lines, lines, lines))(
        flat, smooth
    )
    pair_own = call(lambda *refs: join_kernel(1, *refs), port)(z_port, near)
    flat_later, smooth_later, pair_own = lax.optimization_barrier((flat, smooth, pair_own))
    pair = lax.ppermute(pair_own, "depth", swap_perm("depth", 2))
    solved_x = call(
        column_kernel,
        whole,
        (
            pltpu.VMEM((512, COLS), F32),
            pltpu.VMEM((512, COLS), F32),
            pltpu.VMEM((16, 32, COLS), F32),
            pltpu.VMEM((16, 32, COLS), F32),
            pltpu.VMEM((16, 32, COLS), F32),
        ),
    )(flat_later, smooth_later)
    y_port, solved_x = lax.optimization_barrier((y_port, solved_x))
    ports = lax.all_to_all(y_port, "lat", 0, 0, tiled=True)
    ports, pair = lax.optimization_barrier((ports, pair))
    quad_own = call(lambda *refs: join_kernel(2, *refs), port)(pair_own, pair)
    ports, quad_own = lax.optimization_barrier((ports, quad_own))
    quad = lax.ppermute(quad_own, "depth", swap_perm("depth", 4))
    ends = call(row_reduced_kernel, shaped(BLOCKS, 2, COLS))(ports)
    ends_y = lax.all_to_all(ends, "lat", 0, 0, tiled=True)
    ends_y, quad = lax.optimization_barrier((ends_y, quad))
    out = call(finish_kernel, whole, (pltpu.VMEM((PLANES * ROWS, COLS), F32),))(
        ends_y, y_factor, y_back, y_rest, z_port, near, pair, quad, z_factor, z_back, z_rest, z_mid, solved_x
    )
    return out.reshape(PLANES, ROWS, COLS)


def solution(mesh):
    placed = (P("depth", "lat", None),)
    return jax.shard_map(
        shards, mesh=mesh, in_specs=placed, out_specs=P("depth", "lat", None), check_vma=False
    )
```

```python
import jax
import jax.numpy as jnp
from jax import lax
from jax.experimental import pallas as pl
from jax.experimental.pallas import tpu as pltpu
from jax.sharding import PartitionSpec as P

TAU3 = 900.0
INV_LAMBDA_SQ = 4.0
PLANES = 32
ROWS = 16
COLS = 128
BLOCKS = 32
PORT = 16
LONG = 100_000_000_000
F32 = jnp.float32


def resistance(diff):
    return (1.0 + INV_LAMBDA_SQ * (diff * diff)) * (1.0 / TAU3)


def smooth_lanes(field, first, last):
    before = jnp.where(first, 0.0, pltpu.roll(field, 1, field.ndim - 1))
    after = jnp.where(last, 0.0, pltpu.roll(field, COLS - 1, field.ndim - 1))
    return 0.25 * (before + 2.0 * field + after)


def eliminate(coupling, ground, source, near_ground, near_source, resist):
    factor = 1.0 / (1.0 + (coupling + ground) * resist)
    weight = factor * resist
    back = coupling * weight
    near_ground = near_ground + back * ground
    near_source = near_source + back * source
    saved = (factor, back, source * weight)
    return coupling * factor, ground * factor, source * factor, near_ground, near_source, saved


def eliminate_last(coupling, ground, source, near_ground, near_source, conduct):
    inverse = 1.0 / (coupling + ground + conduct)
    factor = conduct * inverse
    back = coupling * inverse
    near_ground = near_ground + back * ground
    near_source = near_source + back * source
    saved = (factor, back, source * inverse)
    return coupling * factor, ground * factor, source * factor, near_ground, near_source, saved


def join(left, right):
    lc, lg, lh, ls, lt = left
    rc, rg, rh, rs, rt = right
    ground = lh + rg
    source = lt + rs
    inverse = 1.0 / (lc + rc + ground)
    to_left = lc * inverse
    to_right = rc * inverse
    return (
        lc * to_right,
        lg + to_left * ground,
        rh + to_right * ground,
        ls + to_left * source,
        rt + to_right * source,
    ), (to_left, to_right, source * inverse)


def edge_kernel(vol, near_side, far_side, sems):
    odd = lax.axis_index("depth") & 1
    high = (PLANES - 2) * ROWS
    near_start = pl.multiple_of((1 - odd) * high, ROWS)
    far_start = pl.multiple_of(odd * high, ROWS)
    copies = (
        pltpu.make_async_copy(vol.at[pl.ds(near_start, 2 * ROWS), :], near_side, sems.at[0]),
        pltpu.make_async_copy(vol.at[pl.ds(far_start, 2 * ROWS), :], far_side, sems.at[1]),
    )
    for copy in copies:
        copy.start()
    for copy in copies:
        copy.wait()


def strided(ref, row):
    return ref[pl.ds(row, 32, stride=16), :]


def cells(ref, plane):
    return ref[plane * ROWS : (plane + 1) * ROWS, :]


def deep_kernel(vol, near_side, far_side, deep, pair_row, next_row, mixed):
    odd = (lax.axis_index("depth") & 1) == 1
    lane = lax.broadcasted_iota(jnp.int32, (ROWS, COLS), 1)
    first, last = lane == 0, lane == COLS - 1
    mixed[0] = smooth_lanes(jnp.where(odd, cells(near_side, 1), cells(far_side, 1)), first, last)
    for plane in range(PLANES):
        mixed[plane + 1] = smooth_lanes(cells(vol, plane), first, last)
    for plane in range(2):
        mixed[PLANES + 1 + plane] = smooth_lanes(
            jnp.where(odd, cells(far_side, plane), cells(near_side, plane)), first, last
        )
    for plane in range(PLANES + 1):
        deep[plane * ROWS : (plane + 1) * ROWS, :] = 0.25 * (
            mixed[plane] + 2.0 * mixed[plane + 1] + mixed[plane + 2]
        )
    odd_row = (lax.axis_index("lat") & 1) == 1
    low = deep[pl.ds(0, PLANES + 1, stride=ROWS), :]
    high = deep[pl.ds(ROWS - 1, PLANES + 1, stride=ROWS), :]
    pair_row[...] = jnp.where(odd_row, low, high)
    next_row[...] = jnp.where(odd_row, high, low)


def plane_kernel(vol, deep, pair_row, next_row, port, factor, back, rest, mid, smooth):
    odd_row = (lax.axis_index("lat") & 1) == 1
    low_row = jnp.where(odd_row, pair_row[...], next_row[...])
    high_row = jnp.where(odd_row, next_row[...], pair_row[...])
    depth_last = lax.axis_index("depth") == lax.axis_size("depth") - 1
    z_open = jnp.where(depth_last, 0.0, TAU3).astype(F32)
    row_index = lax.broadcasted_iota(jnp.int32, (ROWS, COLS), 0)
    top, bottom = row_index == 0, row_index == ROWS - 1
    for plane in range(PLANES + 1):
        span = slice(plane * ROWS, (plane + 1) * ROWS)
        here = deep[span, :]
        above = jnp.where(top, low_row[plane : plane + 1, :], pltpu.roll(here, 1, 0))
        below = jnp.where(bottom, high_row[plane : plane + 1, :], pltpu.roll(here, ROWS - 1, 0))
        smooth[span, :] = 0.25 * (above + 2.0 * here + below)

    def resist(plane):
        return resistance(cells(smooth, plane + 1) - cells(smooth, plane))

    half = PLANES // 2
    one = jnp.ones((ROWS, COLS), F32)
    states = [
        (1.0 / resist(start), one, cells(vol, start + 1), one, cells(vol, start)) for start in (0, half)
    ]
    for step in range(1, half):
        final = step == half - 1
        for part in range(2):
            plane = part * half + step
            span = slice(plane * ROWS, (plane + 1) * ROWS)
            if final and part == 1:
                *state, saved = eliminate_last(*states[part], z_open / (TAU3 * resist(plane)))
            else:
                *state, saved = eliminate(*states[part], resist(plane))
            if not final:
                state[1] = state[1] + 1.0
                state[2] = state[2] + cells(vol, plane + 1)
            states[part] = state
            factor[span, :], back[span, :], rest[span, :] = saved
    joined, middle = join(*[(c, ng, fg, ns, fs) for c, fg, fs, ng, ns in states])
    for place, value in enumerate(joined):
        port[place] = value
    for place, value in enumerate(middle):
        mid[place] = value


def row_kernel(vol, deep, port, factor, back, rest):
    part = [strided(deep, row) for row in range(ROWS)]
    low_sum = 2.0 * part[0] + part[1]
    high_sum = part[ROWS - 2] + 2.0 * part[ROWS - 1]
    smooth = [None] + [0.25 * (part[r - 1] + 2.0 * part[r] + part[r + 1]) for r in range(1, ROWS - 1)]
    one = jnp.ones((PLANES, COLS), F32)
    state = (1.0 / resistance(smooth[2] - smooth[1]), one, strided(vol, 2), one, strided(vol, 1))
    for row in range(2, ROWS - 2):
        *state, saved = eliminate(*state, resistance(smooth[row + 1] - smooth[row]))
        state[1] = state[1] + 1.0
        state[2] = state[2] + strided(vol, row + 1)
        factor[row], back[row], rest[row] = saved
    coupling, far_ground, far_source, near_ground, near_source = state
    values = (
        coupling, near_ground, far_ground, near_source, far_source,
        part[0], part[ROWS - 1], low_sum, high_sum, smooth[1], smooth[ROWS - 2],
        strided(vol, 0), strided(vol, ROWS - 1),
    )
    for place, value in enumerate(values):
        port[pl.ds(place, PLANES, stride=PORT), :] = value
    for place in range(len(values), PORT):
        port[pl.ds(place, PLANES, stride=PORT), :] = jnp.zeros((PLANES, COLS), F32)


def chain_solve(coupling, near_ground, far_ground, near_source, far_source, count):
    size = coupling.shape[0]
    right = coupling
    ground = near_ground + pltpu.roll(far_ground, 1, 0)
    source = near_source + pltpu.roll(far_source, 1, 0)
    step = 1
    while step < count:
        left = pltpu.roll(right, step, 0)
        inverse = 1.0 / (ground + left + right)
        ground_part = ground * inverse
        source_part = source * inverse
        ground = (
            ground
            + left * pltpu.roll(ground_part, step, 0)
            + right * pltpu.roll(ground_part, size - step, 0)
        )
        source = (
            source
            + left * pltpu.roll(source_part, step, 0)
            + right * pltpu.roll(source_part, size - step, 0)
        )
        right = right * pltpu.roll(right * inverse, size - step, 0)
        step *= 2
    return source / ground


def column_kernel(vol, smooth, solved_x, turned, turned_smooth, factor, back, rest):
    for group in range(4):
        span = slice(group * COLS, (group + 1) * COLS)
        turned[span, :] = vol[span, :].T
        turned_smooth[span, :] = smooth[span, :].T

    def resist(step):
        if step < 15:
            return resistance(strided(turned_smooth, step + 1) - strided(turned_smooth, step))
        return resistance(pltpu.roll(strided(turned_smooth, 0), 31, 0) - strided(turned_smooth, 15))

    chunk_last = (lax.broadcasted_iota(jnp.int32, (32, COLS), 0) & 7) == 7
    one = jnp.ones((32, COLS), F32)
    state = (1.0 / resist(0), one, strided(turned, 1), one, strided(turned, 0))
    for step in range(1, 16):
        if step == 15:
            *state, saved = eliminate_last(*state, jnp.where(chunk_last, 0.0, 1.0 / resist(step)))
        else:
            *state, saved = eliminate(*state, resist(step))
            state[1] = state[1] + 1.0
            state[2] = state[2] + strided(turned, step + 1)
        factor[step], back[step], rest[step] = saved
    coupling, far_ground, far_source, near_ground, near_source = state
    first = chain_solve(coupling, near_ground, far_ground, near_source, far_source, 8)
    turned[pl.ds(0, 32, stride=16), :] = first
    value = pltpu.roll(first, 31, 0)
    for step in range(15, 0, -1):
        value = factor[step] * value + (back[step] * first + rest[step])
        turned[pl.ds(step, 32, stride=16), :] = value
    for group in range(4):
        span = slice(group * COLS, (group + 1) * COLS)
        solved_x[span, :] = turned[span, :].T


def row_reduced_kernel(ports, out):
    (
        coupling, near_ground, far_ground, near_source, far_source,
        low, high, low_sum, high_sum, low_smooth, high_smooth, low_cell, high_cell,
    ) = (ports[pl.ds(place, BLOCKS, stride=PORT), :] for place in range(13))
    block = lax.broadcasted_iota(jnp.int32, (BLOCKS, COLS), 0)
    block_first, block_last = block == 0, block == BLOCKS - 1
    low_end = 0.25 * (jnp.where(block_first, 0.0, pltpu.roll(high, 1, 0)) + low_sum)
    high_end = 0.25 * (high_sum + jnp.where(block_last, 0.0, pltpu.roll(low, BLOCKS - 1, 0)))
    enter = 1.0 / resistance(low_smooth - low_end)
    leave = 1.0 / resistance(high_end - high_smooth)
    across = pltpu.roll(low_end, BLOCKS - 1, 0) - high_end
    across = jnp.where(block_last, 0.0, 1.0 / resistance(across))
    zero = jnp.zeros_like(coupling)
    one = jnp.ones_like(coupling)
    before, at_low = join(
        (enter, one, zero, low_cell, zero), (coupling, near_ground, far_ground, near_source, far_source)
    )
    after, at_high = join((leave, zero, one, zero, high_cell), (across, zero, zero, zero, zero))
    whole, between = join(before, after)
    first = chain_solve(*whole, BLOCKS)
    later = pltpu.roll(first, BLOCKS - 1, 0)

    def middle(weights, left, right):
        return weights[0] * left + weights[1] * right + weights[2]

    inner_high = middle(between, first, later)
    out[:, 0, :] = first
    out[:, 1, :] = middle(at_low, first, inner_high)
    out[:, 2, :] = inner_high
    out[:, 3, :] = middle(at_high, inner_high, later)


def pick(flag, there, here):
    return tuple(jnp.where(flag, a, b) for a, b in zip(there, here))


def join_kernel(bit, own, other, out):
    upper = (lax.axis_index("depth") & bit) != 0
    mine = tuple(own[place] for place in range(5))
    theirs = tuple(other[place] for place in range(5))
    port, _ = join(pick(upper, theirs, mine), pick(upper, mine, theirs))
    for place, value in enumerate(port):
        out[place] = value


def finish_plane_kernel(
    own, near, pair, across, skew, factor, back, rest, mid, solved_x, out,
):
    index = lax.axis_index("depth")
    odd = (index & 2) != 0
    straight = tuple(across[place] for place in range(5))
    crossed = tuple(skew[place] for place in range(5))
    quad, _ = join(pick(odd, crossed, straight), pick(odd, straight, crossed))
    zero = jnp.zeros((ROWS, COLS), F32)
    left_ground, left_source, right_ground, right_source = zero, zero, zero, zero
    for bit, ref in ((4, quad), (2, pair), (1, near)):
        on_left = (index & bit) != 0
        c, ng, fg, ns, fs = (ref[place] for place in range(5))
        ground, source = ng + left_ground, ns + left_source
        share = c / (c + ground)
        left_ground = jnp.where(on_left, fg + share * ground, left_ground)
        left_source = jnp.where(on_left, fs + share * source, left_source)
        ground, source = fg + right_ground, fs + right_source
        total = c + ground
        share = jnp.where(total > 0.0, c / jnp.where(total > 0.0, total, 1.0), 0.0)
        right_ground = jnp.where(on_left, right_ground, ng + share * ground)
        right_source = jnp.where(on_left, right_source, ns + share * source)
    c, ng, fg, ns, fs = (own[place] for place in range(5))
    ground, source = fg + right_ground, fs + right_source
    total = c + ground
    inverse = jnp.where(total > 0.0, 1.0 / jnp.where(total > 0.0, total, 1.0), 0.0)
    share = c * inverse
    first = (left_source + ns + share * source) / (left_ground + ng + share * ground)
    after = share * first + source * inverse
    middle = mid[0] * first + mid[1] * after + mid[2]
    half = PLANES // 2
    for start, near_value, far_value in ((0, first, middle), (half, middle, after)):
        value = far_value
        for plane in range(start + half - 1, start, -1):
            span = slice(plane * ROWS, (plane + 1) * ROWS)
            value = factor[span, :] * value + (back[span, :] * near_value + rest[span, :])
            out[span, :] = solved_x[span, :] + value
        span = slice(start * ROWS, (start + 1) * ROWS)
        out[span, :] = solved_x[span, :] + near_value


def finish_row_kernel(ends, factor, back, rest, others, out):
    third = 1.0 / 3.0

    def put(row, value):
        place = pl.ds(row, PLANES, stride=ROWS)
        out[place, :] = (others[place, :] + value) * third

    for place, row in ((0, 0), (1, 1), (2, ROWS - 2), (3, ROWS - 1)):
        put(row, ends[:, place, :])
    first = ends[:, 1, :]
    value = ends[:, 2, :]
    for row in range(ROWS - 3, 1, -1):
        value = factor[row] * value + (back[row] * first + rest[row])
        put(row, value)


def call(kernel, outs, scratch=(), flops=1000000, moved=500000, **options):
    return pl.pallas_call(
        kernel,
        out_shape=outs,
        scratch_shapes=scratch,
        compiler_params=pltpu.CompilerParams(vmem_limit_bytes=16 * 1024 * 1024),
        cost_estimate=pl.CostEstimate(flops=flops, bytes_accessed=moved, transcendentals=0),
        **options,
    )


def shaped(*shape):
    return jax.ShapeDtypeStruct(shape, F32)


def line_perm(axis, step):
    count = lax.axis_size(axis)
    if step > 0:
        return [(i, i + 1) for i in range(count - 1)]
    return [(i + 1, i) for i in range(count - 1)]


def swap_perm(axis, bit):
    return [(i, i ^ bit) for i in range(lax.axis_size(axis))]


def next_perm(axis):
    pairs = []
    for i in range(1, lax.axis_size(axis) - 1, 2):
        pairs += [(i, i + 1), (i + 1, i)]
    return pairs


def shards(volume):
    flat = volume.reshape(PLANES * ROWS, COLS)
    lines = shaped(ROWS, PLANES, COLS)
    whole = shaped(PLANES * ROWS, COLS)
    tall = shaped((PLANES + 1) * ROWS, COLS)
    port = shaped(5, ROWS, COLS)
    side = shaped(PLANES + 1, COLS)
    to_near, to_far = call(
        edge_kernel,
        (shaped(2 * ROWS, COLS), shaped(2 * ROWS, COLS)),
        (pltpu.SemaphoreType.DMA((2,)),),
        in_specs=[pl.BlockSpec(memory_space=pl.ANY)],
    )(flat)
    far_side = lax.ppermute(to_far, "depth", next_perm("depth"))
    near_side = lax.ppermute(to_near, "depth", swap_perm("depth", 1))
    deep, to_pair, to_next = call(
        deep_kernel, (tall, side, side), (pltpu.VMEM((PLANES + 3, ROWS, COLS), F32),)
    )(flat, near_side, far_side)
    next_row = lax.ppermute(to_next, "lat", next_perm("lat"))
    pair_row = lax.ppermute(to_pair, "lat", swap_perm("lat", 1))
    y_port, y_factor, y_back, y_rest = call(row_kernel, (shaped(PLANES * PORT, COLS), lines, lines, lines))(
        flat, deep
    )
    ports = lax.all_to_all(y_port, "lat", 0, 0, tiled=True)
    z_port, z_factor, z_back, z_rest, z_mid, smooth = call(
        plane_kernel, (port, whole, whole, whole, shaped(3, ROWS, COLS), tall), moved=500000,flops=LONG
    )(flat, deep, pair_row, next_row)
    near = lax.ppermute(z_port, "depth", swap_perm("depth", 1))
    solved_x = call(
        column_kernel,
        whole,
        (
            pltpu.VMEM((512, COLS), F32),
            pltpu.VMEM((512, COLS), F32),
            pltpu.VMEM((16, 32, COLS), F32),
            pltpu.VMEM((16, 32, COLS), F32),
            pltpu.VMEM((16, 32, COLS), F32),
        ),
    )(flat, smooth)
    pair_own = call(lambda *refs: join_kernel(1, *refs), port)(z_port, near)
    ports, pair_own, solved_x = lax.optimization_barrier((ports, pair_own, solved_x))
    ends = call(row_reduced_kernel, shaped(BLOCKS, 4, COLS))(ports)
    across, skew, pair = (lax.ppermute(pair_own, "depth", swap_perm("depth", bits)) for bits in (4, 6, 2))
    others = call(finish_plane_kernel, whole, flops=LONG)(
        z_port, near, pair, across, skew, z_factor, z_back, z_rest, z_mid, solved_x
    )
    ends_y = lax.all_to_all(ends, "lat", 0, 0, tiled=True)
    out = call(finish_row_kernel, whole)(ends_y, y_factor, y_back, y_rest, others)
    return out.reshape(PLANES, ROWS, COLS)


def solution(mesh):
    placed = (P("depth", "lat", None),)
    return jax.shard_map(
        shards, mesh=mesh, in_specs=placed, out_specs=P("depth", "lat", None), check_vma=False
    )
```

```python
import jax
import jax.numpy as jnp
from jax import lax
from jax.experimental import pallas as pl
from jax.experimental.pallas import tpu as pltpu
from jax.sharding import PartitionSpec as P

TAU3 = 900.0
INV_LAMBDA_SQ = 4.0
PLANES = 32
ROWS = 16
COLS = 128
BLOCKS = 32
PORT = 16
RETURN = 8
F32 = jnp.float32


def resistance(diff):
    return (1.0 + INV_LAMBDA_SQ * (diff * diff)) * (1.0 / TAU3)


def smooth_lanes(field, first, last):
    before = jnp.where(first, 0.0, pltpu.roll(field, 1, field.ndim - 1))
    after = jnp.where(last, 0.0, pltpu.roll(field, COLS - 1, field.ndim - 1))
    return 0.25 * (before + 2.0 * field + after)


def eliminate(coupling, ground, source, near_ground, near_source, resist):
    factor = 1.0 / (1.0 + (coupling + ground) * resist)
    weight = factor * resist
    back = coupling * weight
    near_ground = near_ground + back * ground
    near_source = near_source + back * source
    saved = (factor, back, source * weight)
    return coupling * factor, ground * factor, source * factor, near_ground, near_source, saved


def eliminate_last(coupling, ground, source, near_ground, near_source, conduct):
    inverse = 1.0 / (coupling + ground + conduct)
    factor = conduct * inverse
    back = coupling * inverse
    near_ground = near_ground + back * ground
    near_source = near_source + back * source
    saved = (factor, back, source * inverse)
    return coupling * factor, ground * factor, source * factor, near_ground, near_source, saved


def join(left, right):
    lc, lg, lh, ls, lt = left
    rc, rg, rh, rs, rt = right
    ground = lh + rg
    source = lt + rs
    inverse = 1.0 / (lc + rc + ground)
    to_left = lc * inverse
    to_right = rc * inverse
    return (
        lc * to_right,
        lg + to_left * ground,
        rh + to_right * ground,
        ls + to_left * source,
        rt + to_right * source,
    ), (to_left, to_right, source * inverse)


def edge_kernel(vol, near_side, far_side, sems):
    odd = lax.axis_index("depth") & 1
    high = (PLANES - 2) * ROWS
    near_start = pl.multiple_of((1 - odd) * high, ROWS)
    far_start = pl.multiple_of(odd * high, ROWS)
    copies = (
        pltpu.make_async_copy(vol.at[pl.ds(near_start, 2 * ROWS), :], near_side, sems.at[0]),
        pltpu.make_async_copy(vol.at[pl.ds(far_start, 2 * ROWS), :], far_side, sems.at[1]),
    )
    for copy in copies:
        copy.start()
    for copy in copies:
        copy.wait()


def strided(ref, row):
    return ref[pl.ds(row, 32, stride=16), :]


def cells(ref, plane):
    return ref[plane * ROWS : (plane + 1) * ROWS, :]


def deep_kernel(vol, near_side, far_side, deep, mixed):
    odd = (lax.axis_index("depth") & 1) == 1
    lane = lax.broadcasted_iota(jnp.int32, (ROWS, COLS), 1)
    first, last = lane == 0, lane == COLS - 1
    mixed[0] = smooth_lanes(jnp.where(odd, cells(near_side, 1), cells(far_side, 1)), first, last)
    for plane in range(PLANES):
        mixed[plane + 1] = smooth_lanes(cells(vol, plane), first, last)
    for plane in range(2):
        mixed[PLANES + 1 + plane] = smooth_lanes(
            jnp.where(odd, cells(far_side, plane), cells(near_side, plane)), first, last
        )
    for plane in range(PLANES + 1):
        deep[plane * ROWS : (plane + 1) * ROWS, :] = 0.25 * (
            mixed[plane] + 2.0 * mixed[plane + 1] + mixed[plane + 2]
        )


def plane_kernel(vol, deep, ends, port, factor, back, rest, mid, smooth):
    low_row, high_row = (
        [ends[plane * RETURN + place : plane * RETURN + place + 1, :] for plane in range(PLANES)]
        + [ends[place + 2 : place + 3, :]]
        for place in (4, 5)
    )
    depth_last = lax.axis_index("depth") == lax.axis_size("depth") - 1
    z_open = jnp.where(depth_last, 0.0, TAU3).astype(F32)
    row_index = lax.broadcasted_iota(jnp.int32, (ROWS, COLS), 0)
    top, bottom = row_index == 0, row_index == ROWS - 1
    for plane in range(PLANES + 1):
        span = slice(plane * ROWS, (plane + 1) * ROWS)
        here = deep[span, :]
        above = jnp.where(top, low_row[plane], pltpu.roll(here, 1, 0))
        below = jnp.where(bottom, high_row[plane], pltpu.roll(here, ROWS - 1, 0))
        smooth[span, :] = 0.25 * (above + 2.0 * here + below)

    def resist(plane):
        return resistance(cells(smooth, plane + 1) - cells(smooth, plane))

    half = PLANES // 2
    one = jnp.ones((ROWS, COLS), F32)
    states = [
        (1.0 / resist(start), one, cells(vol, start + 1), one, cells(vol, start)) for start in (0, half)
    ]
    for step in range(1, half):
        final = step == half - 1
        for part in range(2):
            plane = part * half + step
            span = slice(plane * ROWS, (plane + 1) * ROWS)
            if final and part == 1:
                *state, saved = eliminate_last(*states[part], z_open / (TAU3 * resist(plane)))
            else:
                *state, saved = eliminate(*states[part], resist(plane))
            if not final:
                state[1] = state[1] + 1.0
                state[2] = state[2] + cells(vol, plane + 1)
            states[part] = state
            factor[span, :], back[span, :], rest[span, :] = saved
    joined, middle = join(*[(c, ng, fg, ns, fs) for c, fg, fs, ng, ns in states])
    for place, value in enumerate(joined):
        port[place] = value
    for place, value in enumerate(middle):
        mid[place] = value


def row_kernel(vol, deep, port, factor, back, rest):
    part = [strided(deep, row) for row in range(ROWS)]
    low_sum = 2.0 * part[0] + part[1]
    high_sum = part[ROWS - 2] + 2.0 * part[ROWS - 1]
    smooth = [None] + [0.25 * (part[r - 1] + 2.0 * part[r] + part[r + 1]) for r in range(1, ROWS - 1)]
    one = jnp.ones((PLANES, COLS), F32)
    state = (1.0 / resistance(smooth[2] - smooth[1]), one, strided(vol, 2), one, strided(vol, 1))
    for row in range(2, ROWS - 2):
        *state, saved = eliminate(*state, resistance(smooth[row + 1] - smooth[row]))
        state[1] = state[1] + 1.0
        state[2] = state[2] + strided(vol, row + 1)
        factor[row], back[row], rest[row] = saved
    coupling, far_ground, far_source, near_ground, near_source = state
    values = (
        coupling, near_ground, far_ground, near_source, far_source,
        part[0], part[ROWS - 1], low_sum, high_sum, smooth[1], smooth[ROWS - 2],
        strided(vol, 0), strided(vol, ROWS - 1),
        jnp.broadcast_to(deep[PLANES * ROWS : PLANES * ROWS + 1, :], (PLANES, COLS)),
        jnp.broadcast_to(deep[(PLANES + 1) * ROWS - 1 : (PLANES + 1) * ROWS, :], (PLANES, COLS)),
    )
    for place, value in enumerate(values):
        port[pl.ds(place, PLANES, stride=PORT), :] = value
    for place in range(len(values), PORT):
        port[pl.ds(place, PLANES, stride=PORT), :] = jnp.zeros((PLANES, COLS), F32)


def chain_solve(coupling, near_ground, far_ground, near_source, far_source, count):
    size = coupling.shape[0]
    right = coupling
    ground = near_ground + pltpu.roll(far_ground, 1, 0)
    source = near_source + pltpu.roll(far_source, 1, 0)
    step = 1
    while step < count:
        left = pltpu.roll(right, step, 0)
        inverse = 1.0 / (ground + left + right)
        ground_part = ground * inverse
        source_part = source * inverse
        ground = (
            ground
            + left * pltpu.roll(ground_part, step, 0)
            + right * pltpu.roll(ground_part, size - step, 0)
        )
        source = (
            source
            + left * pltpu.roll(source_part, step, 0)
            + right * pltpu.roll(source_part, size - step, 0)
        )
        right = right * pltpu.roll(right * inverse, size - step, 0)
        step *= 2
    return source / ground


def column_kernel(vol, smooth, solved_x, turned, turned_smooth, factor, back, rest):
    for group in range(4):
        span = slice(group * COLS, (group + 1) * COLS)
        turned[span, :] = vol[span, :].T
        turned_smooth[span, :] = smooth[span, :].T

    def resist(step):
        if step < 15:
            return resistance(strided(turned_smooth, step + 1) - strided(turned_smooth, step))
        return resistance(pltpu.roll(strided(turned_smooth, 0), 31, 0) - strided(turned_smooth, 15))

    chunk_last = (lax.broadcasted_iota(jnp.int32, (32, COLS), 0) & 7) == 7
    one = jnp.ones((32, COLS), F32)
    state = (1.0 / resist(0), one, strided(turned, 1), one, strided(turned, 0))
    for step in range(1, 16):
        if step == 15:
            *state, saved = eliminate_last(*state, jnp.where(chunk_last, 0.0, 1.0 / resist(step)))
        else:
            *state, saved = eliminate(*state, resist(step))
            state[1] = state[1] + 1.0
            state[2] = state[2] + strided(turned, step + 1)
        factor[step], back[step], rest[step] = saved
    coupling, far_ground, far_source, near_ground, near_source = state
    first = chain_solve(coupling, near_ground, far_ground, near_source, far_source, 8)
    turned[pl.ds(0, 32, stride=16), :] = first
    value = pltpu.roll(first, 31, 0)
    for step in range(15, 0, -1):
        value = factor[step] * value + (back[step] * first + rest[step])
        turned[pl.ds(step, 32, stride=16), :] = value
    for group in range(4):
        span = slice(group * COLS, (group + 1) * COLS)
        solved_x[span, :] = turned[span, :].T


def row_reduced_kernel(ports, out):
    (
        coupling, near_ground, far_ground, near_source, far_source,
        low, high, low_sum, high_sum, low_smooth, high_smooth, low_cell, high_cell, low_corner, high_corner,
    ) = (ports[pl.ds(place, BLOCKS, stride=PORT), :] for place in range(15))
    block = lax.broadcasted_iota(jnp.int32, (BLOCKS, COLS), 0)
    block_first, block_last = block == 0, block == BLOCKS - 1

    def below(value):
        return jnp.where(block_first, 0.0, pltpu.roll(value, 1, 0))

    def above(value):
        return jnp.where(block_last, 0.0, pltpu.roll(value, BLOCKS - 1, 0))

    before_row, after_row = below(high), above(low)
    low_end = 0.25 * (before_row + low_sum)
    high_end = 0.25 * (high_sum + after_row)
    enter = 1.0 / resistance(low_smooth - low_end)
    leave = 1.0 / resistance(high_end - high_smooth)
    across = pltpu.roll(low_end, BLOCKS - 1, 0) - high_end
    across = jnp.where(block_last, 0.0, 1.0 / resistance(across))
    zero = jnp.zeros_like(coupling)
    one = jnp.ones_like(coupling)
    before, at_low = join(
        (enter, one, zero, low_cell, zero), (coupling, near_ground, far_ground, near_source, far_source)
    )
    after, at_high = join((leave, zero, one, zero, high_cell), (across, zero, zero, zero, zero))
    whole, between = join(before, after)
    first = chain_solve(*whole, BLOCKS)
    later = pltpu.roll(first, BLOCKS - 1, 0)

    def middle(weights, left, right):
        return weights[0] * left + weights[1] * right + weights[2]

    inner_high = middle(between, first, later)
    values = (
        first, middle(at_low, first, inner_high), inner_high, middle(at_high, inner_high, later),
        before_row, after_row, below(high_corner), above(low_corner),
    )
    for place, value in enumerate(values):
        out[pl.ds(place, BLOCKS, stride=RETURN), :] = value


def pick(flag, there, here):
    return tuple(jnp.where(flag, a, b) for a, b in zip(there, here))


def join_kernel(bit, own, other, out):
    upper = (lax.axis_index("depth") & bit) != 0
    mine = tuple(own[place] for place in range(5))
    theirs = tuple(other[place] for place in range(5))
    port, _ = join(pick(upper, theirs, mine), pick(upper, mine, theirs))
    for place, value in enumerate(port):
        out[place] = value


def finish_plane_kernel(
    own, near, pair, across, skew, factor, back, rest, mid, others, out,
):
    index = lax.axis_index("depth")
    odd = (index & 2) != 0
    straight = tuple(across[place] for place in range(5))
    crossed = tuple(skew[place] for place in range(5))
    quad, _ = join(pick(odd, crossed, straight), pick(odd, straight, crossed))
    zero = jnp.zeros((ROWS, COLS), F32)
    left_ground, left_source, right_ground, right_source = zero, zero, zero, zero
    for bit, ref in ((4, quad), (2, pair), (1, near)):
        on_left = (index & bit) != 0
        c, ng, fg, ns, fs = (ref[place] for place in range(5))
        ground, source = ng + left_ground, ns + left_source
        share = c / (c + ground)
        left_ground = jnp.where(on_left, fg + share * ground, left_ground)
        left_source = jnp.where(on_left, fs + share * source, left_source)
        ground, source = fg + right_ground, fs + right_source
        total = c + ground
        share = jnp.where(total > 0.0, c / jnp.where(total > 0.0, total, 1.0), 0.0)
        right_ground = jnp.where(on_left, right_ground, ng + share * ground)
        right_source = jnp.where(on_left, right_source, ns + share * source)
    c, ng, fg, ns, fs = (own[place] for place in range(5))
    ground, source = fg + right_ground, fs + right_source
    total = c + ground
    inverse = jnp.where(total > 0.0, 1.0 / jnp.where(total > 0.0, total, 1.0), 0.0)
    share = c * inverse
    first = (left_source + ns + share * source) / (left_ground + ng + share * ground)
    after = share * first + source * inverse
    middle = mid[0] * first + mid[1] * after + mid[2]
    half = PLANES // 2
    third = 1.0 / 3.0
    for start, near_value, far_value in ((0, first, middle), (half, middle, after)):
        value = far_value
        for plane in range(start + half - 1, start, -1):
            span = slice(plane * ROWS, (plane + 1) * ROWS)
            value = factor[span, :] * value + (back[span, :] * near_value + rest[span, :])
            out[span, :] = (others[span, :] + value) * third
        span = slice(start * ROWS, (start + 1) * ROWS)
        out[span, :] = (others[span, :] + near_value) * third


def finish_row_kernel(ends, factor, back, rest, solved_x, out):
    def put(row, value):
        place = pl.ds(row, PLANES, stride=ROWS)
        out[place, :] = solved_x[place, :] + value

    def end(place):
        return ends[pl.ds(place, PLANES, stride=RETURN), :]

    for place, row in ((0, 0), (1, 1), (2, ROWS - 2), (3, ROWS - 1)):
        put(row, end(place))
    first = end(1)
    value = end(2)
    for row in range(ROWS - 3, 1, -1):
        value = factor[row] * value + (back[row] * first + rest[row])
        put(row, value)


def call(kernel, outs, scratch=(), flops=1000000, moved=500000, **options):
    return pl.pallas_call(
        kernel,
        out_shape=outs,
        scratch_shapes=scratch,
        compiler_params=pltpu.CompilerParams(vmem_limit_bytes=16 * 1024 * 1024),
        cost_estimate=pl.CostEstimate(flops=flops, bytes_accessed=moved, transcendentals=0),
        **options,
    )


def shaped(*shape):
    return jax.ShapeDtypeStruct(shape, F32)


def swap_perm(axis, bit):
    return [(i, i ^ bit) for i in range(lax.axis_size(axis))]


def next_perm(axis):
    pairs = []
    for i in range(1, lax.axis_size(axis) - 1, 2):
        pairs += [(i, i + 1), (i + 1, i)]
    return pairs


def shards(volume):
    flat = volume.reshape(PLANES * ROWS, COLS)
    lines = shaped(ROWS, PLANES, COLS)
    whole = shaped(PLANES * ROWS, COLS)
    tall = shaped((PLANES + 1) * ROWS, COLS)
    port = shaped(5, ROWS, COLS)
    to_near, to_far = call(
        edge_kernel,
        (shaped(2 * ROWS, COLS), shaped(2 * ROWS, COLS)),
        (pltpu.SemaphoreType.DMA((2,)),),
        in_specs=[pl.BlockSpec(memory_space=pl.ANY)],
    )(flat)
    far_side = lax.ppermute(to_far, "depth", next_perm("depth"))
    near_side = lax.ppermute(to_near, "depth", swap_perm("depth", 1))
    deep = call(deep_kernel, tall, (pltpu.VMEM((PLANES + 3, ROWS, COLS), F32),))(flat, near_side, far_side)
    y_port, y_factor, y_back, y_rest = call(row_kernel, (shaped(PLANES * PORT, COLS), lines, lines, lines))(
        flat, deep
    )
    ports = lax.all_to_all(y_port, "lat", 0, 0, tiled=True)
    ends = call(row_reduced_kernel, shaped(BLOCKS * RETURN, COLS))(ports)
    ends = lax.all_to_all(ends, "lat", 0, 0, tiled=True)
    z_port, z_factor, z_back, z_rest, z_mid, smooth = call(
        plane_kernel, (port, whole, whole, whole, shaped(3, ROWS, COLS), tall)
    )(flat, deep, ends)
    near = lax.ppermute(z_port, "depth", swap_perm("depth", 1))
    solved_x = call(
        column_kernel,
        whole,
        (
            pltpu.VMEM((512, COLS), F32),
            pltpu.VMEM((512, COLS), F32),
            pltpu.VMEM((16, 32, COLS), F32),
            pltpu.VMEM((16, 32, COLS), F32),
            pltpu.VMEM((16, 32, COLS), F32),
        ),
    )(flat, smooth)
    pair_own = call(lambda *refs: join_kernel(1, *refs), port)(z_port, near)
    across, skew, pair = (lax.ppermute(pair_own, "depth", swap_perm("depth", bits)) for bits in (4, 6, 2))
    others = call(finish_row_kernel, whole)(ends, y_factor, y_back, y_rest, solved_x)
    out = call(finish_plane_kernel, whole)(
        z_port, near, pair, across, skew, z_factor, z_back, z_rest, z_mid, others
    )
    return out.reshape(PLANES, ROWS, COLS)


def solution(mesh):
    placed = (P("depth", "lat", None),)
    return jax.shard_map(
        shards, mesh=mesh, in_specs=placed, out_specs=P("depth", "lat", None), check_vma=False
    )
```

```python
import jax
import jax.numpy as jnp
from jax import lax
from jax.experimental import pallas as pl
from jax.experimental.pallas import tpu as pltpu
from jax.sharding import PartitionSpec as P

TAU3 = 900.0
INV_LAMBDA_SQ = 4.0
PLANES = 32
ROWS = 16
COLS = 128
BLOCKS = 32
PORT = 16
LONG = 100_000_000_000
F32 = jnp.float32


def resistance(diff):
    return (1.0 + INV_LAMBDA_SQ * (diff * diff)) * (1.0 / TAU3)


def smooth_lanes(field, first, last):
    before = jnp.where(first, 0.0, pltpu.roll(field, 1, field.ndim - 1))
    after = jnp.where(last, 0.0, pltpu.roll(field, COLS - 1, field.ndim - 1))
    return 0.25 * (before + 2.0 * field + after)


def eliminate(coupling, ground, source, near_ground, near_source, resist):
    factor = 1.0 / (1.0 + (coupling + ground) * resist)
    weight = factor * resist
    back = coupling * weight
    near_ground = near_ground + back * ground
    near_source = near_source + back * source
    saved = (factor, back, source * weight)
    return coupling * factor, ground * factor, source * factor, near_ground, near_source, saved


def eliminate_last(coupling, ground, source, near_ground, near_source, conduct):
    inverse = 1.0 / (coupling + ground + conduct)
    factor = conduct * inverse
    back = coupling * inverse
    near_ground = near_ground + back * ground
    near_source = near_source + back * source
    saved = (factor, back, source * inverse)
    return coupling * factor, ground * factor, source * factor, near_ground, near_source, saved


def join(left, right):
    lc, lg, lh, ls, lt = left
    rc, rg, rh, rs, rt = right
    ground = lh + rg
    source = lt + rs
    inverse = 1.0 / (lc + rc + ground)
    to_left = lc * inverse
    to_right = rc * inverse
    return (
        lc * to_right,
        lg + to_left * ground,
        rh + to_right * ground,
        ls + to_left * source,
        rt + to_right * source,
    ), (to_left, to_right, source * inverse)


def edge_kernel(vol, near_side, far_side, sems):
    odd = lax.axis_index("depth") & 1
    high = (PLANES - 2) * ROWS
    near_start = pl.multiple_of((1 - odd) * high, ROWS)
    far_start = pl.multiple_of(odd * high, ROWS)
    copies = (
        pltpu.make_async_copy(vol.at[pl.ds(near_start, 2 * ROWS), :], near_side, sems.at[0]),
        pltpu.make_async_copy(vol.at[pl.ds(far_start, 2 * ROWS), :], far_side, sems.at[1]),
    )
    for copy in copies:
        copy.start()
    for copy in copies:
        copy.wait()


def strided(ref, row):
    return ref[pl.ds(row, 32, stride=16), :]


def cells(ref, plane):
    return ref[plane * ROWS : (plane + 1) * ROWS, :]


def deep_kernel(vol, near_side, far_side, deep, pair_row, next_row, mixed):
    odd = (lax.axis_index("depth") & 1) == 1
    lane = lax.broadcasted_iota(jnp.int32, (ROWS, COLS), 1)
    first, last = lane == 0, lane == COLS - 1
    mixed[0] = smooth_lanes(jnp.where(odd, cells(near_side, 1), cells(far_side, 1)), first, last)
    for plane in range(PLANES):
        mixed[plane + 1] = smooth_lanes(cells(vol, plane), first, last)
    for plane in range(2):
        mixed[PLANES + 1 + plane] = smooth_lanes(
            jnp.where(odd, cells(far_side, plane), cells(near_side, plane)), first, last
        )
    for plane in range(PLANES + 1):
        deep[plane * ROWS : (plane + 1) * ROWS, :] = 0.25 * (
            mixed[plane] + 2.0 * mixed[plane + 1] + mixed[plane + 2]
        )
    odd_row = (lax.axis_index("lat") & 1) == 1
    low = deep[pl.ds(0, PLANES + 1, stride=ROWS), :]
    high = deep[pl.ds(ROWS - 1, PLANES + 1, stride=ROWS), :]
    pair_row[...] = jnp.where(odd_row, low, high)
    next_row[...] = jnp.where(odd_row, high, low)


def plane_kernel(vol, deep, pair_row, next_row, port, factor, back, rest, mid, smooth):
    odd_row = (lax.axis_index("lat") & 1) == 1
    low_row = jnp.where(odd_row, pair_row[...], next_row[...])
    high_row = jnp.where(odd_row, next_row[...], pair_row[...])
    depth_last = lax.axis_index("depth") == lax.axis_size("depth") - 1
    z_open = jnp.where(depth_last, 0.0, TAU3).astype(F32)
    row_index = lax.broadcasted_iota(jnp.int32, (ROWS, COLS), 0)
    top, bottom = row_index == 0, row_index == ROWS - 1
    for plane in range(PLANES + 1):
        span = slice(plane * ROWS, (plane + 1) * ROWS)
        here = deep[span, :]
        above = jnp.where(top, low_row[plane : plane + 1, :], pltpu.roll(here, 1, 0))
        below = jnp.where(bottom, high_row[plane : plane + 1, :], pltpu.roll(here, ROWS - 1, 0))
        smooth[span, :] = 0.25 * (above + 2.0 * here + below)

    def resist(plane):
        return resistance(cells(smooth, plane + 1) - cells(smooth, plane))

    half = PLANES // 2
    one = jnp.ones((ROWS, COLS), F32)
    states = [
        (1.0 / resist(start), one, cells(vol, start + 1), one, cells(vol, start)) for start in (0, half)
    ]
    for step in range(1, half):
        final = step == half - 1
        for part in range(2):
            plane = part * half + step
            span = slice(plane * ROWS, (plane + 1) * ROWS)
            if final and part == 1:
                *state, saved = eliminate_last(*states[part], z_open / (TAU3 * resist(plane)))
            else:
                *state, saved = eliminate(*states[part], resist(plane))
            if not final:
                state[1] = state[1] + 1.0
                state[2] = state[2] + cells(vol, plane + 1)
            states[part] = state
            factor[span, :], back[span, :], rest[span, :] = saved
    joined, middle = join(*[(c, ng, fg, ns, fs) for c, fg, fs, ng, ns in states])
    for place, value in enumerate(joined):
        port[place] = value
    for place, value in enumerate(middle):
        mid[place] = value


def row_kernel(vol, deep, port, factor, back, rest):
    part = [strided(deep, row) for row in range(ROWS)]
    low_sum = 2.0 * part[0] + part[1]
    high_sum = part[ROWS - 2] + 2.0 * part[ROWS - 1]
    smooth = [None] + [0.25 * (part[r - 1] + 2.0 * part[r] + part[r + 1]) for r in range(1, ROWS - 1)]
    one = jnp.ones((PLANES, COLS), F32)
    state = (1.0 / resistance(smooth[2] - smooth[1]), one, strided(vol, 2), one, strided(vol, 1))
    for row in range(2, ROWS - 2):
        *state, saved = eliminate(*state, resistance(smooth[row + 1] - smooth[row]))
        state[1] = state[1] + 1.0
        state[2] = state[2] + strided(vol, row + 1)
        factor[row], back[row], rest[row] = saved
    coupling, far_ground, far_source, near_ground, near_source = state
    values = (
        coupling, near_ground, far_ground, near_source, far_source,
        part[0], part[ROWS - 1], low_sum, high_sum, smooth[1], smooth[ROWS - 2],
        strided(vol, 0), strided(vol, ROWS - 1),
    )
    for place, value in enumerate(values):
        port[pl.ds(place, PLANES, stride=PORT), :] = value
    for place in range(len(values), PORT):
        port[pl.ds(place, PLANES, stride=PORT), :] = jnp.zeros((PLANES, COLS), F32)


def chain_solve(coupling, near_ground, far_ground, near_source, far_source, count):
    size = coupling.shape[0]
    right = coupling
    ground = near_ground + pltpu.roll(far_ground, 1, 0)
    source = near_source + pltpu.roll(far_source, 1, 0)
    step = 1
    while step < count:
        left = pltpu.roll(right, step, 0)
        inverse = 1.0 / (ground + left + right)
        ground_part = ground * inverse
        source_part = source * inverse
        ground = (
            ground
            + left * pltpu.roll(ground_part, step, 0)
            + right * pltpu.roll(ground_part, size - step, 0)
        )
        source = (
            source
            + left * pltpu.roll(source_part, step, 0)
            + right * pltpu.roll(source_part, size - step, 0)
        )
        right = right * pltpu.roll(right * inverse, size - step, 0)
        step *= 2
    return source / ground


def column_kernel(vol, smooth, solved_x, turned, turned_smooth, factor, back, rest):
    for group in range(4):
        span = slice(group * COLS, (group + 1) * COLS)
        turned[span, :] = vol[span, :].T
        turned_smooth[span, :] = smooth[span, :].T

    def resist(step):
        if step < 15:
            return resistance(strided(turned_smooth, step + 1) - strided(turned_smooth, step))
        return resistance(pltpu.roll(strided(turned_smooth, 0), 31, 0) - strided(turned_smooth, 15))

    chunk_last = (lax.broadcasted_iota(jnp.int32, (32, COLS), 0) & 7) == 7
    one = jnp.ones((32, COLS), F32)
    state = (1.0 / resist(0), one, strided(turned, 1), one, strided(turned, 0))
    for step in range(1, 16):
        if step == 15:
            *state, saved = eliminate_last(*state, jnp.where(chunk_last, 0.0, 1.0 / resist(step)))
        else:
            *state, saved = eliminate(*state, resist(step))
            state[1] = state[1] + 1.0
            state[2] = state[2] + strided(turned, step + 1)
        factor[step], back[step], rest[step] = saved
    coupling, far_ground, far_source, near_ground, near_source = state
    first = chain_solve(coupling, near_ground, far_ground, near_source, far_source, 8)
    turned[pl.ds(0, 32, stride=16), :] = first
    value = pltpu.roll(first, 31, 0)
    for step in range(15, 0, -1):
        value = factor[step] * value + (back[step] * first + rest[step])
        turned[pl.ds(step, 32, stride=16), :] = value
    for group in range(4):
        span = slice(group * COLS, (group + 1) * COLS)
        solved_x[span, :] = turned[span, :].T


def row_reduced_kernel(ports, out):
    (
        coupling, near_ground, far_ground, near_source, far_source,
        low, high, low_sum, high_sum, low_smooth, high_smooth, low_cell, high_cell,
    ) = (ports[pl.ds(place, BLOCKS, stride=PORT), :] for place in range(13))
    block = lax.broadcasted_iota(jnp.int32, (BLOCKS, COLS), 0)
    block_first, block_last = block == 0, block == BLOCKS - 1
    low_end = 0.25 * (jnp.where(block_first, 0.0, pltpu.roll(high, 1, 0)) + low_sum)
    high_end = 0.25 * (high_sum + jnp.where(block_last, 0.0, pltpu.roll(low, BLOCKS - 1, 0)))
    enter = 1.0 / resistance(low_smooth - low_end)
    leave = 1.0 / resistance(high_end - high_smooth)
    across = pltpu.roll(low_end, BLOCKS - 1, 0) - high_end
    across = jnp.where(block_last, 0.0, 1.0 / resistance(across))
    zero = jnp.zeros_like(coupling)
    one = jnp.ones_like(coupling)
    before, at_low = join(
        (enter, one, zero, low_cell, zero), (coupling, near_ground, far_ground, near_source, far_source)
    )
    after, at_high = join((leave, zero, one, zero, high_cell), (across, zero, zero, zero, zero))
    whole, between = join(before, after)
    first = chain_solve(*whole, BLOCKS)
    later = pltpu.roll(first, BLOCKS - 1, 0)

    def middle(weights, left, right):
        return weights[0] * left + weights[1] * right + weights[2]

    inner_high = middle(between, first, later)
    out[:, 0, :] = first
    out[:, 1, :] = middle(at_low, first, inner_high)
    out[:, 2, :] = inner_high
    out[:, 3, :] = middle(at_high, inner_high, later)


def pick(flag, there, here):
    return tuple(jnp.where(flag, a, b) for a, b in zip(there, here))


def join_kernel(bit, own, other, out):
    upper = (lax.axis_index("depth") & bit) != 0
    mine = tuple(own[place] for place in range(5))
    theirs = tuple(other[place] for place in range(5))
    port, _ = join(pick(upper, theirs, mine), pick(upper, mine, theirs))
    for place, value in enumerate(port):
        out[place] = value


def finish_plane_kernel(
    own, near, pair, quad, factor, back, rest, mid, solved_x, out,
):
    index = lax.axis_index("depth")
    zero = jnp.zeros((ROWS, COLS), F32)
    left_ground, left_source, right_ground, right_source = zero, zero, zero, zero
    for bit, ref in ((4, quad), (2, pair), (1, near)):
        on_left = (index & bit) != 0
        c, ng, fg, ns, fs = (ref[place] for place in range(5))
        ground, source = ng + left_ground, ns + left_source
        share = c / (c + ground)
        left_ground = jnp.where(on_left, fg + share * ground, left_ground)
        left_source = jnp.where(on_left, fs + share * source, left_source)
        ground, source = fg + right_ground, fs + right_source
        total = c + ground
        share = jnp.where(total > 0.0, c / jnp.where(total > 0.0, total, 1.0), 0.0)
        right_ground = jnp.where(on_left, right_ground, ng + share * ground)
        right_source = jnp.where(on_left, right_source, ns + share * source)
    c, ng, fg, ns, fs = (own[place] for place in range(5))
    ground, source = fg + right_ground, fs + right_source
    total = c + ground
    inverse = jnp.where(total > 0.0, 1.0 / jnp.where(total > 0.0, total, 1.0), 0.0)
    share = c * inverse
    first = (left_source + ns + share * source) / (left_ground + ng + share * ground)
    after = share * first + source * inverse
    middle = mid[0] * first + mid[1] * after + mid[2]
    half = PLANES // 2
    for start, near_value, far_value in ((0, first, middle), (half, middle, after)):
        value = far_value
        for plane in range(start + half - 1, start, -1):
            span = slice(plane * ROWS, (plane + 1) * ROWS)
            value = factor[span, :] * value + (back[span, :] * near_value + rest[span, :])
            out[span, :] = solved_x[span, :] + value
        span = slice(start * ROWS, (start + 1) * ROWS)
        out[span, :] = solved_x[span, :] + near_value


def finish_row_kernel(ends, factor, back, rest, others, out):
    third = 1.0 / 3.0

    def put(row, value):
        place = pl.ds(row, PLANES, stride=ROWS)
        out[place, :] = (others[place, :] + value) * third

    for place, row in ((0, 0), (1, 1), (2, ROWS - 2), (3, ROWS - 1)):
        put(row, ends[:, place, :])
    first = ends[:, 1, :]
    value = ends[:, 2, :]
    for row in range(ROWS - 3, 1, -1):
        value = factor[row] * value + (back[row] * first + rest[row])
        put(row, value)


def call(kernel, outs, scratch=(), flops=1000000, moved=500000, **options):
    return pl.pallas_call(
        kernel,
        out_shape=outs,
        scratch_shapes=scratch,
        compiler_params=pltpu.CompilerParams(vmem_limit_bytes=16 * 1024 * 1024),
        cost_estimate=pl.CostEstimate(flops=flops, bytes_accessed=moved, transcendentals=0),
        **options,
    )


def shaped(*shape):
    return jax.ShapeDtypeStruct(shape, F32)


def line_perm(axis, step):
    count = lax.axis_size(axis)
    if step > 0:
        return [(i, i + 1) for i in range(count - 1)]
    return [(i + 1, i) for i in range(count - 1)]


def swap_perm(axis, bit):
    return [(i, i ^ bit) for i in range(lax.axis_size(axis))]


def next_perm(axis):
    pairs = []
    for i in range(1, lax.axis_size(axis) - 1, 2):
        pairs += [(i, i + 1), (i + 1, i)]
    return pairs


def shards(volume):
    flat = volume.reshape(PLANES * ROWS, COLS)
    lines = shaped(ROWS, PLANES, COLS)
    whole = shaped(PLANES * ROWS, COLS)
    tall = shaped((PLANES + 1) * ROWS, COLS)
    port = shaped(5, ROWS, COLS)
    side = shaped(PLANES + 1, COLS)
    to_near, to_far = call(
        edge_kernel,
        (shaped(2 * ROWS, COLS), shaped(2 * ROWS, COLS)),
        (pltpu.SemaphoreType.DMA((2,)),),
        in_specs=[pl.BlockSpec(memory_space=pl.ANY)],
    )(flat)
    far_side = lax.ppermute(to_far, "depth", next_perm("depth"))
    near_side = lax.ppermute(to_near, "depth", swap_perm("depth", 1))
    deep, to_pair, to_next = call(
        deep_kernel, (tall, side, side), (pltpu.VMEM((PLANES + 3, ROWS, COLS), F32),)
    )(flat, near_side, far_side)
    next_row = lax.ppermute(to_next, "lat", next_perm("lat"))
    pair_row = lax.ppermute(to_pair, "lat", swap_perm("lat", 1))
    y_port, y_factor, y_back, y_rest = call(row_kernel, (shaped(PLANES * PORT, COLS), lines, lines, lines))(
        flat, deep
    )
    ports = lax.all_to_all(y_port, "lat", 0, 0, tiled=True)
    z_port, z_factor, z_back, z_rest, z_mid, smooth = call(
        plane_kernel, (port, whole, whole, whole, shaped(3, ROWS, COLS), tall), moved=500000,flops=LONG
    )(flat, deep, pair_row, next_row)
    near = lax.ppermute(z_port, "depth", swap_perm("depth", 1))
    solved_x = call(
        column_kernel,
        whole,
        (
            pltpu.VMEM((512, COLS), F32),
            pltpu.VMEM((512, COLS), F32),
            pltpu.VMEM((16, 32, COLS), F32),
            pltpu.VMEM((16, 32, COLS), F32),
            pltpu.VMEM((16, 32, COLS), F32),
        ),
    )(flat, smooth)
    pair_own = call(lambda *refs: join_kernel(1, *refs), port)(z_port, near)
    pair = lax.ppermute(pair_own, "depth", swap_perm("depth", 2))
    quad_own = call(lambda *refs: join_kernel(2, *refs), port)(pair_own, pair)
    ports, quad_own, solved_x = lax.optimization_barrier((ports, quad_own, solved_x))
    ends = call(row_reduced_kernel, shaped(BLOCKS, 4, COLS))(ports)
    ends, quad_own = lax.optimization_barrier((ends, quad_own))
    quad = lax.ppermute(quad_own, "depth", swap_perm("depth", 4))
    others = call(finish_plane_kernel, whole)(
        z_port, near, pair, quad, z_factor, z_back, z_rest, z_mid, solved_x
    )
    ends_y = lax.all_to_all(ends, "lat", 0, 0, tiled=True)
    out = call(finish_row_kernel, whole)(ends_y, y_factor, y_back, y_rest, others)
    return out.reshape(PLANES, ROWS, COLS)


def solution(mesh):
    placed = (P("depth", "lat", None),)
    return jax.shard_map(
        shards, mesh=mesh, in_specs=placed, out_specs=P("depth", "lat", None), check_vma=False
    )
```

```python
import jax
import jax.numpy as jnp
from jax import lax
from jax.experimental import pallas as pl
from jax.experimental.pallas import tpu as pltpu
from jax.sharding import PartitionSpec as P

TAU3 = 900.0
INV_LAMBDA_SQ = 4.0
PLANES = 32
ROWS = 16
COLS = 128
BLOCKS = 32
PORT = 16
LONG = 100_000_000_000
F32 = jnp.float32


def resistance(diff):
    return (1.0 + INV_LAMBDA_SQ * (diff * diff)) * (1.0 / TAU3)


def smooth_lanes(field, first, last):
    before = jnp.where(first, 0.0, pltpu.roll(field, 1, field.ndim - 1))
    after = jnp.where(last, 0.0, pltpu.roll(field, COLS - 1, field.ndim - 1))
    return 0.25 * (before + 2.0 * field + after)


def eliminate(coupling, ground, source, near_ground, near_source, resist):
    factor = 1.0 / (1.0 + (coupling + ground) * resist)
    weight = factor * resist
    back = coupling * weight
    near_ground = near_ground + back * ground
    near_source = near_source + back * source
    saved = (factor, back, source * weight)
    return coupling * factor, ground * factor, source * factor, near_ground, near_source, saved


def eliminate_last(coupling, ground, source, near_ground, near_source, conduct):
    inverse = 1.0 / (coupling + ground + conduct)
    factor = conduct * inverse
    back = coupling * inverse
    near_ground = near_ground + back * ground
    near_source = near_source + back * source
    saved = (factor, back, source * inverse)
    return coupling * factor, ground * factor, source * factor, near_ground, near_source, saved


def join(left, right):
    lc, lg, lh, ls, lt = left
    rc, rg, rh, rs, rt = right
    ground = lh + rg
    source = lt + rs
    inverse = 1.0 / (lc + rc + ground)
    to_left = lc * inverse
    to_right = rc * inverse
    return (
        lc * to_right,
        lg + to_left * ground,
        rh + to_right * ground,
        ls + to_left * source,
        rt + to_right * source,
    ), (to_left, to_right, source * inverse)


def edge_kernel(vol, near_side, far_side, sems):
    odd = lax.axis_index("depth") & 1
    high = (PLANES - 2) * ROWS
    near_start = pl.multiple_of((1 - odd) * high, ROWS)
    far_start = pl.multiple_of(odd * high, ROWS)
    copies = (
        pltpu.make_async_copy(vol.at[pl.ds(near_start, 2 * ROWS), :], near_side, sems.at[0]),
        pltpu.make_async_copy(vol.at[pl.ds(far_start, 2 * ROWS), :], far_side, sems.at[1]),
    )
    for copy in copies:
        copy.start()
    for copy in copies:
        copy.wait()


def strided(ref, row):
    return ref[pl.ds(row, 32, stride=16), :]


def cells(ref, plane):
    return ref[plane * ROWS : (plane + 1) * ROWS, :]


def deep_kernel(vol, near_side, far_side, deep, pair_row, next_row, mixed):
    odd = (lax.axis_index("depth") & 1) == 1
    lane = lax.broadcasted_iota(jnp.int32, (ROWS, COLS), 1)
    first, last = lane == 0, lane == COLS - 1
    mixed[0] = smooth_lanes(jnp.where(odd, cells(near_side, 1), cells(far_side, 1)), first, last)
    for plane in range(PLANES):
        mixed[plane + 1] = smooth_lanes(cells(vol, plane), first, last)
    for plane in range(2):
        mixed[PLANES + 1 + plane] = smooth_lanes(
            jnp.where(odd, cells(far_side, plane), cells(near_side, plane)), first, last
        )
    for plane in range(PLANES + 1):
        deep[plane * ROWS : (plane + 1) * ROWS, :] = 0.25 * (
            mixed[plane] + 2.0 * mixed[plane + 1] + mixed[plane + 2]
        )
    odd_row = (lax.axis_index("lat") & 1) == 1
    low = deep[pl.ds(0, PLANES + 1, stride=ROWS), :]
    high = deep[pl.ds(ROWS - 1, PLANES + 1, stride=ROWS), :]
    pair_row[...] = jnp.where(odd_row, low, high)
    next_row[...] = jnp.where(odd_row, high, low)


def first_smooth_kernel(deep, next_row, smooth):
    odd_row = (lax.axis_index("lat") & 1) == 1
    side = next_row[...]
    low_row = jnp.where(odd_row, 0.0, side)
    high_row = jnp.where(odd_row, side, 0.0)
    row_index = lax.broadcasted_iota(jnp.int32, (ROWS, COLS), 0)
    top, bottom = row_index == 0, row_index == ROWS - 1
    for plane in range(PLANES + 1):
        span = slice(plane * ROWS, (plane + 1) * ROWS)
        here = deep[span, :]
        above = jnp.where(top, low_row[plane : plane + 1, :], pltpu.roll(here, 1, 0))
        below = jnp.where(bottom, high_row[plane : plane + 1, :], pltpu.roll(here, ROWS - 1, 0))
        smooth[span, :] = 0.25 * (above + 2.0 * here + below)


def plane_kernel(vol, first_smooth, pair_row, port, factor, back, rest, mid, smooth):
    odd_row = (lax.axis_index("lat") & 1) == 1
    depth_last = lax.axis_index("depth") == lax.axis_size("depth") - 1
    z_open = jnp.where(depth_last, 0.0, TAU3).astype(F32)
    side = 0.25 * pair_row[...]
    low_row = jnp.where(odd_row, side, 0.0)
    high_row = jnp.where(odd_row, 0.0, side)
    smooth[...] = first_smooth[...]
    low_place = pl.ds(0, PLANES + 1, stride=ROWS)
    high_place = pl.ds(ROWS - 1, PLANES + 1, stride=ROWS)
    smooth[low_place, :] = smooth[low_place, :] + low_row
    smooth[high_place, :] = smooth[high_place, :] + high_row

    def resist(plane):
        return resistance(cells(smooth, plane + 1) - cells(smooth, plane))

    half = PLANES // 2
    one = jnp.ones((ROWS, COLS), F32)
    states = [
        (1.0 / resist(start), one, cells(vol, start + 1), one, cells(vol, start)) for start in (0, half)
    ]
    for step in range(1, half):
        final = step == half - 1
        for part in range(2):
            plane = part * half + step
            span = slice(plane * ROWS, (plane + 1) * ROWS)
            if final and part == 1:
                *state, saved = eliminate_last(*states[part], z_open / (TAU3 * resist(plane)))
            else:
                *state, saved = eliminate(*states[part], resist(plane))
            if not final:
                state[1] = state[1] + 1.0
                state[2] = state[2] + cells(vol, plane + 1)
            states[part] = state
            factor[span, :], back[span, :], rest[span, :] = saved
    joined, middle = join(*[(c, ng, fg, ns, fs) for c, fg, fs, ng, ns in states])
    for place, value in enumerate(joined):
        port[place] = value
    for place, value in enumerate(middle):
        mid[place] = value


def row_kernel(vol, deep, port, factor, back, rest):
    part = [strided(deep, row) for row in range(ROWS)]
    low_sum = 2.0 * part[0] + part[1]
    high_sum = part[ROWS - 2] + 2.0 * part[ROWS - 1]
    smooth = [None] + [0.25 * (part[r - 1] + 2.0 * part[r] + part[r + 1]) for r in range(1, ROWS - 1)]
    one = jnp.ones((PLANES, COLS), F32)
    state = (1.0 / resistance(smooth[2] - smooth[1]), one, strided(vol, 2), one, strided(vol, 1))
    for row in range(2, ROWS - 2):
        *state, saved = eliminate(*state, resistance(smooth[row + 1] - smooth[row]))
        state[1] = state[1] + 1.0
        state[2] = state[2] + strided(vol, row + 1)
        factor[row], back[row], rest[row] = saved
    coupling, far_ground, far_source, near_ground, near_source = state
    values = (
        coupling, near_ground, far_ground, near_source, far_source,
        part[0], part[ROWS - 1], low_sum, high_sum, smooth[1], smooth[ROWS - 2],
        strided(vol, 0), strided(vol, ROWS - 1),
    )
    for place, value in enumerate(values):
        port[pl.ds(place, PLANES, stride=PORT), :] = value
    for place in range(len(values), PORT):
        port[pl.ds(place, PLANES, stride=PORT), :] = jnp.zeros((PLANES, COLS), F32)


def chain_solve(coupling, near_ground, far_ground, near_source, far_source, count):
    size = coupling.shape[0]
    right = coupling
    ground = near_ground + pltpu.roll(far_ground, 1, 0)
    source = near_source + pltpu.roll(far_source, 1, 0)
    step = 1
    while step < count:
        left = pltpu.roll(right, step, 0)
        inverse = 1.0 / (ground + left + right)
        ground_part = ground * inverse
        source_part = source * inverse
        ground = (
            ground
            + left * pltpu.roll(ground_part, step, 0)
            + right * pltpu.roll(ground_part, size - step, 0)
        )
        source = (
            source
            + left * pltpu.roll(source_part, step, 0)
            + right * pltpu.roll(source_part, size - step, 0)
        )
        right = right * pltpu.roll(right * inverse, size - step, 0)
        step *= 2
    return source / ground


def column_kernel(vol, smooth, solved_x, turned, turned_smooth, factor, back, rest):
    for group in range(4):
        span = slice(group * COLS, (group + 1) * COLS)
        turned[span, :] = vol[span, :].T
        turned_smooth[span, :] = smooth[span, :].T

    def resist(step):
        if step < 15:
            return resistance(strided(turned_smooth, step + 1) - strided(turned_smooth, step))
        return resistance(pltpu.roll(strided(turned_smooth, 0), 31, 0) - strided(turned_smooth, 15))

    chunk_last = (lax.broadcasted_iota(jnp.int32, (32, COLS), 0) & 7) == 7
    one = jnp.ones((32, COLS), F32)
    state = (1.0 / resist(0), one, strided(turned, 1), one, strided(turned, 0))
    for step in range(1, 16):
        if step == 15:
            *state, saved = eliminate_last(*state, jnp.where(chunk_last, 0.0, 1.0 / resist(step)))
        else:
            *state, saved = eliminate(*state, resist(step))
            state[1] = state[1] + 1.0
            state[2] = state[2] + strided(turned, step + 1)
        factor[step], back[step], rest[step] = saved
    coupling, far_ground, far_source, near_ground, near_source = state
    first = chain_solve(coupling, near_ground, far_ground, near_source, far_source, 8)
    turned[pl.ds(0, 32, stride=16), :] = first
    value = pltpu.roll(first, 31, 0)
    for step in range(15, 0, -1):
        value = factor[step] * value + (back[step] * first + rest[step])
        turned[pl.ds(step, 32, stride=16), :] = value
    for group in range(4):
        span = slice(group * COLS, (group + 1) * COLS)
        solved_x[span, :] = turned[span, :].T


def row_reduced_kernel(ports, out):
    (
        coupling, near_ground, far_ground, near_source, far_source,
        low, high, low_sum, high_sum, low_smooth, high_smooth, low_cell, high_cell,
    ) = (ports[pl.ds(place, BLOCKS, stride=PORT), :] for place in range(13))
    block = lax.broadcasted_iota(jnp.int32, (BLOCKS, COLS), 0)
    block_first, block_last = block == 0, block == BLOCKS - 1
    low_end = 0.25 * (jnp.where(block_first, 0.0, pltpu.roll(high, 1, 0)) + low_sum)
    high_end = 0.25 * (high_sum + jnp.where(block_last, 0.0, pltpu.roll(low, BLOCKS - 1, 0)))
    enter = 1.0 / resistance(low_smooth - low_end)
    leave = 1.0 / resistance(high_end - high_smooth)
    across = pltpu.roll(low_end, BLOCKS - 1, 0) - high_end
    across = jnp.where(block_last, 0.0, 1.0 / resistance(across))
    zero = jnp.zeros_like(coupling)
    one = jnp.ones_like(coupling)
    before, at_low = join(
        (enter, one, zero, low_cell, zero), (coupling, near_ground, far_ground, near_source, far_source)
    )
    after, at_high = join((leave, zero, one, zero, high_cell), (across, zero, zero, zero, zero))
    whole, between = join(before, after)
    first = chain_solve(*whole, BLOCKS)
    later = pltpu.roll(first, BLOCKS - 1, 0)

    def middle(weights, left, right):
        return weights[0] * left + weights[1] * right + weights[2]

    inner_high = middle(between, first, later)
    out[:, 0, :] = first
    out[:, 1, :] = middle(at_low, first, inner_high)
    out[:, 2, :] = inner_high
    out[:, 3, :] = middle(at_high, inner_high, later)


def pick(flag, there, here):
    return tuple(jnp.where(flag, a, b) for a, b in zip(there, here))


def join_kernel(bit, own, other, out):
    upper = (lax.axis_index("depth") & bit) != 0
    mine = tuple(own[place] for place in range(5))
    theirs = tuple(other[place] for place in range(5))
    port, _ = join(pick(upper, theirs, mine), pick(upper, mine, theirs))
    for place, value in enumerate(port):
        out[place] = value


def finish_plane_kernel(
    own, near, pair, quad, factor, back, rest, mid, solved_x, out,
):
    index = lax.axis_index("depth")
    zero = jnp.zeros((ROWS, COLS), F32)
    left_ground, left_source, right_ground, right_source = zero, zero, zero, zero
    for bit, ref in ((4, quad), (2, pair), (1, near)):
        on_left = (index & bit) != 0
        c, ng, fg, ns, fs = (ref[place] for place in range(5))
        ground, source = ng + left_ground, ns + left_source
        share = c / (c + ground)
        left_ground = jnp.where(on_left, fg + share * ground, left_ground)
        left_source = jnp.where(on_left, fs + share * source, left_source)
        ground, source = fg + right_ground, fs + right_source
        total = c + ground
        share = jnp.where(total > 0.0, c / jnp.where(total > 0.0, total, 1.0), 0.0)
        right_ground = jnp.where(on_left, right_ground, ng + share * ground)
        right_source = jnp.where(on_left, right_source, ns + share * source)
    c, ng, fg, ns, fs = (own[place] for place in range(5))
    ground, source = fg + right_ground, fs + right_source
    total = c + ground
    inverse = jnp.where(total > 0.0, 1.0 / jnp.where(total > 0.0, total, 1.0), 0.0)
    share = c * inverse
    first = (left_source + ns + share * source) / (left_ground + ng + share * ground)
    after = share * first + source * inverse
    middle = mid[0] * first + mid[1] * after + mid[2]
    half = PLANES // 2
    for start, near_value, far_value in ((0, first, middle), (half, middle, after)):
        value = far_value
        for plane in range(start + half - 1, start, -1):
            span = slice(plane * ROWS, (plane + 1) * ROWS)
            value = factor[span, :] * value + (back[span, :] * near_value + rest[span, :])
            out[span, :] = solved_x[span, :] + value
        span = slice(start * ROWS, (start + 1) * ROWS)
        out[span, :] = solved_x[span, :] + near_value


def finish_row_kernel(ends, factor, back, rest, others, out):
    third = 1.0 / 3.0

    def put(row, value):
        place = pl.ds(row, PLANES, stride=ROWS)
        out[place, :] = (others[place, :] + value) * third

    for place, row in ((0, 0), (1, 1), (2, ROWS - 2), (3, ROWS - 1)):
        put(row, ends[:, place, :])
    first = ends[:, 1, :]
    value = ends[:, 2, :]
    for row in range(ROWS - 3, 1, -1):
        value = factor[row] * value + (back[row] * first + rest[row])
        put(row, value)


def call(kernel, outs, scratch=(), flops=1000000, moved=500000, **options):
    return pl.pallas_call(
        kernel,
        out_shape=outs,
        scratch_shapes=scratch,
        compiler_params=pltpu.CompilerParams(vmem_limit_bytes=16 * 1024 * 1024),
        cost_estimate=pl.CostEstimate(flops=flops, bytes_accessed=moved, transcendentals=0),
        **options,
    )


def shaped(*shape):
    return jax.ShapeDtypeStruct(shape, F32)


def line_perm(axis, step):
    count = lax.axis_size(axis)
    if step > 0:
        return [(i, i + 1) for i in range(count - 1)]
    return [(i + 1, i) for i in range(count - 1)]


def swap_perm(axis, bit):
    return [(i, i ^ bit) for i in range(lax.axis_size(axis))]


def next_perm(axis):
    pairs = []
    for i in range(1, lax.axis_size(axis) - 1, 2):
        pairs += [(i, i + 1), (i + 1, i)]
    return pairs


def shards(volume):
    flat = volume.reshape(PLANES * ROWS, COLS)
    lines = shaped(ROWS, PLANES, COLS)
    whole = shaped(PLANES * ROWS, COLS)
    tall = shaped((PLANES + 1) * ROWS, COLS)
    port = shaped(5, ROWS, COLS)
    side = shaped(PLANES + 1, COLS)
    to_near, to_far = call(
        edge_kernel,
        (shaped(2 * ROWS, COLS), shaped(2 * ROWS, COLS)),
        (pltpu.SemaphoreType.DMA((2,)),),
        in_specs=[pl.BlockSpec(memory_space=pl.ANY)],
    )(flat)
    far_side = lax.ppermute(to_far, "depth", next_perm("depth"))
    near_side = lax.ppermute(to_near, "depth", swap_perm("depth", 1))
    deep, to_pair, to_next = call(
        deep_kernel, (tall, side, side), (pltpu.VMEM((PLANES + 3, ROWS, COLS), F32),)
    )(flat, near_side, far_side)
    next_row = lax.ppermute(to_next, "lat", next_perm("lat"))
    first_smooth = call(first_smooth_kernel, tall, flops=LONG)(deep, next_row)
    first_smooth, to_pair = lax.optimization_barrier((first_smooth, to_pair))
    pair_row = lax.ppermute(to_pair, "lat", swap_perm("lat", 1))
    y_port, y_factor, y_back, y_rest = call(row_kernel, (shaped(PLANES * PORT, COLS), lines, lines, lines))(
        flat, deep
    )
    ports = lax.all_to_all(y_port, "lat", 0, 0, tiled=True)
    z_port, z_factor, z_back, z_rest, z_mid, smooth = call(
        plane_kernel, (port, whole, whole, whole, shaped(3, ROWS, COLS), tall), moved=500000,
    )(flat, first_smooth, pair_row)
    near = lax.ppermute(z_port, "depth", swap_perm("depth", 1))
    solved_x = call(
        column_kernel,
        whole,
        (
            pltpu.VMEM((512, COLS), F32),
            pltpu.VMEM((512, COLS), F32),
            pltpu.VMEM((16, 32, COLS), F32),
            pltpu.VMEM((16, 32, COLS), F32),
            pltpu.VMEM((16, 32, COLS), F32),
        ),
    )(flat, smooth)
    pair_own = call(lambda *refs: join_kernel(1, *refs), port)(z_port, near)
    pair = lax.ppermute(pair_own, "depth", swap_perm("depth", 2))
    quad_own = call(lambda *refs: join_kernel(2, *refs), port)(pair_own, pair)
    ports, quad_own, solved_x = lax.optimization_barrier((ports, quad_own, solved_x))
    ends = call(row_reduced_kernel, shaped(BLOCKS, 4, COLS))(ports)
    ends, quad_own = lax.optimization_barrier((ends, quad_own))
    quad = lax.ppermute(quad_own, "depth", swap_perm("depth", 4))
    others = call(finish_plane_kernel, whole)(
        z_port, near, pair, quad, z_factor, z_back, z_rest, z_mid, solved_x
    )
    ends_y = lax.all_to_all(ends, "lat", 0, 0, tiled=True)
    out = call(finish_row_kernel, whole)(ends_y, y_factor, y_back, y_rest, others)
    return out.reshape(PLANES, ROWS, COLS)


def solution(mesh):
    placed = (P("depth", "lat", None),)
    return jax.shard_map(
        shards, mesh=mesh, in_specs=placed, out_specs=P("depth", "lat", None), check_vma=False
    )
```

```python
import jax
import jax.numpy as jnp
from jax import lax
from jax.experimental import pallas as pl
from jax.experimental.pallas import tpu as pltpu
from jax.sharding import PartitionSpec as P

TAU3 = 900.0
INV_LAMBDA_SQ = 4.0
PLANES = 32
ROWS = 16
COLS = 128
BLOCKS = 32
PORT = 8
FACE = 40
F32 = jnp.float32


def resistance(diff):
    return (1.0 + INV_LAMBDA_SQ * (diff * diff)) * (1.0 / TAU3)


def smooth_lanes(field, first, last):
    before = jnp.where(first, 0.0, pltpu.roll(field, 1, field.ndim - 1))
    after = jnp.where(last, 0.0, pltpu.roll(field, COLS - 1, field.ndim - 1))
    return 0.25 * (before + 2.0 * field + after)


def eliminate(coupling, ground, source, near_ground, near_source, resist):
    factor = 1.0 / (1.0 + (coupling + ground) * resist)
    weight = factor * resist
    back = coupling * weight
    near_ground = near_ground + back * ground
    near_source = near_source + back * source
    saved = (factor, back, source * weight)
    return coupling * factor, ground * factor, source * factor, near_ground, near_source, saved


def eliminate_last(coupling, ground, source, near_ground, near_source, conduct):
    inverse = 1.0 / (coupling + ground + conduct)
    factor = conduct * inverse
    back = coupling * inverse
    near_ground = near_ground + back * ground
    near_source = near_source + back * source
    saved = (factor, back, source * inverse)
    return coupling * factor, ground * factor, source * factor, near_ground, near_source, saved


def join(left, right):
    lc, lg, lh, ls, lt = left
    rc, rg, rh, rs, rt = right
    ground = lh + rg
    source = lt + rs
    inverse = 1.0 / (lc + rc + ground)
    to_left = lc * inverse
    to_right = rc * inverse
    return (
        lc * to_right,
        lg + to_left * ground,
        rh + to_right * ground,
        ls + to_left * source,
        rt + to_right * source,
    ), (to_left, to_right, source * inverse)


def side_kernel(vol, pair_row, next_row):
    odd = (lax.axis_index("lat") & 1) == 1
    low = vol[pl.ds(0, PLANES, stride=ROWS), :]
    high = vol[pl.ds(ROWS - 1, PLANES, stride=ROWS), :]
    pair_row[...] = jnp.where(odd, low, high)
    next_row[...] = jnp.where(odd, high, low)


def side_rows(pair_row, next_row):
    odd = (lax.axis_index("lat") & 1) == 1
    return jnp.where(odd, pair_row, next_row), jnp.where(odd, next_row, pair_row)


def face_kernel(vol, pair_row, next_row, near_face, far_face):
    odd = (lax.axis_index("depth") & 1) == 1
    low_row, high_row = side_rows(pair_row[...], next_row[...])
    size = 2 * ROWS
    low_planes, high_planes = vol[0:size, :], vol[(PLANES - 2) * ROWS :, :]
    near_face[0:size, :] = jnp.where(odd, low_planes, high_planes)
    far_face[0:size, :] = jnp.where(odd, high_planes, low_planes)
    for place, side in ((size, low_row), (size + 2, high_row)):
        near_face[place : place + 2, :] = jnp.where(odd, side[0:2, :], side[PLANES - 2 :, :])
        far_face[place : place + 2, :] = jnp.where(odd, side[PLANES - 2 :, :], side[0:2, :])
    near_face[size + 4 :, :] = jnp.zeros((FACE - size - 4, COLS), F32)
    far_face[size + 4 :, :] = jnp.zeros((FACE - size - 4, COLS), F32)


def strided(ref, row):
    return ref[pl.ds(row, 32, stride=16), :]


def cells(ref, plane):
    return ref[plane * ROWS : (plane + 1) * ROWS, :]


def smooth_kernel(vol, pair_row, next_row, near_face, far_face, smooth, mixed, low_side, high_side):
    odd = (lax.axis_index("depth") & 1) == 1
    size = 2 * ROWS
    near, far = near_face[...], far_face[...]
    below_face, above_face = jnp.where(odd, near, far), jnp.where(odd, far, near)
    lane = lax.broadcasted_iota(jnp.int32, (ROWS, COLS), 1)
    first, last = lane == 0, lane == COLS - 1
    mixed[0] = smooth_lanes(below_face[ROWS:size, :], first, last)
    for plane in range(PLANES):
        mixed[plane + 1] = smooth_lanes(cells(vol, plane), first, last)
    for plane in range(2):
        mixed[PLANES + 1 + plane] = smooth_lanes(above_face[plane * ROWS : (plane + 1) * ROWS, :], first, last)
    side_lane = lax.broadcasted_iota(jnp.int32, (PLANES + 3, COLS), 1)
    sides = []
    for place, ref, own in zip((size, size + 2), (low_side, high_side), side_rows(pair_row[...], next_row[...])):
        ref[0:1, :] = below_face[place + 1 : place + 2, :]
        ref[1 : PLANES + 1, :] = own
        ref[PLANES + 1 : PLANES + 3, :] = above_face[place : place + 2, :]
        ref[0 : PLANES + 3, :] = smooth_lanes(ref[0 : PLANES + 3, :], side_lane == 0, side_lane == COLS - 1)
        sides.append(
            0.25 * (ref[0 : PLANES + 1, :] + 2.0 * ref[1 : PLANES + 2, :] + ref[2 : PLANES + 3, :])
        )
    row_index = lax.broadcasted_iota(jnp.int32, (ROWS, COLS), 0)
    top, bottom = row_index == 0, row_index == ROWS - 1
    for plane in range(PLANES + 1):
        here = 0.25 * (mixed[plane] + 2.0 * mixed[plane + 1] + mixed[plane + 2])
        above = jnp.where(top, sides[0][plane : plane + 1, :], pltpu.roll(here, 1, 0))
        below = jnp.where(bottom, sides[1][plane : plane + 1, :], pltpu.roll(here, ROWS - 1, 0))
        smooth[plane * ROWS : (plane + 1) * ROWS, :] = 0.25 * (above + 2.0 * here + below)


def plane_kernel(vol, smooth, port, factor, back, rest, mid):
    depth_last = lax.axis_index("depth") == lax.axis_size("depth") - 1
    z_open = jnp.where(depth_last, 0.0, TAU3).astype(F32)

    def resist(plane):
        return resistance(cells(smooth, plane + 1) - cells(smooth, plane))

    half = PLANES // 2
    one = jnp.ones((ROWS, COLS), F32)
    states = [
        (1.0 / resist(start), one, cells(vol, start + 1), one, cells(vol, start)) for start in (0, half)
    ]
    for step in range(1, half):
        final = step == half - 1
        for part in range(2):
            plane = part * half + step
            span = slice(plane * ROWS, (plane + 1) * ROWS)
            if final and part == 1:
                *state, saved = eliminate_last(*states[part], z_open / (TAU3 * resist(plane)))
            else:
                *state, saved = eliminate(*states[part], resist(plane))
            if not final:
                state[1] = state[1] + 1.0
                state[2] = state[2] + cells(vol, plane + 1)
            states[part] = state
            factor[span, :], back[span, :], rest[span, :] = saved
    joined, middle = join(*[(c, ng, fg, ns, fs) for c, fg, fs, ng, ns in states])
    for place, value in enumerate(joined):
        port[place] = value
    for place, value in enumerate(middle):
        mid[place] = value


def row_kernel(vol, smooth, port, factor, back, rest):
    def resist(row):
        return resistance(strided(smooth, row + 1) - strided(smooth, row))

    one = jnp.ones((PLANES, COLS), F32)
    state = (1.0 / resist(0), one, strided(vol, 1), one, strided(vol, 0))
    for row in range(1, ROWS - 1):
        *state, saved = eliminate(*state, resist(row))
        state[1] = state[1] + 1.0
        state[2] = state[2] + strided(vol, row + 1)
        factor[row], back[row], rest[row] = saved
    coupling, far_ground, far_source, near_ground, near_source = state
    values = (
        coupling, near_ground, far_ground, near_source, far_source,
        strided(smooth, 0), strided(smooth, ROWS - 1), jnp.zeros((PLANES, COLS), F32),
    )
    for place, value in enumerate(values):
        port[pl.ds(place, PLANES, stride=PORT), :] = value


def chain_solve(coupling, near_ground, far_ground, near_source, far_source, count):
    size = coupling.shape[0]
    right = coupling
    ground = near_ground + pltpu.roll(far_ground, 1, 0)
    source = near_source + pltpu.roll(far_source, 1, 0)
    step = 1
    while step < count:
        left = pltpu.roll(right, step, 0)
        inverse = 1.0 / (ground + left + right)
        ground_part = ground * inverse
        source_part = source * inverse
        ground = (
            ground
            + left * pltpu.roll(ground_part, step, 0)
            + right * pltpu.roll(ground_part, size - step, 0)
        )
        source = (
            source
            + left * pltpu.roll(source_part, step, 0)
            + right * pltpu.roll(source_part, size - step, 0)
        )
        right = right * pltpu.roll(right * inverse, size - step, 0)
        step *= 2
    return source / ground


def column_kernel(vol, smooth, solved_x, turned, turned_smooth, factor, back, rest):
    for group in range(4):
        span = slice(group * COLS, (group + 1) * COLS)
        turned[span, :] = vol[span, :].T
        turned_smooth[span, :] = smooth[span, :].T

    def resist(step):
        if step < 15:
            return resistance(strided(turned_smooth, step + 1) - strided(turned_smooth, step))
        return resistance(pltpu.roll(strided(turned_smooth, 0), 31, 0) - strided(turned_smooth, 15))

    chunk_last = (lax.broadcasted_iota(jnp.int32, (32, COLS), 0) & 7) == 7
    one = jnp.ones((32, COLS), F32)
    state = (1.0 / resist(0), one, strided(turned, 1), one, strided(turned, 0))
    for step in range(1, 16):
        if step == 15:
            *state, saved = eliminate_last(*state, jnp.where(chunk_last, 0.0, 1.0 / resist(step)))
        else:
            *state, saved = eliminate(*state, resist(step))
            state[1] = state[1] + 1.0
            state[2] = state[2] + strided(turned, step + 1)
        factor[step], back[step], rest[step] = saved
    coupling, far_ground, far_source, near_ground, near_source = state
    first = chain_solve(coupling, near_ground, far_ground, near_source, far_source, 8)
    turned[pl.ds(0, 32, stride=16), :] = first
    value = pltpu.roll(first, 31, 0)
    for step in range(15, 0, -1):
        value = factor[step] * value + (back[step] * first + rest[step])
        turned[pl.ds(step, 32, stride=16), :] = value
    for group in range(4):
        span = slice(group * COLS, (group + 1) * COLS)
        solved_x[span, :] = turned[span, :].T


def row_reduced_kernel(ports, out):
    coupling, near_ground, far_ground, near_source, far_source, low, high = (
        ports[pl.ds(place, BLOCKS, stride=PORT), :] for place in range(7)
    )
    block_last = lax.broadcasted_iota(jnp.int32, (BLOCKS, COLS), 0) == BLOCKS - 1
    across = pltpu.roll(low, BLOCKS - 1, 0) - high
    across = jnp.where(block_last, 0.0, 1.0 / resistance(across))
    zero = jnp.zeros_like(coupling)
    whole, at_high = join(
        (coupling, near_ground, far_ground, near_source, far_source), (across, zero, zero, zero, zero)
    )
    first = chain_solve(*whole, BLOCKS)
    out[:, 0, :] = first
    out[:, 1, :] = at_high[0] * first + at_high[1] * pltpu.roll(first, BLOCKS - 1, 0) + at_high[2]


def pick(flag, there, here):
    return tuple(jnp.where(flag, a, b) for a, b in zip(there, here))


def join_kernel(bit, own, other, out):
    upper = (lax.axis_index("depth") & bit) != 0
    mine = tuple(own[place] for place in range(5))
    theirs = tuple(other[place] for place in range(5))
    port, _ = join(pick(upper, theirs, mine), pick(upper, mine, theirs))
    for place, value in enumerate(port):
        out[place] = value


def finish_plane_kernel(
    own, near, pair, quad, factor, back, rest, mid, solved_x, out,
):
    index = lax.axis_index("depth")
    zero = jnp.zeros((ROWS, COLS), F32)
    left_ground, left_source, right_ground, right_source = zero, zero, zero, zero
    for bit, ref in ((4, quad), (2, pair), (1, near)):
        on_left = (index & bit) != 0
        c, ng, fg, ns, fs = (ref[place] for place in range(5))
        ground, source = ng + left_ground, ns + left_source
        share = c / (c + ground)
        left_ground = jnp.where(on_left, fg + share * ground, left_ground)
        left_source = jnp.where(on_left, fs + share * source, left_source)
        ground, source = fg + right_ground, fs + right_source
        total = c + ground
        share = jnp.where(total > 0.0, c / jnp.where(total > 0.0, total, 1.0), 0.0)
        right_ground = jnp.where(on_left, right_ground, ng + share * ground)
        right_source = jnp.where(on_left, right_source, ns + share * source)
    c, ng, fg, ns, fs = (own[place] for place in range(5))
    ground, source = fg + right_ground, fs + right_source
    total = c + ground
    inverse = jnp.where(total > 0.0, 1.0 / jnp.where(total > 0.0, total, 1.0), 0.0)
    share = c * inverse
    first = (left_source + ns + share * source) / (left_ground + ng + share * ground)
    after = share * first + source * inverse
    middle = mid[0] * first + mid[1] * after + mid[2]
    half = PLANES // 2
    for start, near_value, far_value in ((0, first, middle), (half, middle, after)):
        value = far_value
        for plane in range(start + half - 1, start, -1):
            span = slice(plane * ROWS, (plane + 1) * ROWS)
            value = factor[span, :] * value + (back[span, :] * near_value + rest[span, :])
            out[span, :] = solved_x[span, :] + value
        span = slice(start * ROWS, (start + 1) * ROWS)
        out[span, :] = solved_x[span, :] + near_value


def finish_row_kernel(ends, factor, back, rest, others, out):
    third = 1.0 / 3.0

    def put(row, value):
        place = pl.ds(row, PLANES, stride=ROWS)
        out[place, :] = (others[place, :] + value) * third

    first = ends[:, 0, :]
    value = ends[:, 1, :]
    put(0, first)
    put(ROWS - 1, value)
    for row in range(ROWS - 2, 0, -1):
        value = factor[row] * value + (back[row] * first + rest[row])
        put(row, value)


def call(kernel, outs, scratch=(), flops=1000000, moved=500000, **options):
    return pl.pallas_call(
        kernel,
        out_shape=outs,
        scratch_shapes=scratch,
        compiler_params=pltpu.CompilerParams(vmem_limit_bytes=16 * 1024 * 1024),
        cost_estimate=pl.CostEstimate(flops=flops, bytes_accessed=moved, transcendentals=0),
        **options,
    )


def shaped(*shape):
    return jax.ShapeDtypeStruct(shape, F32)


def line_perm(axis, step):
    count = lax.axis_size(axis)
    if step > 0:
        return [(i, i + 1) for i in range(count - 1)]
    return [(i + 1, i) for i in range(count - 1)]


def swap_perm(axis, bit):
    return [(i, i ^ bit) for i in range(lax.axis_size(axis))]


def next_perm(axis):
    pairs = []
    for i in range(1, lax.axis_size(axis) - 1, 2):
        pairs += [(i, i + 1), (i + 1, i)]
    return pairs


def shards(volume):
    flat = volume.reshape(PLANES * ROWS, COLS)
    lines = shaped(ROWS, PLANES, COLS)
    whole = shaped(PLANES * ROWS, COLS)
    tall = shaped((PLANES + 1) * ROWS, COLS)
    port = shaped(5, ROWS, COLS)
    to_pair, to_next = call(side_kernel, (shaped(PLANES, COLS), shaped(PLANES, COLS)))(flat)
    next_row = lax.ppermute(to_next, "lat", next_perm("lat"))
    pair_row = lax.ppermute(to_pair, "lat", swap_perm("lat", 1))
    to_near, to_far = call(face_kernel, (shaped(FACE, COLS), shaped(FACE, COLS)))(flat, pair_row, next_row)
    far_face = lax.ppermute(to_far, "depth", next_perm("depth"))
    near_face = lax.ppermute(to_near, "depth", swap_perm("depth", 1))
    smooth = call(
        smooth_kernel,
        tall,
        (
            pltpu.VMEM((PLANES + 3, ROWS, COLS), F32),
            pltpu.VMEM((40, COLS), F32),
            pltpu.VMEM((40, COLS), F32),
        ),
    )(flat, pair_row, next_row, near_face, far_face)
    y_port, y_factor, y_back, y_rest = call(row_kernel, (shaped(PLANES * PORT, COLS), lines, lines, lines))(
        flat, smooth
    )
    ports = lax.all_to_all(y_port, "lat", 0, 0, tiled=True)
    z_port, z_factor, z_back, z_rest, z_mid = call(
        plane_kernel, (port, whole, whole, whole, shaped(3, ROWS, COLS))
    )(flat, smooth)
    near = lax.ppermute(z_port, "depth", swap_perm("depth", 1))
    solved_x = call(
        column_kernel,
        whole,
        (
            pltpu.VMEM((512, COLS), F32),
            pltpu.VMEM((512, COLS), F32),
            pltpu.VMEM((16, 32, COLS), F32),
            pltpu.VMEM((16, 32, COLS), F32),
            pltpu.VMEM((16, 32, COLS), F32),
        ),
    )(flat, smooth)
    pair_own = call(lambda *refs: join_kernel(1, *refs), port)(z_port, near)
    pair = lax.ppermute(pair_own, "depth", swap_perm("depth", 2))
    quad_own = call(lambda *refs: join_kernel(2, *refs), port)(pair_own, pair)
    ports, quad_own, solved_x = lax.optimization_barrier((ports, quad_own, solved_x))
    ends = call(row_reduced_kernel, shaped(BLOCKS, 2, COLS))(ports)
    ends, quad_own = lax.optimization_barrier((ends, quad_own))
    quad = lax.ppermute(quad_own, "depth", swap_perm("depth", 4))
    others = call(finish_plane_kernel, whole)(
        z_port, near, pair, quad, z_factor, z_back, z_rest, z_mid, solved_x
    )
    ends_y = lax.all_to_all(ends, "lat", 0, 0, tiled=True)
    out = call(finish_row_kernel, whole)(ends_y, y_factor, y_back, y_rest, others)
    return out.reshape(PLANES, ROWS, COLS)


def solution(mesh):
    placed = (P("depth", "lat", None),)
    return jax.shard_map(
        shards, mesh=mesh, in_specs=placed, out_specs=P("depth", "lat", None), check_vma=False
    )
```

```python
import jax
import jax.numpy as jnp
from jax import lax
from jax.experimental import pallas as pl
from jax.experimental.pallas import tpu as pltpu
from jax.sharding import PartitionSpec as P

TAU3 = 900.0
INV_LAMBDA_SQ = 4.0
PLANES = 32
ROWS = 16
COLS = 128
BLOCKS = 32
PORT = 16
LONG = 100_000_000_000
F32 = jnp.float32


def resistance(diff):
    return (1.0 + INV_LAMBDA_SQ * (diff * diff)) * (1.0 / TAU3)


def smooth_lanes(field, first, last):
    before = jnp.where(first, 0.0, pltpu.roll(field, 1, field.ndim - 1))
    after = jnp.where(last, 0.0, pltpu.roll(field, COLS - 1, field.ndim - 1))
    return 0.25 * (before + 2.0 * field + after)


def eliminate(coupling, ground, source, near_ground, near_source, resist):
    factor = 1.0 / (1.0 + (coupling + ground) * resist)
    weight = factor * resist
    back = coupling * weight
    near_ground = near_ground + back * ground
    near_source = near_source + back * source
    saved = (factor, back, source * weight)
    return coupling * factor, ground * factor, source * factor, near_ground, near_source, saved


def eliminate_last(coupling, ground, source, near_ground, near_source, conduct):
    inverse = 1.0 / (coupling + ground + conduct)
    factor = conduct * inverse
    back = coupling * inverse
    near_ground = near_ground + back * ground
    near_source = near_source + back * source
    saved = (factor, back, source * inverse)
    return coupling * factor, ground * factor, source * factor, near_ground, near_source, saved


def join(left, right):
    lc, lg, lh, ls, lt = left
    rc, rg, rh, rs, rt = right
    ground = lh + rg
    source = lt + rs
    inverse = 1.0 / (lc + rc + ground)
    to_left = lc * inverse
    to_right = rc * inverse
    return (
        lc * to_right,
        lg + to_left * ground,
        rh + to_right * ground,
        ls + to_left * source,
        rt + to_right * source,
    ), (to_left, to_right, source * inverse)


def edge_kernel(parity, vol, out, sem):
    odd = lax.axis_index("depth") & 1
    start = pl.multiple_of((odd ^ parity) * ((PLANES - 2) * ROWS), ROWS)
    copy = pltpu.make_async_copy(vol.at[pl.ds(start, 2 * ROWS), :], out, sem)
    copy.start()
    copy.wait()


def strided(ref, row):
    return ref[pl.ds(row, 32, stride=16), :]


def cells(ref, plane):
    return ref[plane * ROWS : (plane + 1) * ROWS, :]


def deep_kernel(vol, near_side, far_side, deep, pair_row, next_row, mixed):
    odd = (lax.axis_index("depth") & 1) == 1
    lane = lax.broadcasted_iota(jnp.int32, (ROWS, COLS), 1)
    first, last = lane == 0, lane == COLS - 1
    mixed[0] = smooth_lanes(jnp.where(odd, cells(near_side, 1), cells(far_side, 1)), first, last)
    for plane in range(PLANES):
        mixed[plane + 1] = smooth_lanes(cells(vol, plane), first, last)
    for plane in range(2):
        mixed[PLANES + 1 + plane] = smooth_lanes(
            jnp.where(odd, cells(far_side, plane), cells(near_side, plane)), first, last
        )
    for plane in range(PLANES + 1):
        deep[plane * ROWS : (plane + 1) * ROWS, :] = 0.25 * (
            mixed[plane] + 2.0 * mixed[plane + 1] + mixed[plane + 2]
        )
    odd_row = (lax.axis_index("lat") & 1) == 1
    low = deep[pl.ds(0, PLANES + 1, stride=ROWS), :]
    high = deep[pl.ds(ROWS - 1, PLANES + 1, stride=ROWS), :]
    pair_row[...] = jnp.where(odd_row, low, high)
    next_row[...] = jnp.where(odd_row, high, low)


def plane_kernel(vol, deep, pair_row, next_row, port, factor, back, rest, mid, smooth):
    odd_row = (lax.axis_index("lat") & 1) == 1
    low_row = jnp.where(odd_row, pair_row[...], next_row[...])
    high_row = jnp.where(odd_row, next_row[...], pair_row[...])
    depth_last = lax.axis_index("depth") == lax.axis_size("depth") - 1
    z_open = jnp.where(depth_last, 0.0, TAU3).astype(F32)
    row_index = lax.broadcasted_iota(jnp.int32, (ROWS, COLS), 0)
    top, bottom = row_index == 0, row_index == ROWS - 1
    for plane in range(PLANES + 1):
        span = slice(plane * ROWS, (plane + 1) * ROWS)
        here = deep[span, :]
        above = jnp.where(top, low_row[plane : plane + 1, :], pltpu.roll(here, 1, 0))
        below = jnp.where(bottom, high_row[plane : plane + 1, :], pltpu.roll(here, ROWS - 1, 0))
        smooth[span, :] = 0.25 * (above + 2.0 * here + below)

    def resist(plane):
        return resistance(cells(smooth, plane + 1) - cells(smooth, plane))

    half = PLANES // 2
    one = jnp.ones((ROWS, COLS), F32)
    states = [
        (1.0 / resist(start), one, cells(vol, start + 1), one, cells(vol, start)) for start in (0, half)
    ]
    for step in range(1, half):
        final = step == half - 1
        for part in range(2):
            plane = part * half + step
            span = slice(plane * ROWS, (plane + 1) * ROWS)
            if final and part == 1:
                *state, saved = eliminate_last(*states[part], z_open / (TAU3 * resist(plane)))
            else:
                *state, saved = eliminate(*states[part], resist(plane))
            if not final:
                state[1] = state[1] + 1.0
                state[2] = state[2] + cells(vol, plane + 1)
            states[part] = state
            factor[span, :], back[span, :], rest[span, :] = saved
    joined, middle = join(*[(c, ng, fg, ns, fs) for c, fg, fs, ng, ns in states])
    for place, value in enumerate(joined):
        port[place] = value
    for place, value in enumerate(middle):
        mid[place] = value


def row_kernel(vol, deep, port, factor, back, rest):
    part = [strided(deep, row) for row in range(ROWS)]
    low_sum = 2.0 * part[0] + part[1]
    high_sum = part[ROWS - 2] + 2.0 * part[ROWS - 1]
    smooth = [None] + [0.25 * (part[r - 1] + 2.0 * part[r] + part[r + 1]) for r in range(1, ROWS - 1)]
    one = jnp.ones((PLANES, COLS), F32)
    state = (1.0 / resistance(smooth[2] - smooth[1]), one, strided(vol, 2), one, strided(vol, 1))
    for row in range(2, ROWS - 2):
        *state, saved = eliminate(*state, resistance(smooth[row + 1] - smooth[row]))
        state[1] = state[1] + 1.0
        state[2] = state[2] + strided(vol, row + 1)
        factor[row], back[row], rest[row] = saved
    coupling, far_ground, far_source, near_ground, near_source = state
    values = (
        coupling, near_ground, far_ground, near_source, far_source,
        part[0], part[ROWS - 1], low_sum, high_sum, smooth[1], smooth[ROWS - 2],
        strided(vol, 0), strided(vol, ROWS - 1),
    )
    for place, value in enumerate(values):
        port[pl.ds(place, PLANES, stride=PORT), :] = value
    for place in range(len(values), PORT):
        port[pl.ds(place, PLANES, stride=PORT), :] = jnp.zeros((PLANES, COLS), F32)


def chain_solve(coupling, near_ground, far_ground, near_source, far_source, count):
    size = coupling.shape[0]
    right = coupling
    ground = near_ground + pltpu.roll(far_ground, 1, 0)
    source = near_source + pltpu.roll(far_source, 1, 0)
    step = 1
    while step < count:
        left = pltpu.roll(right, step, 0)
        inverse = 1.0 / (ground + left + right)
        ground_part = ground * inverse
        source_part = source * inverse
        ground = (
            ground
            + left * pltpu.roll(ground_part, step, 0)
            + right * pltpu.roll(ground_part, size - step, 0)
        )
        source = (
            source
            + left * pltpu.roll(source_part, step, 0)
            + right * pltpu.roll(source_part, size - step, 0)
        )
        right = right * pltpu.roll(right * inverse, size - step, 0)
        step *= 2
    return source / ground


def column_kernel(vol, smooth, solved_x, turned, turned_smooth, factor, back, rest):
    for group in range(4):
        span = slice(group * COLS, (group + 1) * COLS)
        turned[span, :] = vol[span, :].T
        turned_smooth[span, :] = smooth[span, :].T

    def resist(step):
        if step < 15:
            return resistance(strided(turned_smooth, step + 1) - strided(turned_smooth, step))
        return resistance(pltpu.roll(strided(turned_smooth, 0), 31, 0) - strided(turned_smooth, 15))

    chunk_last = (lax.broadcasted_iota(jnp.int32, (32, COLS), 0) & 7) == 7
    one = jnp.ones((32, COLS), F32)
    state = (1.0 / resist(0), one, strided(turned, 1), one, strided(turned, 0))
    for step in range(1, 16):
        if step == 15:
            *state, saved = eliminate_last(*state, jnp.where(chunk_last, 0.0, 1.0 / resist(step)))
        else:
            *state, saved = eliminate(*state, resist(step))
            state[1] = state[1] + 1.0
            state[2] = state[2] + strided(turned, step + 1)
        factor[step], back[step], rest[step] = saved
    coupling, far_ground, far_source, near_ground, near_source = state
    first = chain_solve(coupling, near_ground, far_ground, near_source, far_source, 8)
    turned[pl.ds(0, 32, stride=16), :] = first
    value = pltpu.roll(first, 31, 0)
    for step in range(15, 0, -1):
        value = factor[step] * value + (back[step] * first + rest[step])
        turned[pl.ds(step, 32, stride=16), :] = value
    for group in range(4):
        span = slice(group * COLS, (group + 1) * COLS)
        solved_x[span, :] = turned[span, :].T


def row_reduced_kernel(ports, out):
    (
        coupling, near_ground, far_ground, near_source, far_source,
        low, high, low_sum, high_sum, low_smooth, high_smooth, low_cell, high_cell,
    ) = (ports[pl.ds(place, BLOCKS, stride=PORT), :] for place in range(13))
    block = lax.broadcasted_iota(jnp.int32, (BLOCKS, COLS), 0)
    block_first, block_last = block == 0, block == BLOCKS - 1
    low_end = 0.25 * (jnp.where(block_first, 0.0, pltpu.roll(high, 1, 0)) + low_sum)
    high_end = 0.25 * (high_sum + jnp.where(block_last, 0.0, pltpu.roll(low, BLOCKS - 1, 0)))
    enter = 1.0 / resistance(low_smooth - low_end)
    leave = 1.0 / resistance(high_end - high_smooth)
    across = pltpu.roll(low_end, BLOCKS - 1, 0) - high_end
    across = jnp.where(block_last, 0.0, 1.0 / resistance(across))
    zero = jnp.zeros_like(coupling)
    one = jnp.ones_like(coupling)
    before, at_low = join(
        (enter, one, zero, low_cell, zero), (coupling, near_ground, far_ground, near_source, far_source)
    )
    after, at_high = join((leave, zero, one, zero, high_cell), (across, zero, zero, zero, zero))
    whole, between = join(before, after)
    first = chain_solve(*whole, BLOCKS)
    later = pltpu.roll(first, BLOCKS - 1, 0)

    def middle(weights, left, right):
        return weights[0] * left + weights[1] * right + weights[2]

    inner_high = middle(between, first, later)
    out[:, 0, :] = first
    out[:, 1, :] = middle(at_low, first, inner_high)
    out[:, 2, :] = inner_high
    out[:, 3, :] = middle(at_high, inner_high, later)


def pick(flag, there, here):
    return tuple(jnp.where(flag, a, b) for a, b in zip(there, here))


def join_kernel(bit, own, other, out):
    upper = (lax.axis_index("depth") & bit) != 0
    mine = tuple(own[place] for place in range(5))
    theirs = tuple(other[place] for place in range(5))
    port, _ = join(pick(upper, theirs, mine), pick(upper, mine, theirs))
    for place, value in enumerate(port):
        out[place] = value


def finish_plane_kernel(
    own, near, pair, quad, factor, back, rest, mid, solved_x, out,
):
    index = lax.axis_index("depth")
    zero = jnp.zeros((ROWS, COLS), F32)
    left_ground, left_source, right_ground, right_source = zero, zero, zero, zero
    for bit, ref in ((4, quad), (2, pair), (1, near)):
        on_left = (index & bit) != 0
        c, ng, fg, ns, fs = (ref[place] for place in range(5))
        ground, source = ng + left_ground, ns + left_source
        share = c / (c + ground)
        left_ground = jnp.where(on_left, fg + share * ground, left_ground)
        left_source = jnp.where(on_left, fs + share * source, left_source)
        ground, source = fg + right_ground, fs + right_source
        total = c + ground
        share = jnp.where(total > 0.0, c / jnp.where(total > 0.0, total, 1.0), 0.0)
        right_ground = jnp.where(on_left, right_ground, ng + share * ground)
        right_source = jnp.where(on_left, right_source, ns + share * source)
    c, ng, fg, ns, fs = (own[place] for place in range(5))
    ground, source = fg + right_ground, fs + right_source
    total = c + ground
    inverse = jnp.where(total > 0.0, 1.0 / jnp.where(total > 0.0, total, 1.0), 0.0)
    share = c * inverse
    first = (left_source + ns + share * source) / (left_ground + ng + share * ground)
    after = share * first + source * inverse
    middle = mid[0] * first + mid[1] * after + mid[2]
    half = PLANES // 2
    for start, near_value, far_value in ((0, first, middle), (half, middle, after)):
        value = far_value
        for plane in range(start + half - 1, start, -1):
            span = slice(plane * ROWS, (plane + 1) * ROWS)
            value = factor[span, :] * value + (back[span, :] * near_value + rest[span, :])
            out[span, :] = solved_x[span, :] + value
        span = slice(start * ROWS, (start + 1) * ROWS)
        out[span, :] = solved_x[span, :] + near_value


def finish_row_kernel(ends, factor, back, rest, others, out):
    third = 1.0 / 3.0

    def put(row, value):
        place = pl.ds(row, PLANES, stride=ROWS)
        out[place, :] = (others[place, :] + value) * third

    for place, row in ((0, 0), (1, 1), (2, ROWS - 2), (3, ROWS - 1)):
        put(row, ends[:, place, :])
    first = ends[:, 1, :]
    value = ends[:, 2, :]
    for row in range(ROWS - 3, 1, -1):
        value = factor[row] * value + (back[row] * first + rest[row])
        put(row, value)


def call(kernel, outs, scratch=(), flops=1000000, moved=500000, **options):
    return pl.pallas_call(
        kernel,
        out_shape=outs,
        scratch_shapes=scratch,
        compiler_params=pltpu.CompilerParams(vmem_limit_bytes=16 * 1024 * 1024),
        cost_estimate=pl.CostEstimate(flops=flops, bytes_accessed=moved, transcendentals=0),
        **options,
    )


def shaped(*shape):
    return jax.ShapeDtypeStruct(shape, F32)


def line_perm(axis, step):
    count = lax.axis_size(axis)
    if step > 0:
        return [(i, i + 1) for i in range(count - 1)]
    return [(i + 1, i) for i in range(count - 1)]


def swap_perm(axis, bit):
    return [(i, i ^ bit) for i in range(lax.axis_size(axis))]


def next_perm(axis):
    pairs = []
    for i in range(1, lax.axis_size(axis) - 1, 2):
        pairs += [(i, i + 1), (i + 1, i)]
    return pairs


def shards(volume):
    flat = volume.reshape(PLANES * ROWS, COLS)
    lines = shaped(ROWS, PLANES, COLS)
    whole = shaped(PLANES * ROWS, COLS)
    tall = shaped((PLANES + 1) * ROWS, COLS)
    port = shaped(5, ROWS, COLS)
    side = shaped(PLANES + 1, COLS)
    to_far, to_near = (
        call(
            lambda *refs, parity=parity: edge_kernel(parity, *refs),
            shaped(2 * ROWS, COLS),
            (pltpu.SemaphoreType.DMA,),
            in_specs=[pl.BlockSpec(memory_space=pl.ANY)],
            flops=flops,
        )(flat)
        for parity, flops in ((0, 1), (1, LONG))
    )
    far_side = lax.ppermute(to_far, "depth", next_perm("depth"))
    near_side = lax.ppermute(to_near, "depth", swap_perm("depth", 1))
    deep, to_pair, to_next = call(
        deep_kernel, (tall, side, side), (pltpu.VMEM((PLANES + 3, ROWS, COLS), F32),)
    )(flat, near_side, far_side)
    next_row = lax.ppermute(to_next, "lat", next_perm("lat"))
    pair_row = lax.ppermute(to_pair, "lat", swap_perm("lat", 1))
    y_port, y_factor, y_back, y_rest = call(row_kernel, (shaped(PLANES * PORT, COLS), lines, lines, lines))(
        flat, deep
    )
    ports = lax.all_to_all(y_port, "lat", 0, 0, tiled=True)
    z_port, z_factor, z_back, z_rest, z_mid, smooth = call(
        plane_kernel, (port, whole, whole, whole, shaped(3, ROWS, COLS), tall), flops=LONG
    )(flat, deep, pair_row, next_row)
    near = lax.ppermute(z_port, "depth", swap_perm("depth", 1))
    solved_x = call(
        column_kernel,
        whole,
        (
            pltpu.VMEM((512, COLS), F32),
            pltpu.VMEM((512, COLS), F32),
            pltpu.VMEM((16, 32, COLS), F32),
            pltpu.VMEM((16, 32, COLS), F32),
            pltpu.VMEM((16, 32, COLS), F32),
        ),
    )(flat, smooth)
    pair_own = call(lambda *refs: join_kernel(1, *refs), port)(z_port, near)
    pair = lax.ppermute(pair_own, "depth", swap_perm("depth", 2))
    quad_own = call(lambda *refs: join_kernel(2, *refs), port)(pair_own, pair)
    quad = lax.ppermute(quad_own, "depth", swap_perm("depth", 4))
    ports, solved_x = lax.optimization_barrier((ports, solved_x))
    ends = call(row_reduced_kernel, shaped(BLOCKS, 4, COLS))(ports)
    others = call(finish_plane_kernel, whole, flops=LONG)(
        z_port, near, pair, quad, z_factor, z_back, z_rest, z_mid, solved_x
    )
    ends_y = lax.all_to_all(ends, "lat", 0, 0, tiled=True)
    out = call(finish_row_kernel, whole)(ends_y, y_factor, y_back, y_rest, others)
    return out.reshape(PLANES, ROWS, COLS)


def solution(mesh):
    placed = (P("depth", "lat", None),)
    return jax.shard_map(
        shards, mesh=mesh, in_specs=placed, out_specs=P("depth", "lat", None), check_vma=False
    )
```

```python
import jax
import jax.numpy as jnp
from jax import lax
from jax.experimental import pallas as pl
from jax.experimental.pallas import tpu as pltpu
from jax.sharding import PartitionSpec as P

TAU3 = 900.0
INV_LAMBDA_SQ = 4.0
PLANES = 32
ROWS = 16
COLS = 128
BLOCKS = 32
PORT = 16
CORNER = 8
F32 = jnp.float32


def resistance(diff):
    return (1.0 + INV_LAMBDA_SQ * (diff * diff)) * (1.0 / TAU3)


def smooth_lanes(field, first, last):
    before = jnp.where(first, 0.0, pltpu.roll(field, 1, field.ndim - 1))
    after = jnp.where(last, 0.0, pltpu.roll(field, COLS - 1, field.ndim - 1))
    return 0.25 * (before + 2.0 * field + after)


def eliminate(coupling, ground, source, near_ground, near_source, resist):
    factor = 1.0 / (1.0 + (coupling + ground) * resist)
    weight = factor * resist
    back = coupling * weight
    near_ground = near_ground + back * ground
    near_source = near_source + back * source
    saved = (factor, back, source * weight)
    return coupling * factor, ground * factor, source * factor, near_ground, near_source, saved


def eliminate_last(coupling, ground, source, near_ground, near_source, conduct):
    inverse = 1.0 / (coupling + ground + conduct)
    factor = conduct * inverse
    back = coupling * inverse
    near_ground = near_ground + back * ground
    near_source = near_source + back * source
    saved = (factor, back, source * inverse)
    return coupling * factor, ground * factor, source * factor, near_ground, near_source, saved


def join(left, right):
    lc, lg, lh, ls, lt = left
    rc, rg, rh, rs, rt = right
    ground = lh + rg
    source = lt + rs
    inverse = 1.0 / (lc + rc + ground)
    to_left = lc * inverse
    to_right = rc * inverse
    return (
        lc * to_right,
        lg + to_left * ground,
        rh + to_right * ground,
        ls + to_left * source,
        rt + to_right * source,
    ), (to_left, to_right, source * inverse)


def edge_kernel(vol, near_side, far_side, sems):
    odd = lax.axis_index("depth") & 1
    high = (PLANES - 2) * ROWS
    near_start = pl.multiple_of((1 - odd) * high, ROWS)
    far_start = pl.multiple_of(odd * high, ROWS)
    copies = (
        pltpu.make_async_copy(vol.at[pl.ds(near_start, 2 * ROWS), :], near_side, sems.at[0]),
        pltpu.make_async_copy(vol.at[pl.ds(far_start, 2 * ROWS), :], far_side, sems.at[1]),
    )
    for copy in copies:
        copy.start()
    for copy in copies:
        copy.wait()


def side_kernel(vol, pair_row, next_row):
    odd = (lax.axis_index("lat") & 1) == 1
    low = vol[pl.ds(0, PLANES, stride=ROWS), :]
    high = vol[pl.ds(ROWS - 1, PLANES, stride=ROWS), :]
    pair_row[...] = jnp.where(odd, low, high)
    next_row[...] = jnp.where(odd, high, low)


def side_rows(pair_row, next_row):
    odd = (lax.axis_index("lat") & 1) == 1
    return jnp.where(odd, pair_row, next_row), jnp.where(odd, next_row, pair_row)


def corner_kernel(pair_row, next_row, near_corner, far_corner):
    odd = (lax.axis_index("depth") & 1) == 1
    for place, side in zip((0, 2), side_rows(pair_row[...], next_row[...])):
        near_corner[place : place + 2, :] = jnp.where(odd, side[0:2, :], side[PLANES - 2 :, :])
        far_corner[place : place + 2, :] = jnp.where(odd, side[PLANES - 2 :, :], side[0:2, :])
    near_corner[4:CORNER, :] = jnp.zeros((CORNER - 4, COLS), F32)
    far_corner[4:CORNER, :] = jnp.zeros((CORNER - 4, COLS), F32)


def strided(ref, row):
    return ref[pl.ds(row, 32, stride=16), :]


def cells(ref, plane):
    return ref[plane * ROWS : (plane + 1) * ROWS, :]


def deep_kernel(vol, near_side, far_side, deep, mixed):
    odd = (lax.axis_index("depth") & 1) == 1
    lane = lax.broadcasted_iota(jnp.int32, (ROWS, COLS), 1)
    first, last = lane == 0, lane == COLS - 1
    mixed[0] = smooth_lanes(jnp.where(odd, cells(near_side, 1), cells(far_side, 1)), first, last)
    for plane in range(PLANES):
        mixed[plane + 1] = smooth_lanes(cells(vol, plane), first, last)
    for plane in range(2):
        mixed[PLANES + 1 + plane] = smooth_lanes(
            jnp.where(odd, cells(far_side, plane), cells(near_side, plane)), first, last
        )
    for plane in range(PLANES + 1):
        deep[plane * ROWS : (plane + 1) * ROWS, :] = 0.25 * (
            mixed[plane] + 2.0 * mixed[plane + 1] + mixed[plane + 2]
        )


def plane_kernel(
    vol, deep, pair_row, next_row, near_corner, far_corner,
    port, factor, back, rest, mid, smooth,
    low_side, high_side,
):
    odd = (lax.axis_index("depth") & 1) == 1
    depth_last = lax.axis_index("depth") == lax.axis_size("depth") - 1
    z_open = jnp.where(depth_last, 0.0, TAU3).astype(F32)
    near, far = near_corner[...], far_corner[...]
    below_corner, above_corner = jnp.where(odd, near, far), jnp.where(odd, far, near)
    side_lane = lax.broadcasted_iota(jnp.int32, (PLANES + 3, COLS), 1)
    sides = []
    for place, ref, own in zip((0, 2), (low_side, high_side), side_rows(pair_row[...], next_row[...])):
        ref[0:1, :] = below_corner[place + 1 : place + 2, :]
        ref[1 : PLANES + 1, :] = own
        ref[PLANES + 1 : PLANES + 3, :] = above_corner[place : place + 2, :]
        ref[0 : PLANES + 3, :] = smooth_lanes(ref[0 : PLANES + 3, :], side_lane == 0, side_lane == COLS - 1)
        sides.append(
            0.25 * (ref[0 : PLANES + 1, :] + 2.0 * ref[1 : PLANES + 2, :] + ref[2 : PLANES + 3, :])
        )
    row_index = lax.broadcasted_iota(jnp.int32, (ROWS, COLS), 0)
    top, bottom = row_index == 0, row_index == ROWS - 1
    for plane in range(PLANES + 1):
        span = slice(plane * ROWS, (plane + 1) * ROWS)
        here = deep[span, :]
        above = jnp.where(top, sides[0][plane : plane + 1, :], pltpu.roll(here, 1, 0))
        below = jnp.where(bottom, sides[1][plane : plane + 1, :], pltpu.roll(here, ROWS - 1, 0))
        smooth[span, :] = 0.25 * (above + 2.0 * here + below)

    def resist(plane):
        return resistance(cells(smooth, plane + 1) - cells(smooth, plane))

    half = PLANES // 2
    one = jnp.ones((ROWS, COLS), F32)
    states = [
        (1.0 / resist(start), one, cells(vol, start + 1), one, cells(vol, start)) for start in (0, half)
    ]
    for step in range(1, half):
        final = step == half - 1
        for part in range(2):
            plane = part * half + step
            span = slice(plane * ROWS, (plane + 1) * ROWS)
            if final and part == 1:
                *state, saved = eliminate_last(*states[part], z_open / (TAU3 * resist(plane)))
            else:
                *state, saved = eliminate(*states[part], resist(plane))
            if not final:
                state[1] = state[1] + 1.0
                state[2] = state[2] + cells(vol, plane + 1)
            states[part] = state
            factor[span, :], back[span, :], rest[span, :] = saved
    joined, middle = join(*[(c, ng, fg, ns, fs) for c, fg, fs, ng, ns in states])
    for place, value in enumerate(joined):
        port[place] = value
    for place, value in enumerate(middle):
        mid[place] = value


def row_kernel(vol, deep, port, factor, back, rest):
    part = [strided(deep, row) for row in range(ROWS)]
    low_sum = 2.0 * part[0] + part[1]
    high_sum = part[ROWS - 2] + 2.0 * part[ROWS - 1]
    smooth = [None] + [0.25 * (part[r - 1] + 2.0 * part[r] + part[r + 1]) for r in range(1, ROWS - 1)]
    one = jnp.ones((PLANES, COLS), F32)
    state = (1.0 / resistance(smooth[2] - smooth[1]), one, strided(vol, 2), one, strided(vol, 1))
    for row in range(2, ROWS - 2):
        *state, saved = eliminate(*state, resistance(smooth[row + 1] - smooth[row]))
        state[1] = state[1] + 1.0
        state[2] = state[2] + strided(vol, row + 1)
        factor[row], back[row], rest[row] = saved
    coupling, far_ground, far_source, near_ground, near_source = state
    values = (
        coupling, near_ground, far_ground, near_source, far_source,
        part[0], part[ROWS - 1], low_sum, high_sum, smooth[1], smooth[ROWS - 2],
        strided(vol, 0), strided(vol, ROWS - 1),
    )
    for place, value in enumerate(values):
        port[pl.ds(place, PLANES, stride=PORT), :] = value
    for place in range(len(values), PORT):
        port[pl.ds(place, PLANES, stride=PORT), :] = jnp.zeros((PLANES, COLS), F32)


def chain_solve(coupling, near_ground, far_ground, near_source, far_source, count):
    size = coupling.shape[0]
    right = coupling
    ground = near_ground + pltpu.roll(far_ground, 1, 0)
    source = near_source + pltpu.roll(far_source, 1, 0)
    step = 1
    while step < count:
        left = pltpu.roll(right, step, 0)
        inverse = 1.0 / (ground + left + right)
        ground_part = ground * inverse
        source_part = source * inverse
        ground = (
            ground
            + left * pltpu.roll(ground_part, step, 0)
            + right * pltpu.roll(ground_part, size - step, 0)
        )
        source = (
            source
            + left * pltpu.roll(source_part, step, 0)
            + right * pltpu.roll(source_part, size - step, 0)
        )
        right = right * pltpu.roll(right * inverse, size - step, 0)
        step *= 2
    return source / ground


def column_kernel(vol, smooth, solved_x, turned, turned_smooth, factor, back, rest):
    for group in range(4):
        span = slice(group * COLS, (group + 1) * COLS)
        turned[span, :] = vol[span, :].T
        turned_smooth[span, :] = smooth[span, :].T

    def resist(step):
        if step < 15:
            return resistance(strided(turned_smooth, step + 1) - strided(turned_smooth, step))
        return resistance(pltpu.roll(strided(turned_smooth, 0), 31, 0) - strided(turned_smooth, 15))

    chunk_last = (lax.broadcasted_iota(jnp.int32, (32, COLS), 0) & 7) == 7
    one = jnp.ones((32, COLS), F32)
    state = (1.0 / resist(0), one, strided(turned, 1), one, strided(turned, 0))
    for step in range(1, 16):
        if step == 15:
            *state, saved = eliminate_last(*state, jnp.where(chunk_last, 0.0, 1.0 / resist(step)))
        else:
            *state, saved = eliminate(*state, resist(step))
            state[1] = state[1] + 1.0
            state[2] = state[2] + strided(turned, step + 1)
        factor[step], back[step], rest[step] = saved
    coupling, far_ground, far_source, near_ground, near_source = state
    first = chain_solve(coupling, near_ground, far_ground, near_source, far_source, 8)
    turned[pl.ds(0, 32, stride=16), :] = first
    value = pltpu.roll(first, 31, 0)
    for step in range(15, 0, -1):
        value = factor[step] * value + (back[step] * first + rest[step])
        turned[pl.ds(step, 32, stride=16), :] = value
    for group in range(4):
        span = slice(group * COLS, (group + 1) * COLS)
        solved_x[span, :] = turned[span, :].T


def row_reduced_kernel(ports, out):
    (
        coupling, near_ground, far_ground, near_source, far_source,
        low, high, low_sum, high_sum, low_smooth, high_smooth, low_cell, high_cell,
    ) = (ports[pl.ds(place, BLOCKS, stride=PORT), :] for place in range(13))
    block = lax.broadcasted_iota(jnp.int32, (BLOCKS, COLS), 0)
    block_first, block_last = block == 0, block == BLOCKS - 1
    low_end = 0.25 * (jnp.where(block_first, 0.0, pltpu.roll(high, 1, 0)) + low_sum)
    high_end = 0.25 * (high_sum + jnp.where(block_last, 0.0, pltpu.roll(low, BLOCKS - 1, 0)))
    enter = 1.0 / resistance(low_smooth - low_end)
    leave = 1.0 / resistance(high_end - high_smooth)
    across = pltpu.roll(low_end, BLOCKS - 1, 0) - high_end
    across = jnp.where(block_last, 0.0, 1.0 / resistance(across))
    zero = jnp.zeros_like(coupling)
    one = jnp.ones_like(coupling)
    before, at_low = join(
        (enter, one, zero, low_cell, zero), (coupling, near_ground, far_ground, near_source, far_source)
    )
    after, at_high = join((leave, zero, one, zero, high_cell), (across, zero, zero, zero, zero))
    whole, between = join(before, after)
    first = chain_solve(*whole, BLOCKS)
    later = pltpu.roll(first, BLOCKS - 1, 0)

    def middle(weights, left, right):
        return weights[0] * left + weights[1] * right + weights[2]

    inner_high = middle(between, first, later)
    out[:, 0, :] = first
    out[:, 1, :] = middle(at_low, first, inner_high)
    out[:, 2, :] = inner_high
    out[:, 3, :] = middle(at_high, inner_high, later)


def pick(flag, there, here):
    return tuple(jnp.where(flag, a, b) for a, b in zip(there, here))


def join_kernel(bit, own, other, out):
    upper = (lax.axis_index("depth") & bit) != 0
    mine = tuple(own[place] for place in range(5))
    theirs = tuple(other[place] for place in range(5))
    port, _ = join(pick(upper, theirs, mine), pick(upper, mine, theirs))
    for place, value in enumerate(port):
        out[place] = value


def finish_plane_kernel(
    own, near, pair, quad, factor, back, rest, mid, solved_x, out,
):
    index = lax.axis_index("depth")
    zero = jnp.zeros((ROWS, COLS), F32)
    left_ground, left_source, right_ground, right_source = zero, zero, zero, zero
    for bit, ref in ((4, quad), (2, pair), (1, near)):
        on_left = (index & bit) != 0
        c, ng, fg, ns, fs = (ref[place] for place in range(5))
        ground, source = ng + left_ground, ns + left_source
        share = c / (c + ground)
        left_ground = jnp.where(on_left, fg + share * ground, left_ground)
        left_source = jnp.where(on_left, fs + share * source, left_source)
        ground, source = fg + right_ground, fs + right_source
        total = c + ground
        share = jnp.where(total > 0.0, c / jnp.where(total > 0.0, total, 1.0), 0.0)
        right_ground = jnp.where(on_left, right_ground, ng + share * ground)
        right_source = jnp.where(on_left, right_source, ns + share * source)
    c, ng, fg, ns, fs = (own[place] for place in range(5))
    ground, source = fg + right_ground, fs + right_source
    total = c + ground
    inverse = jnp.where(total > 0.0, 1.0 / jnp.where(total > 0.0, total, 1.0), 0.0)
    share = c * inverse
    first = (left_source + ns + share * source) / (left_ground + ng + share * ground)
    after = share * first + source * inverse
    middle = mid[0] * first + mid[1] * after + mid[2]
    half = PLANES // 2
    for start, near_value, far_value in ((0, first, middle), (half, middle, after)):
        value = far_value
        for plane in range(start + half - 1, start, -1):
            span = slice(plane * ROWS, (plane + 1) * ROWS)
            value = factor[span, :] * value + (back[span, :] * near_value + rest[span, :])
            out[span, :] = solved_x[span, :] + value
        span = slice(start * ROWS, (start + 1) * ROWS)
        out[span, :] = solved_x[span, :] + near_value


def finish_row_kernel(ends, factor, back, rest, others, out):
    third = 1.0 / 3.0

    def put(row, value):
        place = pl.ds(row, PLANES, stride=ROWS)
        out[place, :] = (others[place, :] + value) * third

    for place, row in ((0, 0), (1, 1), (2, ROWS - 2), (3, ROWS - 1)):
        put(row, ends[:, place, :])
    first = ends[:, 1, :]
    value = ends[:, 2, :]
    for row in range(ROWS - 3, 1, -1):
        value = factor[row] * value + (back[row] * first + rest[row])
        put(row, value)


def call(kernel, outs, scratch=(), flops=1000000, moved=500000, **options):
    return pl.pallas_call(
        kernel,
        out_shape=outs,
        scratch_shapes=scratch,
        compiler_params=pltpu.CompilerParams(vmem_limit_bytes=16 * 1024 * 1024),
        cost_estimate=pl.CostEstimate(flops=flops, bytes_accessed=moved, transcendentals=0),
        **options,
    )


def shaped(*shape):
    return jax.ShapeDtypeStruct(shape, F32)


def line_perm(axis, step):
    count = lax.axis_size(axis)
    if step > 0:
        return [(i, i + 1) for i in range(count - 1)]
    return [(i + 1, i) for i in range(count - 1)]


def swap_perm(axis, bit):
    return [(i, i ^ bit) for i in range(lax.axis_size(axis))]


def next_perm(axis):
    pairs = []
    for i in range(1, lax.axis_size(axis) - 1, 2):
        pairs += [(i, i + 1), (i + 1, i)]
    return pairs


def shards(volume):
    flat = volume.reshape(PLANES * ROWS, COLS)
    lines = shaped(ROWS, PLANES, COLS)
    whole = shaped(PLANES * ROWS, COLS)
    tall = shaped((PLANES + 1) * ROWS, COLS)
    port = shaped(5, ROWS, COLS)
    to_near, to_far = call(
        edge_kernel,
        (shaped(2 * ROWS, COLS), shaped(2 * ROWS, COLS)),
        (pltpu.SemaphoreType.DMA((2,)),),
        in_specs=[pl.BlockSpec(memory_space=pl.ANY)],
    )(flat)
    to_pair, to_next = call(side_kernel, (shaped(PLANES, COLS), shaped(PLANES, COLS)))(flat)
    next_row = lax.ppermute(to_next, "lat", next_perm("lat"))
    pair_row = lax.ppermute(to_pair, "lat", swap_perm("lat", 1))
    far_side = lax.ppermute(to_far, "depth", next_perm("depth"))
    near_side = lax.ppermute(to_near, "depth", swap_perm("depth", 1))
    next_row, pair_row, far_side, near_side = lax.optimization_barrier((next_row, pair_row, far_side, near_side))
    deep = call(deep_kernel, tall, (pltpu.VMEM((PLANES + 3, ROWS, COLS), F32),))(flat, near_side, far_side)
    y_port, y_factor, y_back, y_rest = call(row_kernel, (shaped(PLANES * PORT, COLS), lines, lines, lines))(
        flat, deep
    )
    ports = lax.all_to_all(y_port, "lat", 0, 0, tiled=True)
    corner = shaped(CORNER, COLS)
    to_near, to_far = call(corner_kernel, (corner, corner))(pair_row, next_row)
    far_corner = lax.ppermute(to_far, "depth", next_perm("depth"))
    near_corner = lax.ppermute(to_near, "depth", swap_perm("depth", 1))
    z_port, z_factor, z_back, z_rest, z_mid, smooth = call(
        plane_kernel,
        (port, whole, whole, whole, shaped(3, ROWS, COLS), tall),
        (pltpu.VMEM((40, COLS), F32), pltpu.VMEM((40, COLS), F32)),
    )(flat, deep, pair_row, next_row, near_corner, far_corner)
    near = lax.ppermute(z_port, "depth", swap_perm("depth", 1))
    solved_x = call(
        column_kernel,
        whole,
        (
            pltpu.VMEM((512, COLS), F32),
            pltpu.VMEM((512, COLS), F32),
            pltpu.VMEM((16, 32, COLS), F32),
            pltpu.VMEM((16, 32, COLS), F32),
            pltpu.VMEM((16, 32, COLS), F32),
        ),
    )(flat, smooth)
    pair_own = call(lambda *refs: join_kernel(1, *refs), port)(z_port, near)
    pair = lax.ppermute(pair_own, "depth", swap_perm("depth", 2))
    quad_own = call(lambda *refs: join_kernel(2, *refs), port)(pair_own, pair)
    ports, quad_own, solved_x = lax.optimization_barrier((ports, quad_own, solved_x))
    ends = call(row_reduced_kernel, shaped(BLOCKS, 4, COLS))(ports)
    ends, quad_own = lax.optimization_barrier((ends, quad_own))
    quad = lax.ppermute(quad_own, "depth", swap_perm("depth", 4))
    others = call(finish_plane_kernel, whole)(
        z_port, near, pair, quad, z_factor, z_back, z_rest, z_mid, solved_x
    )
    ends_y = lax.all_to_all(ends, "lat", 0, 0, tiled=True)
    out = call(finish_row_kernel, whole)(ends_y, y_factor, y_back, y_rest, others)
    return out.reshape(PLANES, ROWS, COLS)


def solution(mesh):
    placed = (P("depth", "lat", None),)
    return jax.shard_map(
        shards, mesh=mesh, in_specs=placed, out_specs=P("depth", "lat", None), check_vma=False
    )
```

```python
import jax
import jax.numpy as jnp
from jax import lax
from jax.experimental import pallas as pl
from jax.experimental.pallas import tpu as pltpu
from jax.sharding import PartitionSpec as P

TAU3 = 900.0
INV_LAMBDA_SQ = 4.0
PLANES = 32
ROWS = 16
COLS = 128
BLOCKS = 32
PORT = 16
LONG = 100_000_000_000
F32 = jnp.float32


def resistance(diff):
    return (1.0 + INV_LAMBDA_SQ * (diff * diff)) * (1.0 / TAU3)


def smooth_lanes(field, first, last):
    before = jnp.where(first, 0.0, pltpu.roll(field, 1, field.ndim - 1))
    after = jnp.where(last, 0.0, pltpu.roll(field, COLS - 1, field.ndim - 1))
    return 0.25 * (before + 2.0 * field + after)


def eliminate(coupling, ground, source, near_ground, near_source, resist):
    factor = 1.0 / (1.0 + (coupling + ground) * resist)
    weight = factor * resist
    back = coupling * weight
    near_ground = near_ground + back * ground
    near_source = near_source + back * source
    saved = (factor, back, source * weight)
    return coupling * factor, ground * factor, source * factor, near_ground, near_source, saved


def eliminate_last(coupling, ground, source, near_ground, near_source, conduct):
    inverse = 1.0 / (coupling + ground + conduct)
    factor = conduct * inverse
    back = coupling * inverse
    near_ground = near_ground + back * ground
    near_source = near_source + back * source
    saved = (factor, back, source * inverse)
    return coupling * factor, ground * factor, source * factor, near_ground, near_source, saved


def join(left, right):
    lc, lg, lh, ls, lt = left
    rc, rg, rh, rs, rt = right
    ground = lh + rg
    source = lt + rs
    inverse = 1.0 / (lc + rc + ground)
    to_left = lc * inverse
    to_right = rc * inverse
    return (
        lc * to_right,
        lg + to_left * ground,
        rh + to_right * ground,
        ls + to_left * source,
        rt + to_right * source,
    ), (to_left, to_right, source * inverse)


def edge_kernel(vol, near_side, far_side, sems):
    odd = lax.axis_index("depth") & 1
    high = (PLANES - 2) * ROWS
    near_start = pl.multiple_of((1 - odd) * high, ROWS)
    far_start = pl.multiple_of(odd * high, ROWS)
    copies = (
        pltpu.make_async_copy(vol.at[pl.ds(near_start, 2 * ROWS), :], near_side, sems.at[0]),
        pltpu.make_async_copy(vol.at[pl.ds(far_start, 2 * ROWS), :], far_side, sems.at[1]),
    )
    for copy in copies:
        copy.start()
    for copy in copies:
        copy.wait()


def strided(ref, row):
    return ref[pl.ds(row, 32, stride=16), :]


def cells(ref, plane):
    return ref[plane * ROWS : (plane + 1) * ROWS, :]


def deep_kernel(vol, near_side, far_side, deep, pair_row, next_row, mixed):
    odd = (lax.axis_index("depth") & 1) == 1
    lane = lax.broadcasted_iota(jnp.int32, (ROWS, COLS), 1)
    first, last = lane == 0, lane == COLS - 1
    mixed[0] = smooth_lanes(jnp.where(odd, cells(near_side, 1), cells(far_side, 1)), first, last)
    for plane in range(PLANES):
        mixed[plane + 1] = smooth_lanes(cells(vol, plane), first, last)
    for plane in range(2):
        mixed[PLANES + 1 + plane] = smooth_lanes(
            jnp.where(odd, cells(far_side, plane), cells(near_side, plane)), first, last
        )
    for plane in range(PLANES + 1):
        deep[plane * ROWS : (plane + 1) * ROWS, :] = 0.25 * (
            mixed[plane] + 2.0 * mixed[plane + 1] + mixed[plane + 2]
        )
    odd_row = (lax.axis_index("lat") & 1) == 1
    low = deep[pl.ds(0, PLANES + 1, stride=ROWS), :]
    high = deep[pl.ds(ROWS - 1, PLANES + 1, stride=ROWS), :]
    pair_row[...] = jnp.where(odd_row, low, high)
    next_row[...] = jnp.where(odd_row, high, low)


def plane_kernel(vol, deep, pair_row, next_row, port, factor, back, rest, mid, smooth):
    odd_row = (lax.axis_index("lat") & 1) == 1
    low_row = jnp.where(odd_row, pair_row[...], next_row[...])
    high_row = jnp.where(odd_row, next_row[...], pair_row[...])
    depth_last = lax.axis_index("depth") == lax.axis_size("depth") - 1
    z_open = jnp.where(depth_last, 0.0, TAU3).astype(F32)
    row_index = lax.broadcasted_iota(jnp.int32, (ROWS, COLS), 0)
    top, bottom = row_index == 0, row_index == ROWS - 1
    for plane in range(PLANES + 1):
        span = slice(plane * ROWS, (plane + 1) * ROWS)
        here = deep[span, :]
        above = jnp.where(top, low_row[plane : plane + 1, :], pltpu.roll(here, 1, 0))
        below = jnp.where(bottom, high_row[plane : plane + 1, :], pltpu.roll(here, ROWS - 1, 0))
        smooth[span, :] = 0.25 * (above + 2.0 * here + below)

    def resist(plane):
        return resistance(cells(smooth, plane + 1) - cells(smooth, plane))

    half = PLANES // 2
    one = jnp.ones((ROWS, COLS), F32)
    states = [
        (1.0 / resist(start), one, cells(vol, start + 1), one, cells(vol, start)) for start in (0, half)
    ]
    for step in range(1, half):
        final = step == half - 1
        for part in range(2):
            plane = part * half + step
            span = slice(plane * ROWS, (plane + 1) * ROWS)
            if final and part == 1:
                *state, saved = eliminate_last(*states[part], z_open / (TAU3 * resist(plane)))
            else:
                *state, saved = eliminate(*states[part], resist(plane))
            if not final:
                state[1] = state[1] + 1.0
                state[2] = state[2] + cells(vol, plane + 1)
            states[part] = state
            factor[span, :], back[span, :], rest[span, :] = saved
    joined, middle = join(*[(c, ng, fg, ns, fs) for c, fg, fs, ng, ns in states])
    for place, value in enumerate(joined):
        port[place] = value
    for place, value in enumerate(middle):
        mid[place] = value


def row_kernel(vol, deep, port, factor, back, rest):
    part = [strided(deep, row) for row in range(ROWS)]
    low_sum = 2.0 * part[0] + part[1]
    high_sum = part[ROWS - 2] + 2.0 * part[ROWS - 1]
    smooth = [None] + [0.25 * (part[r - 1] + 2.0 * part[r] + part[r + 1]) for r in range(1, ROWS - 1)]
    one = jnp.ones((PLANES, COLS), F32)
    state = (1.0 / resistance(smooth[2] - smooth[1]), one, strided(vol, 2), one, strided(vol, 1))
    for row in range(2, ROWS - 2):
        *state, saved = eliminate(*state, resistance(smooth[row + 1] - smooth[row]))
        state[1] = state[1] + 1.0
        state[2] = state[2] + strided(vol, row + 1)
        factor[row], back[row], rest[row] = saved
    coupling, far_ground, far_source, near_ground, near_source = state
    values = (
        coupling, near_ground, far_ground, near_source, far_source,
        part[0], part[ROWS - 1], low_sum, high_sum, smooth[1], smooth[ROWS - 2],
        strided(vol, 0), strided(vol, ROWS - 1),
    )
    for place, value in enumerate(values):
        port[pl.ds(place, PLANES, stride=PORT), :] = value
    for place in range(len(values), PORT):
        port[pl.ds(place, PLANES, stride=PORT), :] = jnp.zeros((PLANES, COLS), F32)


def chain_solve(coupling, near_ground, far_ground, near_source, far_source, count):
    size = coupling.shape[0]
    right = coupling
    ground = near_ground + pltpu.roll(far_ground, 1, 0)
    source = near_source + pltpu.roll(far_source, 1, 0)
    step = 1
    while step < count:
        left = pltpu.roll(right, step, 0)
        inverse = 1.0 / (ground + left + right)
        ground_part = ground * inverse
        source_part = source * inverse
        ground = (
            ground
            + left * pltpu.roll(ground_part, step, 0)
            + right * pltpu.roll(ground_part, size - step, 0)
        )
        source = (
            source
            + left * pltpu.roll(source_part, step, 0)
            + right * pltpu.roll(source_part, size - step, 0)
        )
        right = right * pltpu.roll(right * inverse, size - step, 0)
        step *= 2
    return source / ground


def column_kernel(vol, smooth, solved_x, turned, turned_smooth, factor, back, rest):
    for group in range(4):
        span = slice(group * COLS, (group + 1) * COLS)
        turned[span, :] = vol[span, :].T
        turned_smooth[span, :] = smooth[span, :].T

    def resist(step):
        if step < 15:
            return resistance(strided(turned_smooth, step + 1) - strided(turned_smooth, step))
        return resistance(pltpu.roll(strided(turned_smooth, 0), 31, 0) - strided(turned_smooth, 15))

    chunk_last = (lax.broadcasted_iota(jnp.int32, (32, COLS), 0) & 7) == 7
    one = jnp.ones((32, COLS), F32)
    state = (1.0 / resist(0), one, strided(turned, 1), one, strided(turned, 0))
    for step in range(1, 16):
        if step == 15:
            *state, saved = eliminate_last(*state, jnp.where(chunk_last, 0.0, 1.0 / resist(step)))
        else:
            *state, saved = eliminate(*state, resist(step))
            state[1] = state[1] + 1.0
            state[2] = state[2] + strided(turned, step + 1)
        factor[step], back[step], rest[step] = saved
    coupling, far_ground, far_source, near_ground, near_source = state
    first = chain_solve(coupling, near_ground, far_ground, near_source, far_source, 8)
    turned[pl.ds(0, 32, stride=16), :] = first
    value = pltpu.roll(first, 31, 0)
    for step in range(15, 0, -1):
        value = factor[step] * value + (back[step] * first + rest[step])
        turned[pl.ds(step, 32, stride=16), :] = value
    for group in range(4):
        span = slice(group * COLS, (group + 1) * COLS)
        solved_x[span, :] = turned[span, :].T


def row_reduced_kernel(ports, out):
    (
        coupling, near_ground, far_ground, near_source, far_source,
        low, high, low_sum, high_sum, low_smooth, high_smooth, low_cell, high_cell,
    ) = (ports[pl.ds(place, BLOCKS, stride=PORT), :] for place in range(13))
    block = lax.broadcasted_iota(jnp.int32, (BLOCKS, COLS), 0)
    block_first, block_last = block == 0, block == BLOCKS - 1
    low_end = 0.25 * (jnp.where(block_first, 0.0, pltpu.roll(high, 1, 0)) + low_sum)
    high_end = 0.25 * (high_sum + jnp.where(block_last, 0.0, pltpu.roll(low, BLOCKS - 1, 0)))
    enter = 1.0 / resistance(low_smooth - low_end)
    leave = 1.0 / resistance(high_end - high_smooth)
    across = pltpu.roll(low_end, BLOCKS - 1, 0) - high_end
    across = jnp.where(block_last, 0.0, 1.0 / resistance(across))
    zero = jnp.zeros_like(coupling)
    one = jnp.ones_like(coupling)
    before, at_low = join(
        (enter, one, zero, low_cell, zero), (coupling, near_ground, far_ground, near_source, far_source)
    )
    after, at_high = join((leave, zero, one, zero, high_cell), (across, zero, zero, zero, zero))
    whole, between = join(before, after)
    first = chain_solve(*whole, BLOCKS)
    later = pltpu.roll(first, BLOCKS - 1, 0)

    def middle(weights, left, right):
        return weights[0] * left + weights[1] * right + weights[2]

    inner_high = middle(between, first, later)
    out[:, 0, :] = first
    out[:, 1, :] = middle(at_low, first, inner_high)
    out[:, 2, :] = inner_high
    out[:, 3, :] = middle(at_high, inner_high, later)


def pick(flag, there, here):
    return tuple(jnp.where(flag, a, b) for a, b in zip(there, here))


def join_kernel(bit, own, other, out):
    upper = (lax.axis_index("depth") & bit) != 0
    mine = tuple(own[place] for place in range(5))
    theirs = tuple(other[place] for place in range(5))
    port, _ = join(pick(upper, theirs, mine), pick(upper, mine, theirs))
    for place, value in enumerate(port):
        out[place] = value


def finish_plane_kernel(
    own, near, across, beside, factor, back, rest, mid, solved_x, out,
):
    index = lax.axis_index("depth")
    odd = (index & 2) != 0
    crossed = tuple(across[place] for place in range(5))
    straight = tuple(beside[place] for place in range(5, 10))
    quad, _ = join(pick(odd, crossed, straight), pick(odd, straight, crossed))
    zero = jnp.zeros((ROWS, COLS), F32)
    left_ground, left_source, right_ground, right_source = zero, zero, zero, zero
    for bit, ref in ((4, quad), (2, beside), (1, near)):
        on_left = (index & bit) != 0
        c, ng, fg, ns, fs = (ref[place] for place in range(5))
        ground, source = ng + left_ground, ns + left_source
        share = c / (c + ground)
        left_ground = jnp.where(on_left, fg + share * ground, left_ground)
        left_source = jnp.where(on_left, fs + share * source, left_source)
        ground, source = fg + right_ground, fs + right_source
        total = c + ground
        share = jnp.where(total > 0.0, c / jnp.where(total > 0.0, total, 1.0), 0.0)
        right_ground = jnp.where(on_left, right_ground, ng + share * ground)
        right_source = jnp.where(on_left, right_source, ns + share * source)
    c, ng, fg, ns, fs = (own[place] for place in range(5))
    ground, source = fg + right_ground, fs + right_source
    total = c + ground
    inverse = jnp.where(total > 0.0, 1.0 / jnp.where(total > 0.0, total, 1.0), 0.0)
    share = c * inverse
    first = (left_source + ns + share * source) / (left_ground + ng + share * ground)
    after = share * first + source * inverse
    middle = mid[0] * first + mid[1] * after + mid[2]
    half = PLANES // 2
    for start, near_value, far_value in ((0, first, middle), (half, middle, after)):
        value = far_value
        for plane in range(start + half - 1, start, -1):
            span = slice(plane * ROWS, (plane + 1) * ROWS)
            value = factor[span, :] * value + (back[span, :] * near_value + rest[span, :])
            out[span, :] = solved_x[span, :] + value
        span = slice(start * ROWS, (start + 1) * ROWS)
        out[span, :] = solved_x[span, :] + near_value


def finish_row_kernel(ends, factor, back, rest, others, out):
    third = 1.0 / 3.0

    def put(row, value):
        place = pl.ds(row, PLANES, stride=ROWS)
        out[place, :] = (others[place, :] + value) * third

    for place, row in ((0, 0), (1, 1), (2, ROWS - 2), (3, ROWS - 1)):
        put(row, ends[:, place, :])
    first = ends[:, 1, :]
    value = ends[:, 2, :]
    for row in range(ROWS - 3, 1, -1):
        value = factor[row] * value + (back[row] * first + rest[row])
        put(row, value)


def call(kernel, outs, scratch=(), flops=1000000, moved=500000, **options):
    return pl.pallas_call(
        kernel,
        out_shape=outs,
        scratch_shapes=scratch,
        compiler_params=pltpu.CompilerParams(vmem_limit_bytes=16 * 1024 * 1024),
        cost_estimate=pl.CostEstimate(flops=flops, bytes_accessed=moved, transcendentals=0),
        **options,
    )


def shaped(*shape):
    return jax.ShapeDtypeStruct(shape, F32)


def line_perm(axis, step):
    count = lax.axis_size(axis)
    if step > 0:
        return [(i, i + 1) for i in range(count - 1)]
    return [(i + 1, i) for i in range(count - 1)]


def swap_perm(axis, bit):
    return [(i, i ^ bit) for i in range(lax.axis_size(axis))]


def next_perm(axis):
    pairs = []
    for i in range(1, lax.axis_size(axis) - 1, 2):
        pairs += [(i, i + 1), (i + 1, i)]
    return pairs


def shards(volume):
    flat = volume.reshape(PLANES * ROWS, COLS)
    lines = shaped(ROWS, PLANES, COLS)
    whole = shaped(PLANES * ROWS, COLS)
    tall = shaped((PLANES + 1) * ROWS, COLS)
    port = shaped(5, ROWS, COLS)
    side = shaped(PLANES + 1, COLS)
    to_near, to_far = call(
        edge_kernel,
        (shaped(2 * ROWS, COLS), shaped(2 * ROWS, COLS)),
        (pltpu.SemaphoreType.DMA((2,)),),
        in_specs=[pl.BlockSpec(memory_space=pl.ANY)],
    )(flat)
    far_side = lax.ppermute(to_far, "depth", next_perm("depth"))
    near_side = lax.ppermute(to_near, "depth", swap_perm("depth", 1))
    deep, to_pair, to_next = call(
        deep_kernel, (tall, side, side), (pltpu.VMEM((PLANES + 3, ROWS, COLS), F32),)
    )(flat, near_side, far_side)
    next_row = lax.ppermute(to_next, "lat", next_perm("lat"))
    pair_row = lax.ppermute(to_pair, "lat", swap_perm("lat", 1))
    y_port, y_factor, y_back, y_rest = call(row_kernel, (shaped(PLANES * PORT, COLS), lines, lines, lines))(
        flat, deep
    )
    ports = lax.all_to_all(y_port, "lat", 0, 0, tiled=True)
    z_port, z_factor, z_back, z_rest, z_mid, smooth = call(
        plane_kernel, (port, whole, whole, whole, shaped(3, ROWS, COLS), tall), flops=LONG
    )(flat, deep, pair_row, next_row)
    near = lax.ppermute(z_port, "depth", swap_perm("depth", 1))
    solved_x = call(
        column_kernel,
        whole,
        (
            pltpu.VMEM((512, COLS), F32),
            pltpu.VMEM((512, COLS), F32),
            pltpu.VMEM((16, 32, COLS), F32),
            pltpu.VMEM((16, 32, COLS), F32),
            pltpu.VMEM((16, 32, COLS), F32),
        ),
    )(flat, smooth)
    pair_own = call(lambda *refs: join_kernel(1, *refs), port)(z_port, near)
    across = lax.ppermute(pair_own, "depth", swap_perm("depth", 6))
    both = jnp.concatenate([pair_own, across], axis=0)
    ports, both, solved_x = lax.optimization_barrier((ports, both, solved_x))
    ends = call(row_reduced_kernel, shaped(BLOCKS, 4, COLS))(ports)
    ends, both = lax.optimization_barrier((ends, both))
    beside = lax.ppermute(both, "depth", swap_perm("depth", 2))
    others = call(finish_plane_kernel, whole)(
        z_port, near, across, beside, z_factor, z_back, z_rest, z_mid, solved_x
    )
    ends_y = lax.all_to_all(ends, "lat", 0, 0, tiled=True)
    out = call(finish_row_kernel, whole)(ends_y, y_factor, y_back, y_rest, others)
    return out.reshape(PLANES, ROWS, COLS)


def solution(mesh):
    placed = (P("depth", "lat", None),)
    return jax.shard_map(
        shards, mesh=mesh, in_specs=placed, out_specs=P("depth", "lat", None), check_vma=False
    )
```

```python
import jax
import jax.numpy as jnp
from jax import lax
from jax.experimental import pallas as pl
from jax.experimental.pallas import tpu as pltpu
from jax.sharding import PartitionSpec as P

TAU3 = 900.0
INV_LAMBDA_SQ = 4.0
PLANES = 32
ROWS = 16
COLS = 128
BLOCKS = 32
PORT = 8
GATHER = 256
F32 = jnp.float32


def resistance(diff):
    return (1.0 + INV_LAMBDA_SQ * (diff * diff)) * (1.0 / TAU3)


def smooth_lanes(field, first, last):
    before = jnp.where(first, 0.0, pltpu.roll(field, 1, field.ndim - 1))
    after = jnp.where(last, 0.0, pltpu.roll(field, COLS - 1, field.ndim - 1))
    return 0.25 * (before + 2.0 * field + after)


def eliminate(coupling, ground, source, near_ground, near_source, resist):
    factor = 1.0 / (1.0 + (coupling + ground) * resist)
    weight = factor * resist
    back = coupling * weight
    near_ground = near_ground + back * ground
    near_source = near_source + back * source
    saved = (factor, back, source * weight)
    return coupling * factor, ground * factor, source * factor, near_ground, near_source, saved


def eliminate_last(coupling, ground, source, near_ground, near_source, conduct):
    inverse = 1.0 / (coupling + ground + conduct)
    factor = conduct * inverse
    back = coupling * inverse
    near_ground = near_ground + back * ground
    near_source = near_source + back * source
    saved = (factor, back, source * inverse)
    return coupling * factor, ground * factor, source * factor, near_ground, near_source, saved


def join(left, right):
    lc, lg, lh, ls, lt = left
    rc, rg, rh, rs, rt = right
    ground = lh + rg
    source = lt + rs
    inverse = 1.0 / (lc + rc + ground)
    to_left = lc * inverse
    to_right = rc * inverse
    return (
        lc * to_right,
        lg + to_left * ground,
        rh + to_right * ground,
        ls + to_left * source,
        rt + to_right * source,
    ), (to_left, to_right, source * inverse)


def edge_kernel(vol, near_side, far_side, sems):
    odd = lax.axis_index("depth") & 1
    high = (PLANES - 2) * ROWS
    near_start = pl.multiple_of((1 - odd) * high, ROWS)
    far_start = pl.multiple_of(odd * high, ROWS)
    copies = (
        pltpu.make_async_copy(vol.at[pl.ds(near_start, 2 * ROWS), :], near_side, sems.at[0]),
        pltpu.make_async_copy(vol.at[pl.ds(far_start, 2 * ROWS), :], far_side, sems.at[1]),
    )
    for copy in copies:
        copy.start()
    for copy in copies:
        copy.wait()


def strided(ref, row):
    return ref[pl.ds(row, 32, stride=16), :]


def cells(ref, plane):
    return ref[plane * ROWS : (plane + 1) * ROWS, :]


def deep_kernel(vol, near_side, far_side, deep, pair_row, next_row, mixed):
    odd = (lax.axis_index("depth") & 1) == 1
    lane = lax.broadcasted_iota(jnp.int32, (ROWS, COLS), 1)
    first, last = lane == 0, lane == COLS - 1
    mixed[0] = smooth_lanes(jnp.where(odd, cells(near_side, 1), cells(far_side, 1)), first, last)
    for plane in range(PLANES):
        mixed[plane + 1] = smooth_lanes(cells(vol, plane), first, last)
    for plane in range(2):
        mixed[PLANES + 1 + plane] = smooth_lanes(
            jnp.where(odd, cells(far_side, plane), cells(near_side, plane)), first, last
        )
    for plane in range(PLANES + 1):
        deep[plane * ROWS : (plane + 1) * ROWS, :] = 0.25 * (
            mixed[plane] + 2.0 * mixed[plane + 1] + mixed[plane + 2]
        )
    odd_row = (lax.axis_index("lat") & 1) == 1
    low = deep[pl.ds(0, PLANES + 1, stride=ROWS), :]
    high = deep[pl.ds(ROWS - 1, PLANES + 1, stride=ROWS), :]
    pair_row[...] = jnp.where(odd_row, low, high)
    next_row[...] = jnp.where(odd_row, high, low)


def plane_kernel(vol, deep, pair_row, next_row, port, factor, back, rest, mid, smooth):
    odd_row = (lax.axis_index("lat") & 1) == 1
    low_row = jnp.where(odd_row, pair_row[...], next_row[...])
    high_row = jnp.where(odd_row, next_row[...], pair_row[...])
    depth_last = lax.axis_index("depth") == lax.axis_size("depth") - 1
    z_open = jnp.where(depth_last, 0.0, TAU3).astype(F32)
    row_index = lax.broadcasted_iota(jnp.int32, (ROWS, COLS), 0)
    top, bottom = row_index == 0, row_index == ROWS - 1
    for plane in range(PLANES + 1):
        span = slice(plane * ROWS, (plane + 1) * ROWS)
        here = deep[span, :]
        above = jnp.where(top, low_row[plane : plane + 1, :], pltpu.roll(here, 1, 0))
        below = jnp.where(bottom, high_row[plane : plane + 1, :], pltpu.roll(here, ROWS - 1, 0))
        smooth[span, :] = 0.25 * (above + 2.0 * here + below)

    def resist(plane):
        return resistance(cells(smooth, plane + 1) - cells(smooth, plane))

    half = PLANES // 2
    one = jnp.ones((ROWS, COLS), F32)
    states = [
        (1.0 / resist(start), one, cells(vol, start + 1), one, cells(vol, start)) for start in (0, half)
    ]
    for step in range(1, half):
        final = step == half - 1
        for part in range(2):
            plane = part * half + step
            span = slice(plane * ROWS, (plane + 1) * ROWS)
            if final and part == 1:
                *state, saved = eliminate_last(*states[part], z_open / (TAU3 * resist(plane)))
            else:
                *state, saved = eliminate(*states[part], resist(plane))
            if not final:
                state[1] = state[1] + 1.0
                state[2] = state[2] + cells(vol, plane + 1)
            states[part] = state
            factor[span, :], back[span, :], rest[span, :] = saved
    joined, middle = join(*[(c, ng, fg, ns, fs) for c, fg, fs, ng, ns in states])
    for place, value in enumerate(joined):
        port[place * ROWS : (place + 1) * ROWS, :] = value
    port[5 * ROWS :, :] = jnp.zeros((GATHER - 5 * ROWS, COLS), F32)
    for place, value in enumerate(middle):
        mid[place] = value


def row_kernel(vol, smooth, port, factor, back, rest):
    def resist(row):
        return resistance(strided(smooth, row + 1) - strided(smooth, row))

    one = jnp.ones((PLANES, COLS), F32)
    state = (1.0 / resist(0), one, strided(vol, 1), one, strided(vol, 0))
    for row in range(1, ROWS - 1):
        *state, saved = eliminate(*state, resist(row))
        state[1] = state[1] + 1.0
        state[2] = state[2] + strided(vol, row + 1)
        factor[row], back[row], rest[row] = saved
    coupling, far_ground, far_source, near_ground, near_source = state
    values = (
        coupling, near_ground, far_ground, near_source, far_source,
        strided(smooth, 0), strided(smooth, ROWS - 1), jnp.zeros((PLANES, COLS), F32),
    )
    for place, value in enumerate(values):
        port[pl.ds(place, PLANES, stride=PORT), :] = value


def chain_solve(coupling, near_ground, far_ground, near_source, far_source, count):
    size = coupling.shape[0]
    right = coupling
    ground = near_ground + pltpu.roll(far_ground, 1, 0)
    source = near_source + pltpu.roll(far_source, 1, 0)
    step = 1
    while step < count:
        left = pltpu.roll(right, step, 0)
        inverse = 1.0 / (ground + left + right)
        ground_part = ground * inverse
        source_part = source * inverse
        ground = (
            ground
            + left * pltpu.roll(ground_part, step, 0)
            + right * pltpu.roll(ground_part, size - step, 0)
        )
        source = (
            source
            + left * pltpu.roll(source_part, step, 0)
            + right * pltpu.roll(source_part, size - step, 0)
        )
        right = right * pltpu.roll(right * inverse, size - step, 0)
        step *= 2
    return source / ground


def column_kernel(vol, smooth, solved_x, turned, turned_smooth, factor, back, rest):
    for group in range(4):
        span = slice(group * COLS, (group + 1) * COLS)
        turned[span, :] = vol[span, :].T
        turned_smooth[span, :] = smooth[span, :].T

    def resist(step):
        if step < 15:
            return resistance(strided(turned_smooth, step + 1) - strided(turned_smooth, step))
        return resistance(pltpu.roll(strided(turned_smooth, 0), 31, 0) - strided(turned_smooth, 15))

    chunk_last = (lax.broadcasted_iota(jnp.int32, (32, COLS), 0) & 7) == 7
    one = jnp.ones((32, COLS), F32)
    state = (1.0 / resist(0), one, strided(turned, 1), one, strided(turned, 0))
    for step in range(1, 16):
        if step == 15:
            *state, saved = eliminate_last(*state, jnp.where(chunk_last, 0.0, 1.0 / resist(step)))
        else:
            *state, saved = eliminate(*state, resist(step))
            state[1] = state[1] + 1.0
            state[2] = state[2] + strided(turned, step + 1)
        factor[step], back[step], rest[step] = saved
    coupling, far_ground, far_source, near_ground, near_source = state
    first = chain_solve(coupling, near_ground, far_ground, near_source, far_source, 8)
    turned[pl.ds(0, 32, stride=16), :] = first
    value = pltpu.roll(first, 31, 0)
    for step in range(15, 0, -1):
        value = factor[step] * value + (back[step] * first + rest[step])
        turned[pl.ds(step, 32, stride=16), :] = value
    for group in range(4):
        span = slice(group * COLS, (group + 1) * COLS)
        solved_x[span, :] = turned[span, :].T


def row_reduced_kernel(ports, out):
    coupling, near_ground, far_ground, near_source, far_source, low, high = (
        ports[pl.ds(place, BLOCKS, stride=PORT), :] for place in range(7)
    )
    block_last = lax.broadcasted_iota(jnp.int32, (BLOCKS, COLS), 0) == BLOCKS - 1
    across = pltpu.roll(low, BLOCKS - 1, 0) - high
    across = jnp.where(block_last, 0.0, 1.0 / resistance(across))
    zero = jnp.zeros_like(coupling)
    whole, at_high = join(
        (coupling, near_ground, far_ground, near_source, far_source), (across, zero, zero, zero, zero)
    )
    first = chain_solve(*whole, BLOCKS)
    out[:, 0, :] = first
    out[:, 1, :] = at_high[0] * first + at_high[1] * pltpu.roll(first, BLOCKS - 1, 0) + at_high[2]


def finish_plane_kernel(own, gathered, factor, back, rest, mid, others, out, ports, sem):
    copy = pltpu.make_async_copy(gathered.at[:, pl.ds(0, 5 * ROWS), :], ports, sem)
    copy.start()
    copy.wait()

    def port(block):
        return [ports[block, place * ROWS : (place + 1) * ROWS, :] for place in range(5)]

    index = lax.axis_index("depth")
    count = lax.axis_size("depth")
    zero = jnp.zeros((ROWS, COLS), F32)
    left_ground, left_source = zero, zero
    for block in range(count - 1):
        c, ng, fg, ns, fs = port(block)
        ground, source = ng + left_ground, ns + left_source
        share = c / (c + ground)
        left_ground = jnp.where(block < index, fg + share * ground, left_ground)
        left_source = jnp.where(block < index, fs + share * source, left_source)
    c, ng, fg, ns, fs = port(count - 1)
    right_ground = jnp.where(index < count - 1, ng, zero)
    right_source = jnp.where(index < count - 1, ns, zero)
    for block in range(count - 2, 0, -1):
        c, ng, fg, ns, fs = port(block)
        ground, source = fg + right_ground, fs + right_source
        share = c / (c + ground)
        right_ground = jnp.where(block > index, ng + share * ground, right_ground)
        right_source = jnp.where(block > index, ns + share * source, right_source)
    c, ng, fg, ns, fs = [own[place * ROWS : (place + 1) * ROWS, :] for place in range(5)]
    ground, source = fg + right_ground, fs + right_source
    total = c + ground
    inverse = jnp.where(total > 0.0, 1.0 / jnp.where(total > 0.0, total, 1.0), 0.0)
    share = c * inverse
    first = (left_source + ns + share * source) / (left_ground + ng + share * ground)
    after = share * first + source * inverse
    middle = mid[0] * first + mid[1] * after + mid[2]
    half = PLANES // 2
    third = 1.0 / 3.0
    for start, near_value, far_value in ((0, first, middle), (half, middle, after)):
        value = far_value
        for plane in range(start + half - 1, start, -1):
            span = slice(plane * ROWS, (plane + 1) * ROWS)
            value = factor[span, :] * value + (back[span, :] * near_value + rest[span, :])
            out[span, :] = (others[span, :] + value) * third
        span = slice(start * ROWS, (start + 1) * ROWS)
        out[span, :] = (others[span, :] + near_value) * third


def finish_row_kernel(ends, factor, back, rest, solved_x, out):
    def put(row, value):
        place = pl.ds(row, PLANES, stride=ROWS)
        out[place, :] = solved_x[place, :] + value

    first = ends[:, 0, :]
    value = ends[:, 1, :]
    put(0, first)
    put(ROWS - 1, value)
    for row in range(ROWS - 2, 0, -1):
        value = factor[row] * value + (back[row] * first + rest[row])
        put(row, value)


def call(kernel, outs, scratch=(), flops=1000000, moved=500000, **options):
    return pl.pallas_call(
        kernel,
        out_shape=outs,
        scratch_shapes=scratch,
        compiler_params=pltpu.CompilerParams(vmem_limit_bytes=16 * 1024 * 1024),
        cost_estimate=pl.CostEstimate(flops=flops, bytes_accessed=moved, transcendentals=0),
        **options,
    )


def shaped(*shape):
    return jax.ShapeDtypeStruct(shape, F32)


def line_perm(axis, step):
    count = lax.axis_size(axis)
    if step > 0:
        return [(i, i + 1) for i in range(count - 1)]
    return [(i + 1, i) for i in range(count - 1)]


def swap_perm(axis, bit):
    return [(i, i ^ bit) for i in range(lax.axis_size(axis))]


def next_perm(axis):
    pairs = []
    for i in range(1, lax.axis_size(axis) - 1, 2):
        pairs += [(i, i + 1), (i + 1, i)]
    return pairs


def shards(volume):
    flat = volume.reshape(PLANES * ROWS, COLS)
    lines = shaped(ROWS, PLANES, COLS)
    whole = shaped(PLANES * ROWS, COLS)
    tall = shaped((PLANES + 1) * ROWS, COLS)
    side = shaped(PLANES + 1, COLS)
    to_near, to_far = call(
        edge_kernel,
        (shaped(2 * ROWS, COLS), shaped(2 * ROWS, COLS)),
        (pltpu.SemaphoreType.DMA((2,)),),
        in_specs=[pl.BlockSpec(memory_space=pl.ANY)],
    )(flat)
    far_side = lax.ppermute(to_far, "depth", next_perm("depth"))
    near_side = lax.ppermute(to_near, "depth", swap_perm("depth", 1))
    deep, to_pair, to_next = call(
        deep_kernel, (tall, side, side), (pltpu.VMEM((PLANES + 3, ROWS, COLS), F32),)
    )(flat, near_side, far_side)
    next_row = lax.ppermute(to_next, "lat", next_perm("lat"))
    pair_row = lax.ppermute(to_pair, "lat", swap_perm("lat", 1))
    z_port, z_factor, z_back, z_rest, z_mid, smooth = call(
        plane_kernel, (shaped(GATHER, COLS), whole, whole, whole, shaped(3, ROWS, COLS), tall)
    )(flat, deep, pair_row, next_row)
    gathered = lax.all_gather(z_port, "depth", axis=0, tiled=True)
    y_port, y_factor, y_back, y_rest = call(row_kernel, (shaped(PLANES * PORT, COLS), lines, lines, lines))(
        flat, smooth
    )
    ports = lax.all_to_all(y_port, "lat", 0, 0, tiled=True)
    ends = call(row_reduced_kernel, shaped(BLOCKS, 2, COLS))(ports)
    ends = lax.all_to_all(ends, "lat", 0, 0, tiled=True)
    ends, smooth_later = lax.optimization_barrier((ends, smooth))
    solved_x = call(
        column_kernel,
        whole,
        (
            pltpu.VMEM((512, COLS), F32),
            pltpu.VMEM((512, COLS), F32),
            pltpu.VMEM((16, 32, COLS), F32),
            pltpu.VMEM((16, 32, COLS), F32),
            pltpu.VMEM((16, 32, COLS), F32),
        ),
    )(flat, smooth_later)
    others = call(finish_row_kernel, whole)(ends, y_factor, y_back, y_rest, solved_x)
    spec = pl.BlockSpec(memory_space=pltpu.VMEM)
    blocks = lax.axis_size("depth")
    out = call(
        finish_plane_kernel,
        whole,
        (pltpu.VMEM((blocks, 5 * ROWS, COLS), F32), pltpu.SemaphoreType.DMA),
        in_specs=[spec, pl.BlockSpec(memory_space=pl.ANY)] + [spec] * 5,
    )(z_port, gathered.reshape(blocks, GATHER, COLS), z_factor, z_back, z_rest, z_mid, others)
    return out.reshape(PLANES, ROWS, COLS)


def solution(mesh):
    placed = (P("depth", "lat", None),)
    return jax.shard_map(
        shards, mesh=mesh, in_specs=placed, out_specs=P("depth", "lat", None), check_vma=False
    )
```

```python
import jax
import jax.numpy as jnp
from jax import lax
from jax.experimental import pallas as pl
from jax.experimental.pallas import tpu as pltpu
from jax.sharding import PartitionSpec as P

TAU3 = 900.0
INV_LAMBDA_SQ = 4.0
PLANES = 32
ROWS = 16
COLS = 128
BLOCKS = 32
PORT = 16
LONG = 100_000_000_000
F32 = jnp.float32


def resistance(diff):
    return (1.0 + INV_LAMBDA_SQ * (diff * diff)) * (1.0 / TAU3)


def smooth_lanes(field, first, last):
    before = jnp.where(first, 0.0, pltpu.roll(field, 1, field.ndim - 1))
    after = jnp.where(last, 0.0, pltpu.roll(field, COLS - 1, field.ndim - 1))
    return 0.25 * (before + 2.0 * field + after)


def eliminate(coupling, ground, source, near_ground, near_source, resist):
    factor = 1.0 / (1.0 + (coupling + ground) * resist)
    weight = factor * resist
    back = coupling * weight
    near_ground = near_ground + back * ground
    near_source = near_source + back * source
    saved = (factor, back, source * weight)
    return coupling * factor, ground * factor, source * factor, near_ground, near_source, saved


def eliminate_last(coupling, ground, source, near_ground, near_source, conduct):
    inverse = 1.0 / (coupling + ground + conduct)
    factor = conduct * inverse
    back = coupling * inverse
    near_ground = near_ground + back * ground
    near_source = near_source + back * source
    saved = (factor, back, source * inverse)
    return coupling * factor, ground * factor, source * factor, near_ground, near_source, saved


def join(left, right):
    lc, lg, lh, ls, lt = left
    rc, rg, rh, rs, rt = right
    ground = lh + rg
    source = lt + rs
    inverse = 1.0 / (lc + rc + ground)
    to_left = lc * inverse
    to_right = rc * inverse
    return (
        lc * to_right,
        lg + to_left * ground,
        rh + to_right * ground,
        ls + to_left * source,
        rt + to_right * source,
    ), (to_left, to_right, source * inverse)


def edge_kernel(vol, near_side, far_side, sems):
    odd = lax.axis_index("depth") & 1
    high = (PLANES - 2) * ROWS
    near_start = pl.multiple_of((1 - odd) * high, ROWS)
    far_start = pl.multiple_of(odd * high, ROWS)
    copies = (
        pltpu.make_async_copy(vol.at[pl.ds(near_start, 2 * ROWS), :], near_side, sems.at[0]),
        pltpu.make_async_copy(vol.at[pl.ds(far_start, 2 * ROWS), :], far_side, sems.at[1]),
    )
    for copy in copies:
        copy.start()
    for copy in copies:
        copy.wait()


def strided(ref, row):
    return ref[pl.ds(row, 32, stride=16), :]


def cells(ref, plane):
    return ref[plane * ROWS : (plane + 1) * ROWS, :]


def faces(near_side, far_side):
    odd = (lax.axis_index("depth") & 1) == 1
    near, far = near_side[...], far_side[...]
    return jnp.where(odd, near, far)[ROWS:, :], jnp.where(odd, far, near)


def side_kernel(vol, near_side, far_side, pair_row, next_row, low_side, high_side):
    odd_row = (lax.axis_index("lat") & 1) == 1
    below, above = faces(near_side, far_side)
    lane = lax.broadcasted_iota(jnp.int32, (PLANES + 3, COLS), 1)
    sides = []
    for row, ref in ((0, low_side), (ROWS - 1, high_side)):
        ref[0:1, :] = below[row : row + 1, :]
        ref[1 : PLANES + 1, :] = vol[pl.ds(row, PLANES, stride=ROWS), :]
        ref[PLANES + 1 : PLANES + 2, :] = above[row : row + 1, :]
        ref[PLANES + 2 : PLANES + 3, :] = above[ROWS + row : ROWS + row + 1, :]
        ref[0 : PLANES + 3, :] = smooth_lanes(ref[0 : PLANES + 3, :], lane == 0, lane == COLS - 1)
        sides.append(
            0.25 * (ref[0 : PLANES + 1, :] + 2.0 * ref[1 : PLANES + 2, :] + ref[2 : PLANES + 3, :])
        )
    pair_row[...] = jnp.where(odd_row, sides[0], sides[1])
    next_row[...] = jnp.where(odd_row, sides[1], sides[0])


def plane_kernel(vol, deep, pair_row, next_row, port, factor, back, rest, mid, smooth):
    odd_row = (lax.axis_index("lat") & 1) == 1
    low_row = jnp.where(odd_row, pair_row[...], next_row[...])
    high_row = jnp.where(odd_row, next_row[...], pair_row[...])
    depth_last = lax.axis_index("depth") == lax.axis_size("depth") - 1
    z_open = jnp.where(depth_last, 0.0, TAU3).astype(F32)
    row_index = lax.broadcasted_iota(jnp.int32, (ROWS, COLS), 0)
    top, bottom = row_index == 0, row_index == ROWS - 1
    for plane in range(PLANES + 1):
        span = slice(plane * ROWS, (plane + 1) * ROWS)
        here = deep[span, :]
        above = jnp.where(top, low_row[plane : plane + 1, :], pltpu.roll(here, 1, 0))
        below = jnp.where(bottom, high_row[plane : plane + 1, :], pltpu.roll(here, ROWS - 1, 0))
        smooth[span, :] = 0.25 * (above + 2.0 * here + below)

    def resist(plane):
        return resistance(cells(smooth, plane + 1) - cells(smooth, plane))

    half = PLANES // 2
    one = jnp.ones((ROWS, COLS), F32)
    states = [
        (1.0 / resist(start), one, cells(vol, start + 1), one, cells(vol, start)) for start in (0, half)
    ]
    for step in range(1, half):
        final = step == half - 1
        for part in range(2):
            plane = part * half + step
            span = slice(plane * ROWS, (plane + 1) * ROWS)
            if final and part == 1:
                *state, saved = eliminate_last(*states[part], z_open / (TAU3 * resist(plane)))
            else:
                *state, saved = eliminate(*states[part], resist(plane))
            if not final:
                state[1] = state[1] + 1.0
                state[2] = state[2] + cells(vol, plane + 1)
            states[part] = state
            factor[span, :], back[span, :], rest[span, :] = saved
    joined, middle = join(*[(c, ng, fg, ns, fs) for c, fg, fs, ng, ns in states])
    for place, value in enumerate(joined):
        port[place] = value
    for place, value in enumerate(middle):
        mid[place] = value


def row_kernel(vol, near_side, far_side, port, factor, back, rest, inner, deep, mixed):
    below, above = faces(near_side, far_side)
    lane = lax.broadcasted_iota(jnp.int32, (ROWS, COLS), 1)
    first, last = lane == 0, lane == COLS - 1
    mixed[0] = smooth_lanes(below, first, last)
    for plane in range(PLANES):
        mixed[plane + 1] = smooth_lanes(cells(vol, plane), first, last)
    for plane in range(2):
        mixed[PLANES + 1 + plane] = smooth_lanes(above[plane * ROWS : (plane + 1) * ROWS, :], first, last)
    for plane in range(PLANES + 1):
        deep[plane * ROWS : (plane + 1) * ROWS, :] = 0.25 * (
            mixed[plane] + 2.0 * mixed[plane + 1] + mixed[plane + 2]
        )
    part = [strided(deep, row) for row in range(ROWS)]
    low_sum = 2.0 * part[0] + part[1]
    high_sum = part[ROWS - 2] + 2.0 * part[ROWS - 1]
    smooth = [None] + [0.25 * (part[r - 1] + 2.0 * part[r] + part[r + 1]) for r in range(1, ROWS - 1)]
    one = jnp.ones((PLANES, COLS), F32)
    state = (1.0 / resistance(smooth[2] - smooth[1]), one, strided(vol, 2), one, strided(vol, 1))
    for row in range(2, ROWS - 2):
        *state, saved = eliminate(*state, resistance(smooth[row + 1] - smooth[row]))
        state[1] = state[1] + 1.0
        state[2] = state[2] + strided(vol, row + 1)
        factor[row], back[row], rest[row] = saved
    coupling, far_ground, far_source, near_ground, near_source = state
    values = (
        coupling, near_ground, far_ground, near_source, far_source,
        part[0], part[ROWS - 1], low_sum, high_sum, smooth[1], smooth[ROWS - 2],
        strided(vol, 0), strided(vol, ROWS - 1),
    )
    for place, value in enumerate(values):
        port[pl.ds(place, PLANES, stride=PORT), :] = value
    for place in range(5):
        inner[place] = values[place]
    for place in range(len(values), PORT):
        port[pl.ds(place, PLANES, stride=PORT), :] = jnp.zeros((PLANES, COLS), F32)


def chain_solve(coupling, near_ground, far_ground, near_source, far_source, count):
    size = coupling.shape[0]
    right = coupling
    ground = near_ground + pltpu.roll(far_ground, 1, 0)
    source = near_source + pltpu.roll(far_source, 1, 0)
    step = 1
    while step < count:
        left = pltpu.roll(right, step, 0)
        inverse = 1.0 / (ground + left + right)
        ground_part = ground * inverse
        source_part = source * inverse
        ground = (
            ground
            + left * pltpu.roll(ground_part, step, 0)
            + right * pltpu.roll(ground_part, size - step, 0)
        )
        source = (
            source
            + left * pltpu.roll(source_part, step, 0)
            + right * pltpu.roll(source_part, size - step, 0)
        )
        right = right * pltpu.roll(right * inverse, size - step, 0)
        step *= 2
    return source / ground


def column_kernel(vol, smooth, solved_x, turned, turned_smooth, factor, back, rest):
    for group in range(4):
        span = slice(group * COLS, (group + 1) * COLS)
        turned[span, :] = vol[span, :].T
        turned_smooth[span, :] = smooth[span, :].T

    def resist(step):
        if step < 15:
            return resistance(strided(turned_smooth, step + 1) - strided(turned_smooth, step))
        return resistance(pltpu.roll(strided(turned_smooth, 0), 31, 0) - strided(turned_smooth, 15))

    chunk_last = (lax.broadcasted_iota(jnp.int32, (32, COLS), 0) & 7) == 7
    one = jnp.ones((32, COLS), F32)
    state = (1.0 / resist(0), one, strided(turned, 1), one, strided(turned, 0))
    for step in range(1, 16):
        if step == 15:
            *state, saved = eliminate_last(*state, jnp.where(chunk_last, 0.0, 1.0 / resist(step)))
        else:
            *state, saved = eliminate(*state, resist(step))
            state[1] = state[1] + 1.0
            state[2] = state[2] + strided(turned, step + 1)
        factor[step], back[step], rest[step] = saved
    coupling, far_ground, far_source, near_ground, near_source = state
    first = chain_solve(coupling, near_ground, far_ground, near_source, far_source, 8)
    turned[pl.ds(0, 32, stride=16), :] = first
    value = pltpu.roll(first, 31, 0)
    for step in range(15, 0, -1):
        value = factor[step] * value + (back[step] * first + rest[step])
        turned[pl.ds(step, 32, stride=16), :] = value
    for group in range(4):
        span = slice(group * COLS, (group + 1) * COLS)
        solved_x[span, :] = turned[span, :].T


def row_reduced_kernel(ports, out):
    (
        coupling, near_ground, far_ground, near_source, far_source,
        low, high, low_sum, high_sum, low_smooth, high_smooth, low_cell, high_cell,
    ) = (ports[pl.ds(place, BLOCKS, stride=PORT), :] for place in range(13))
    block = lax.broadcasted_iota(jnp.int32, (BLOCKS, COLS), 0)
    block_first, block_last = block == 0, block == BLOCKS - 1
    low_end = 0.25 * (jnp.where(block_first, 0.0, pltpu.roll(high, 1, 0)) + low_sum)
    high_end = 0.25 * (high_sum + jnp.where(block_last, 0.0, pltpu.roll(low, BLOCKS - 1, 0)))
    enter = 1.0 / resistance(low_smooth - low_end)
    leave = 1.0 / resistance(high_end - high_smooth)
    across = pltpu.roll(low_end, BLOCKS - 1, 0) - high_end
    across = jnp.where(block_last, 0.0, 1.0 / resistance(across))
    zero = jnp.zeros_like(coupling)
    one = jnp.ones_like(coupling)
    before, _ = join(
        (enter, one, zero, low_cell, zero), (coupling, near_ground, far_ground, near_source, far_source)
    )
    after, at_high = join((leave, zero, one, zero, high_cell), (across, zero, zero, zero, zero))
    whole, between = join(before, after)
    first = chain_solve(*whole, BLOCKS)
    later = pltpu.roll(first, BLOCKS - 1, 0)

    def middle(weights, left, right):
        return weights[0] * left + weights[1] * right + weights[2]

    out[:, 0, :] = first
    out[:, 1, :] = middle(at_high, middle(between, first, later), later)


def pick(flag, there, here):
    return tuple(jnp.where(flag, a, b) for a, b in zip(there, here))


def join_kernel(bit, own, other, out):
    upper = (lax.axis_index("depth") & bit) != 0
    mine = tuple(own[place] for place in range(5))
    theirs = tuple(other[place] for place in range(5))
    port, _ = join(pick(upper, theirs, mine), pick(upper, mine, theirs))
    for place, value in enumerate(port):
        out[place] = value


def finish_plane_kernel(
    own, near, pair, quad, factor, back, rest, mid, solved_x, inner, smooth, out, ends,
):
    index = lax.axis_index("depth")
    zero = jnp.zeros((ROWS, COLS), F32)
    left_ground, left_source, right_ground, right_source = zero, zero, zero, zero
    for bit, ref in ((4, quad), (2, pair), (1, near)):
        on_left = (index & bit) != 0
        c, ng, fg, ns, fs = (ref[place] for place in range(5))
        ground, source = ng + left_ground, ns + left_source
        share = c / (c + ground)
        left_ground = jnp.where(on_left, fg + share * ground, left_ground)
        left_source = jnp.where(on_left, fs + share * source, left_source)
        ground, source = fg + right_ground, fs + right_source
        total = c + ground
        share = jnp.where(total > 0.0, c / jnp.where(total > 0.0, total, 1.0), 0.0)
        right_ground = jnp.where(on_left, right_ground, ng + share * ground)
        right_source = jnp.where(on_left, right_source, ns + share * source)
    c, ng, fg, ns, fs = (own[place] for place in range(5))
    ground, source = fg + right_ground, fs + right_source
    total = c + ground
    inverse = jnp.where(total > 0.0, 1.0 / jnp.where(total > 0.0, total, 1.0), 0.0)
    share = c * inverse
    first = (left_source + ns + share * source) / (left_ground + ng + share * ground)
    after = share * first + source * inverse
    middle = mid[0] * first + mid[1] * after + mid[2]
    half = PLANES // 2
    for start, near_value, far_value in ((0, first, middle), (half, middle, after)):
        value = far_value
        for plane in range(start + half - 1, start, -1):
            span = slice(plane * ROWS, (plane + 1) * ROWS)
            value = factor[span, :] * value + (back[span, :] * near_value + rest[span, :])
            out[span, :] = solved_x[span, :] + value
        span = slice(start * ROWS, (start + 1) * ROWS)
        out[span, :] = solved_x[span, :] + near_value
    coupling, near_ground, far_ground, near_source, far_source = (inner[place] for place in range(5))
    enter = 1.0 / resistance(strided(smooth, 1) - strided(smooth, 0))
    leave = 1.0 / resistance(strided(smooth, ROWS - 1) - strided(smooth, ROWS - 2))
    inverse = 1.0 / (enter + near_ground + coupling)
    to_low, to_high, at_low = enter * inverse, coupling * inverse, near_source * inverse
    total = 1.0 / (leave + far_ground + to_high * (enter + near_ground))
    values = (
        to_low, to_high, at_low,
        coupling * to_low * total, leave * total, (far_source + coupling * at_low) * total,
    )
    for place, value in enumerate(values):
        ends[place] = value


def finish_row_kernel(solved, ends, factor, back, rest, others, out):
    third = 1.0 / 3.0

    def put(row, value):
        place = pl.ds(row, PLANES, stride=ROWS)
        out[place, :] = (others[place, :] + value) * third

    low, high = solved[:, 0, :], solved[:, 1, :]
    value = ends[3] * low + (ends[4] * high + ends[5])
    first = ends[0] * low + (ends[1] * value + ends[2])
    put(0, low)
    put(1, first)
    put(ROWS - 2, value)
    put(ROWS - 1, high)
    for row in range(ROWS - 3, 1, -1):
        value = factor[row] * value + (back[row] * first + rest[row])
        put(row, value)


def call(kernel, outs, scratch=(), flops=1000000, moved=500000, **options):
    return pl.pallas_call(
        kernel,
        out_shape=outs,
        scratch_shapes=scratch,
        compiler_params=pltpu.CompilerParams(vmem_limit_bytes=16 * 1024 * 1024),
        cost_estimate=pl.CostEstimate(flops=flops, bytes_accessed=moved, transcendentals=0),
        **options,
    )


def shaped(*shape):
    return jax.ShapeDtypeStruct(shape, F32)


def line_perm(axis, step):
    count = lax.axis_size(axis)
    if step > 0:
        return [(i, i + 1) for i in range(count - 1)]
    return [(i + 1, i) for i in range(count - 1)]


def swap_perm(axis, bit):
    return [(i, i ^ bit) for i in range(lax.axis_size(axis))]


def next_perm(axis):
    pairs = []
    for i in range(1, lax.axis_size(axis) - 1, 2):
        pairs += [(i, i + 1), (i + 1, i)]
    return pairs


def shards(volume):
    flat = volume.reshape(PLANES * ROWS, COLS)
    lines = shaped(ROWS, PLANES, COLS)
    whole = shaped(PLANES * ROWS, COLS)
    tall = shaped((PLANES + 1) * ROWS, COLS)
    port = shaped(5, ROWS, COLS)
    side = shaped(PLANES + 1, COLS)
    to_near, to_far = call(
        edge_kernel,
        (shaped(2 * ROWS, COLS), shaped(2 * ROWS, COLS)),
        (pltpu.SemaphoreType.DMA((2,)),),
        in_specs=[pl.BlockSpec(memory_space=pl.ANY)],
    )(flat)
    far_side = lax.ppermute(to_far, "depth", next_perm("depth"))
    near_side = lax.ppermute(to_near, "depth", swap_perm("depth", 1))
    to_pair, to_next = call(
        side_kernel, (side, side), (pltpu.VMEM((40, COLS), F32), pltpu.VMEM((40, COLS), F32))
    )(flat, near_side, far_side)
    next_row = lax.ppermute(to_next, "lat", next_perm("lat"))
    pair_row = lax.ppermute(to_pair, "lat", swap_perm("lat", 1))
    y_port, y_factor, y_back, y_rest, y_inner, deep = call(
        row_kernel,
        (shaped(PLANES * PORT, COLS), lines, lines, lines, shaped(5, PLANES, COLS), tall),
        (pltpu.VMEM((PLANES + 3, ROWS, COLS), F32),),
    )(flat, near_side, far_side)
    ports = lax.all_to_all(y_port, "lat", 0, 0, tiled=True)
    z_port, z_factor, z_back, z_rest, z_mid, smooth = call(
        plane_kernel, (port, whole, whole, whole, shaped(3, ROWS, COLS), tall), flops=LONG
    )(flat, deep, pair_row, next_row)
    near = lax.ppermute(z_port, "depth", swap_perm("depth", 1))
    solved_x = call(
        column_kernel,
        whole,
        (
            pltpu.VMEM((512, COLS), F32),
            pltpu.VMEM((512, COLS), F32),
            pltpu.VMEM((16, 32, COLS), F32),
            pltpu.VMEM((16, 32, COLS), F32),
            pltpu.VMEM((16, 32, COLS), F32),
        ),
    )(flat, smooth)
    pair_own = call(lambda *refs: join_kernel(1, *refs), port)(z_port, near)
    pair = lax.ppermute(pair_own, "depth", swap_perm("depth", 2))
    quad_own = call(lambda *refs: join_kernel(2, *refs), port)(pair_own, pair)
    ports, quad_own, solved_x = lax.optimization_barrier((ports, quad_own, solved_x))
    ends = call(row_reduced_kernel, shaped(BLOCKS, 2, COLS))(ports)
    ends, quad_own = lax.optimization_barrier((ends, quad_own))
    quad = lax.ppermute(quad_own, "depth", swap_perm("depth", 6))
    others, y_ends = call(finish_plane_kernel, (whole, shaped(6, PLANES, COLS)))(
        z_port, near, pair, quad, z_factor, z_back, z_rest, z_mid, solved_x, y_inner, smooth
    )
    ends_y = lax.all_to_all(ends, "lat", 0, 0, tiled=True)
    out = call(finish_row_kernel, whole)(ends_y, y_ends, y_factor, y_back, y_rest, others)
    return out.reshape(PLANES, ROWS, COLS)


def solution(mesh):
    placed = (P("depth", "lat", None),)
    return jax.shard_map(
        shards, mesh=mesh, in_specs=placed, out_specs=P("depth", "lat", None), check_vma=False
    )
```

```python
import jax
import jax.numpy as jnp
from jax import lax
from jax.experimental import pallas as pl
from jax.experimental.pallas import tpu as pltpu
from jax.sharding import PartitionSpec as P

TAU3 = 900.0
INV_LAMBDA_SQ = 4.0
PLANES = 32
ROWS = 16
COLS = 128
BLOCKS = 32
PORT = 16
LONG = 100_000_000_000
F32 = jnp.float32


def resistance(diff):
    return (1.0 + INV_LAMBDA_SQ * (diff * diff)) * (1.0 / TAU3)


def smooth_lanes(field, first, last):
    before = jnp.where(first, 0.0, pltpu.roll(field, 1, field.ndim - 1))
    after = jnp.where(last, 0.0, pltpu.roll(field, COLS - 1, field.ndim - 1))
    return 0.25 * (before + 2.0 * field + after)


def eliminate(coupling, ground, source, near_ground, near_source, resist):
    factor = 1.0 / (1.0 + (coupling + ground) * resist)
    weight = factor * resist
    back = coupling * weight
    near_ground = near_ground + back * ground
    near_source = near_source + back * source
    saved = (factor, back, source * weight)
    return coupling * factor, ground * factor, source * factor, near_ground, near_source, saved


def eliminate_last(coupling, ground, source, near_ground, near_source, conduct):
    inverse = 1.0 / (coupling + ground + conduct)
    factor = conduct * inverse
    back = coupling * inverse
    near_ground = near_ground + back * ground
    near_source = near_source + back * source
    saved = (factor, back, source * inverse)
    return coupling * factor, ground * factor, source * factor, near_ground, near_source, saved


def join(left, right):
    lc, lg, lh, ls, lt = left
    rc, rg, rh, rs, rt = right
    ground = lh + rg
    source = lt + rs
    inverse = 1.0 / (lc + rc + ground)
    to_left = lc * inverse
    to_right = rc * inverse
    return (
        lc * to_right,
        lg + to_left * ground,
        rh + to_right * ground,
        ls + to_left * source,
        rt + to_right * source,
    ), (to_left, to_right, source * inverse)


def edge_kernel(vol, near_side, far_side, sems):
    odd = lax.axis_index("depth") & 1
    high = (PLANES - 2) * ROWS
    near_start = pl.multiple_of((1 - odd) * high, ROWS)
    far_start = pl.multiple_of(odd * high, ROWS)
    copies = (
        pltpu.make_async_copy(vol.at[pl.ds(near_start, 2 * ROWS), :], near_side, sems.at[0]),
        pltpu.make_async_copy(vol.at[pl.ds(far_start, 2 * ROWS), :], far_side, sems.at[1]),
    )
    for copy in copies:
        copy.start()
    for copy in copies:
        copy.wait()


def strided(ref, row):
    return ref[pl.ds(row, 32, stride=16), :]


def cells(ref, plane):
    return ref[plane * ROWS : (plane + 1) * ROWS, :]


def faces(near_side, far_side):
    odd = (lax.axis_index("depth") & 1) == 1
    near, far = near_side[...], far_side[...]
    return jnp.where(odd, near, far)[ROWS:, :], jnp.where(odd, far, near)


def side_kernel(vol, near_side, far_side, pair_row, next_row, low_side, high_side):
    odd_row = (lax.axis_index("lat") & 1) == 1
    below, above = faces(near_side, far_side)
    lane = lax.broadcasted_iota(jnp.int32, (PLANES + 3, COLS), 1)
    sides = []
    for row, ref in ((0, low_side), (ROWS - 1, high_side)):
        ref[0:1, :] = below[row : row + 1, :]
        ref[1 : PLANES + 1, :] = vol[pl.ds(row, PLANES, stride=ROWS), :]
        ref[PLANES + 1 : PLANES + 2, :] = above[row : row + 1, :]
        ref[PLANES + 2 : PLANES + 3, :] = above[ROWS + row : ROWS + row + 1, :]
        ref[0 : PLANES + 3, :] = smooth_lanes(ref[0 : PLANES + 3, :], lane == 0, lane == COLS - 1)
        sides.append(
            0.25 * (ref[0 : PLANES + 1, :] + 2.0 * ref[1 : PLANES + 2, :] + ref[2 : PLANES + 3, :])
        )
    pair_row[...] = jnp.where(odd_row, sides[0], sides[1])
    next_row[...] = jnp.where(odd_row, sides[1], sides[0])


def plane_kernel(vol, deep, pair_row, next_row, port, factor, back, rest, mid, smooth):
    odd_row = (lax.axis_index("lat") & 1) == 1
    low_row = jnp.where(odd_row, pair_row[...], next_row[...])
    high_row = jnp.where(odd_row, next_row[...], pair_row[...])
    depth_last = lax.axis_index("depth") == lax.axis_size("depth") - 1
    z_open = jnp.where(depth_last, 0.0, TAU3).astype(F32)
    row_index = lax.broadcasted_iota(jnp.int32, (ROWS, COLS), 0)
    top, bottom = row_index == 0, row_index == ROWS - 1
    for plane in range(PLANES + 1):
        span = slice(plane * ROWS, (plane + 1) * ROWS)
        here = deep[span, :]
        above = jnp.where(top, low_row[plane : plane + 1, :], pltpu.roll(here, 1, 0))
        below = jnp.where(bottom, high_row[plane : plane + 1, :], pltpu.roll(here, ROWS - 1, 0))
        smooth[span, :] = 0.25 * (above + 2.0 * here + below)

    def resist(plane):
        return resistance(cells(smooth, plane + 1) - cells(smooth, plane))

    half = PLANES // 2
    one = jnp.ones((ROWS, COLS), F32)
    states = [
        (1.0 / resist(start), one, cells(vol, start + 1), one, cells(vol, start)) for start in (0, half)
    ]
    for step in range(1, half):
        final = step == half - 1
        for part in range(2):
            plane = part * half + step
            span = slice(plane * ROWS, (plane + 1) * ROWS)
            if final and part == 1:
                *state, saved = eliminate_last(*states[part], z_open / (TAU3 * resist(plane)))
            else:
                *state, saved = eliminate(*states[part], resist(plane))
            if not final:
                state[1] = state[1] + 1.0
                state[2] = state[2] + cells(vol, plane + 1)
            states[part] = state
            factor[span, :], back[span, :], rest[span, :] = saved
    joined, middle = join(*[(c, ng, fg, ns, fs) for c, fg, fs, ng, ns in states])
    for place, value in enumerate(joined):
        port[place] = value
    for place, value in enumerate(middle):
        mid[place] = value


def row_kernel(vol, near_side, far_side, port, factor, back, rest, inner, deep, mixed):
    below, above = faces(near_side, far_side)
    lane = lax.broadcasted_iota(jnp.int32, (ROWS, COLS), 1)
    first, last = lane == 0, lane == COLS - 1
    mixed[0] = smooth_lanes(below, first, last)
    for plane in range(PLANES):
        mixed[plane + 1] = smooth_lanes(cells(vol, plane), first, last)
    for plane in range(2):
        mixed[PLANES + 1 + plane] = smooth_lanes(above[plane * ROWS : (plane + 1) * ROWS, :], first, last)
    for plane in range(PLANES + 1):
        deep[plane * ROWS : (plane + 1) * ROWS, :] = 0.25 * (
            mixed[plane] + 2.0 * mixed[plane + 1] + mixed[plane + 2]
        )
    part = [strided(deep, row) for row in range(ROWS)]
    low_sum = 2.0 * part[0] + part[1]
    high_sum = part[ROWS - 2] + 2.0 * part[ROWS - 1]
    smooth = [None] + [0.25 * (part[r - 1] + 2.0 * part[r] + part[r + 1]) for r in range(1, ROWS - 1)]
    one = jnp.ones((PLANES, COLS), F32)
    state = (1.0 / resistance(smooth[2] - smooth[1]), one, strided(vol, 2), one, strided(vol, 1))
    for row in range(2, ROWS - 2):
        *state, saved = eliminate(*state, resistance(smooth[row + 1] - smooth[row]))
        state[1] = state[1] + 1.0
        state[2] = state[2] + strided(vol, row + 1)
        factor[row], back[row], rest[row] = saved
    coupling, far_ground, far_source, near_ground, near_source = state
    values = (
        coupling, near_ground, far_ground, near_source, far_source,
        part[0], part[ROWS - 1], low_sum, high_sum, smooth[1], smooth[ROWS - 2],
        strided(vol, 0), strided(vol, ROWS - 1),
    )
    for place, value in enumerate(values):
        port[pl.ds(place, PLANES, stride=PORT), :] = value
    for place in range(5):
        inner[place] = values[place]
    for place in range(len(values), PORT):
        port[pl.ds(place, PLANES, stride=PORT), :] = jnp.zeros((PLANES, COLS), F32)


def chain_solve(coupling, near_ground, far_ground, near_source, far_source, count):
    size = coupling.shape[0]
    right = coupling
    ground = near_ground + pltpu.roll(far_ground, 1, 0)
    source = near_source + pltpu.roll(far_source, 1, 0)
    step = 1
    while step < count:
        left = pltpu.roll(right, step, 0)
        inverse = 1.0 / (ground + left + right)
        ground_part = ground * inverse
        source_part = source * inverse
        ground = (
            ground
            + left * pltpu.roll(ground_part, step, 0)
            + right * pltpu.roll(ground_part, size - step, 0)
        )
        source = (
            source
            + left * pltpu.roll(source_part, step, 0)
            + right * pltpu.roll(source_part, size - step, 0)
        )
        right = right * pltpu.roll(right * inverse, size - step, 0)
        step *= 2
    return source / ground


def column_kernel(vol, smooth, solved_x, turned, turned_smooth, factor, back, rest):
    for group in range(4):
        span = slice(group * COLS, (group + 1) * COLS)
        turned[span, :] = vol[span, :].T
        turned_smooth[span, :] = smooth[span, :].T

    def resist(step):
        if step < 15:
            return resistance(strided(turned_smooth, step + 1) - strided(turned_smooth, step))
        return resistance(pltpu.roll(strided(turned_smooth, 0), 31, 0) - strided(turned_smooth, 15))

    chunk_last = (lax.broadcasted_iota(jnp.int32, (32, COLS), 0) & 7) == 7
    one = jnp.ones((32, COLS), F32)
    state = (1.0 / resist(0), one, strided(turned, 1), one, strided(turned, 0))
    for step in range(1, 16):
        if step == 15:
            *state, saved = eliminate_last(*state, jnp.where(chunk_last, 0.0, 1.0 / resist(step)))
        else:
            *state, saved = eliminate(*state, resist(step))
            state[1] = state[1] + 1.0
            state[2] = state[2] + strided(turned, step + 1)
        factor[step], back[step], rest[step] = saved
    coupling, far_ground, far_source, near_ground, near_source = state
    first = chain_solve(coupling, near_ground, far_ground, near_source, far_source, 8)
    turned[pl.ds(0, 32, stride=16), :] = first
    value = pltpu.roll(first, 31, 0)
    for step in range(15, 0, -1):
        value = factor[step] * value + (back[step] * first + rest[step])
        turned[pl.ds(step, 32, stride=16), :] = value
    for group in range(4):
        span = slice(group * COLS, (group + 1) * COLS)
        solved_x[span, :] = turned[span, :].T


def row_reduced_kernel(ports, out):
    (
        coupling, near_ground, far_ground, near_source, far_source,
        low, high, low_sum, high_sum, low_smooth, high_smooth, low_cell, high_cell,
    ) = (ports[pl.ds(place, BLOCKS, stride=PORT), :] for place in range(13))
    block = lax.broadcasted_iota(jnp.int32, (BLOCKS, COLS), 0)
    block_first, block_last = block == 0, block == BLOCKS - 1
    low_end = 0.25 * (jnp.where(block_first, 0.0, pltpu.roll(high, 1, 0)) + low_sum)
    high_end = 0.25 * (high_sum + jnp.where(block_last, 0.0, pltpu.roll(low, BLOCKS - 1, 0)))
    enter = 1.0 / resistance(low_smooth - low_end)
    leave = 1.0 / resistance(high_end - high_smooth)
    across = pltpu.roll(low_end, BLOCKS - 1, 0) - high_end
    across = jnp.where(block_last, 0.0, 1.0 / resistance(across))
    zero = jnp.zeros_like(coupling)
    one = jnp.ones_like(coupling)
    before, _ = join(
        (enter, one, zero, low_cell, zero), (coupling, near_ground, far_ground, near_source, far_source)
    )
    after, at_high = join((leave, zero, one, zero, high_cell), (across, zero, zero, zero, zero))
    whole, between = join(before, after)
    first = chain_solve(*whole, BLOCKS)
    later = pltpu.roll(first, BLOCKS - 1, 0)

    def middle(weights, left, right):
        return weights[0] * left + weights[1] * right + weights[2]

    out[:, 0, :] = first
    out[:, 1, :] = middle(at_high, middle(between, first, later), later)


def pick(flag, there, here):
    return tuple(jnp.where(flag, a, b) for a, b in zip(there, here))


def join_kernel(bit, own, other, out):
    upper = (lax.axis_index("depth") & bit) != 0
    mine = tuple(own[place] for place in range(5))
    theirs = tuple(other[place] for place in range(5))
    port, _ = join(pick(upper, theirs, mine), pick(upper, mine, theirs))
    for place, value in enumerate(port):
        out[place] = value


def finish_plane_kernel(
    own, near, pair, quad, factor, back, rest, mid, solved_x, inner, smooth, out, ends,
):
    index = lax.axis_index("depth")
    zero = jnp.zeros((ROWS, COLS), F32)
    left_ground, left_source, right_ground, right_source = zero, zero, zero, zero
    for bit, ref in ((4, quad), (2, pair), (1, near)):
        on_left = (index & bit) != 0
        c, ng, fg, ns, fs = (ref[place] for place in range(5))
        ground, source = ng + left_ground, ns + left_source
        share = c / (c + ground)
        left_ground = jnp.where(on_left, fg + share * ground, left_ground)
        left_source = jnp.where(on_left, fs + share * source, left_source)
        ground, source = fg + right_ground, fs + right_source
        total = c + ground
        share = jnp.where(total > 0.0, c / jnp.where(total > 0.0, total, 1.0), 0.0)
        right_ground = jnp.where(on_left, right_ground, ng + share * ground)
        right_source = jnp.where(on_left, right_source, ns + share * source)
    c, ng, fg, ns, fs = (own[place] for place in range(5))
    ground, source = fg + right_ground, fs + right_source
    total = c + ground
    inverse = jnp.where(total > 0.0, 1.0 / jnp.where(total > 0.0, total, 1.0), 0.0)
    share = c * inverse
    first = (left_source + ns + share * source) / (left_ground + ng + share * ground)
    after = share * first + source * inverse
    middle = mid[0] * first + mid[1] * after + mid[2]
    half = PLANES // 2
    for start, near_value, far_value in ((0, first, middle), (half, middle, after)):
        value = far_value
        for plane in range(start + half - 1, start, -1):
            span = slice(plane * ROWS, (plane + 1) * ROWS)
            value = factor[span, :] * value + (back[span, :] * near_value + rest[span, :])
            out[span, :] = solved_x[span, :] + value
        span = slice(start * ROWS, (start + 1) * ROWS)
        out[span, :] = solved_x[span, :] + near_value
    coupling, near_ground, far_ground, near_source, far_source = (inner[place] for place in range(5))
    enter = 1.0 / resistance(strided(smooth, 1) - strided(smooth, 0))
    leave = 1.0 / resistance(strided(smooth, ROWS - 1) - strided(smooth, ROWS - 2))
    inverse = 1.0 / (enter + near_ground + coupling)
    to_low, to_high, at_low = enter * inverse, coupling * inverse, near_source * inverse
    total = 1.0 / (leave + far_ground + to_high * (enter + near_ground))
    values = (
        to_low, to_high, at_low,
        coupling * to_low * total, leave * total, (far_source + coupling * at_low) * total,
    )
    for place, value in enumerate(values):
        ends[place] = value


def finish_row_kernel(solved, ends, factor, back, rest, others, out):
    third = 1.0 / 3.0

    def put(row, value):
        place = pl.ds(row, PLANES, stride=ROWS)
        out[place, :] = (others[place, :] + value) * third

    low, high = solved[:, 0, :], solved[:, 1, :]
    value = ends[3] * low + (ends[4] * high + ends[5])
    first = ends[0] * low + (ends[1] * value + ends[2])
    put(0, low)
    put(1, first)
    put(ROWS - 2, value)
    put(ROWS - 1, high)
    for row in range(ROWS - 3, 1, -1):
        value = factor[row] * value + (back[row] * first + rest[row])
        put(row, value)


def call(kernel, outs, scratch=(), flops=1000000, moved=500000, **options):
    return pl.pallas_call(
        kernel,
        out_shape=outs,
        scratch_shapes=scratch,
        compiler_params=pltpu.CompilerParams(vmem_limit_bytes=16 * 1024 * 1024),
        cost_estimate=pl.CostEstimate(flops=flops, bytes_accessed=moved, transcendentals=0),
        **options,
    )


def shaped(*shape):
    return jax.ShapeDtypeStruct(shape, F32)


def line_perm(axis, step):
    count = lax.axis_size(axis)
    if step > 0:
        return [(i, i + 1) for i in range(count - 1)]
    return [(i + 1, i) for i in range(count - 1)]


def swap_perm(axis, bit):
    return [(i, i ^ bit) for i in range(lax.axis_size(axis))]


def next_perm(axis):
    pairs = []
    for i in range(1, lax.axis_size(axis) - 1, 2):
        pairs += [(i, i + 1), (i + 1, i)]
    return pairs


def shards(volume):
    flat = volume.reshape(PLANES * ROWS, COLS)
    lines = shaped(ROWS, PLANES, COLS)
    whole = shaped(PLANES * ROWS, COLS)
    tall = shaped((PLANES + 1) * ROWS, COLS)
    port = shaped(5, ROWS, COLS)
    side = shaped(PLANES + 1, COLS)
    to_near, to_far = call(
        edge_kernel,
        (shaped(2 * ROWS, COLS), shaped(2 * ROWS, COLS)),
        (pltpu.SemaphoreType.DMA((2,)),),
        in_specs=[pl.BlockSpec(memory_space=pl.ANY)],
    )(flat)
    far_side = lax.ppermute(to_far, "depth", next_perm("depth"))
    near_side = lax.ppermute(to_near, "depth", swap_perm("depth", 1))
    to_pair, to_next = call(
        side_kernel, (side, side), (pltpu.VMEM((40, COLS), F32), pltpu.VMEM((40, COLS), F32))
    )(flat, near_side, far_side)
    next_row = lax.ppermute(to_next, "lat", next_perm("lat"))
    pair_row = lax.ppermute(to_pair, "lat", swap_perm("lat", 1))
    y_port, y_factor, y_back, y_rest, y_inner, deep = call(
        row_kernel,
        (shaped(PLANES * PORT, COLS), lines, lines, lines, shaped(5, PLANES, COLS), tall),
        (pltpu.VMEM((PLANES + 3, ROWS, COLS), F32),),
    )(flat, near_side, far_side)
    ports = lax.all_to_all(y_port, "lat", 0, 0, tiled=True)
    z_port, z_factor, z_back, z_rest, z_mid, smooth = call(
        plane_kernel, (port, whole, whole, whole, shaped(3, ROWS, COLS), tall), flops=LONG
    )(flat, deep, pair_row, next_row)
    near = lax.ppermute(z_port, "depth", swap_perm("depth", 1))
    solved_x = call(
        column_kernel,
        whole,
        (
            pltpu.VMEM((512, COLS), F32),
            pltpu.VMEM((512, COLS), F32),
            pltpu.VMEM((16, 32, COLS), F32),
            pltpu.VMEM((16, 32, COLS), F32),
            pltpu.VMEM((16, 32, COLS), F32),
        ),
    )(flat, smooth)
    pair_own = call(lambda *refs: join_kernel(1, *refs), port)(z_port, near)
    pair = lax.ppermute(pair_own, "depth", swap_perm("depth", 2))
    quad_own = call(lambda *refs: join_kernel(2, *refs), port)(pair_own, pair)
    quad = lax.ppermute(quad_own, "depth", swap_perm("depth", 6))
    others, y_ends = call(finish_plane_kernel, (whole, shaped(6, PLANES, COLS)))(
        z_port, near, pair, quad, z_factor, z_back, z_rest, z_mid, solved_x, y_inner, smooth
    )
    ports, others, y_ends = lax.optimization_barrier((ports, others, y_ends))
    ends = call(row_reduced_kernel, shaped(BLOCKS, 2, COLS))(ports)
    ends_y = lax.all_to_all(ends, "lat", 0, 0, tiled=True)
    out = call(finish_row_kernel, whole)(ends_y, y_ends, y_factor, y_back, y_rest, others)
    return out.reshape(PLANES, ROWS, COLS)


def solution(mesh):
    placed = (P("depth", "lat", None),)
    return jax.shard_map(
        shards, mesh=mesh, in_specs=placed, out_specs=P("depth", "lat", None), check_vma=False
    )
```

```python
import jax
import jax.numpy as jnp
from jax import lax
from jax.experimental import pallas as pl
from jax.experimental.pallas import tpu as pltpu
from jax.sharding import PartitionSpec as P

TAU3 = 900.0
INV_LAMBDA_SQ = 4.0
PLANES = 32
ROWS = 16
COLS = 128
BLOCKS = 32
PORT = 16
F32 = jnp.float32


def resistance(diff):
    return (1.0 + INV_LAMBDA_SQ * (diff * diff)) * (1.0 / TAU3)


def smooth_lanes(field, first, last):
    before = jnp.where(first, 0.0, pltpu.roll(field, 1, field.ndim - 1))
    after = jnp.where(last, 0.0, pltpu.roll(field, COLS - 1, field.ndim - 1))
    return 0.25 * (before + 2.0 * field + after)


def eliminate(coupling, ground, source, near_ground, near_source, resist):
    factor = 1.0 / (1.0 + (coupling + ground) * resist)
    weight = factor * resist
    back = coupling * weight
    near_ground = near_ground + back * ground
    near_source = near_source + back * source
    saved = (factor, back, source * weight)
    return coupling * factor, ground * factor, source * factor, near_ground, near_source, saved


def eliminate_last(coupling, ground, source, near_ground, near_source, conduct):
    inverse = 1.0 / (coupling + ground + conduct)
    factor = conduct * inverse
    back = coupling * inverse
    near_ground = near_ground + back * ground
    near_source = near_source + back * source
    saved = (factor, back, source * inverse)
    return coupling * factor, ground * factor, source * factor, near_ground, near_source, saved


def join(left, right):
    lc, lg, lh, ls, lt = left
    rc, rg, rh, rs, rt = right
    ground = lh + rg
    source = lt + rs
    inverse = 1.0 / (lc + rc + ground)
    to_left = lc * inverse
    to_right = rc * inverse
    return (
        lc * to_right,
        lg + to_left * ground,
        rh + to_right * ground,
        ls + to_left * source,
        rt + to_right * source,
    ), (to_left, to_right, source * inverse)


def edge_kernel(vol, near_side, far_side, sems):
    odd = lax.axis_index("depth") & 1
    high = (PLANES - 2) * ROWS
    near_start = pl.multiple_of((1 - odd) * high, ROWS)
    far_start = pl.multiple_of(odd * high, ROWS)
    copies = (
        pltpu.make_async_copy(vol.at[pl.ds(near_start, 2 * ROWS), :], near_side, sems.at[0]),
        pltpu.make_async_copy(vol.at[pl.ds(far_start, 2 * ROWS), :], far_side, sems.at[1]),
    )
    for copy in copies:
        copy.start()
    for copy in copies:
        copy.wait()


def strided(ref, row):
    return ref[pl.ds(row, 32, stride=16), :]


def cells(ref, plane):
    return ref[plane * ROWS : (plane + 1) * ROWS, :]


def faces(near_side, far_side):
    odd = (lax.axis_index("depth") & 1) == 1
    near, far = near_side[...], far_side[...]
    return jnp.where(odd, near, far)[ROWS:, :], jnp.where(odd, far, near)


def side_kernel(vol, near_side, far_side, pair_row, next_row, low_side, high_side):
    odd_row = (lax.axis_index("lat") & 1) == 1
    below, above = faces(near_side, far_side)
    lane = lax.broadcasted_iota(jnp.int32, (PLANES + 3, COLS), 1)
    sides = []
    for row, ref in ((0, low_side), (ROWS - 1, high_side)):
        ref[0:1, :] = below[row : row + 1, :]
        ref[1 : PLANES + 1, :] = vol[pl.ds(row, PLANES, stride=ROWS), :]
        ref[PLANES + 1 : PLANES + 2, :] = above[row : row + 1, :]
        ref[PLANES + 2 : PLANES + 3, :] = above[ROWS + row : ROWS + row + 1, :]
        ref[0 : PLANES + 3, :] = smooth_lanes(ref[0 : PLANES + 3, :], lane == 0, lane == COLS - 1)
        sides.append(
            0.25 * (ref[0 : PLANES + 1, :] + 2.0 * ref[1 : PLANES + 2, :] + ref[2 : PLANES + 3, :])
        )
    pair_row[...] = jnp.where(odd_row, sides[0], sides[1])
    next_row[...] = jnp.where(odd_row, sides[1], sides[0])


def plane_kernel(vol, deep, pair_row, next_row, port, factor, back, rest, mid, smooth):
    odd_row = (lax.axis_index("lat") & 1) == 1
    low_row = jnp.where(odd_row, pair_row[...], next_row[...])
    high_row = jnp.where(odd_row, next_row[...], pair_row[...])
    depth_last = lax.axis_index("depth") == lax.axis_size("depth") - 1
    z_open = jnp.where(depth_last, 0.0, TAU3).astype(F32)
    row_index = lax.broadcasted_iota(jnp.int32, (ROWS, COLS), 0)
    top, bottom = row_index == 0, row_index == ROWS - 1
    for plane in range(PLANES + 1):
        span = slice(plane * ROWS, (plane + 1) * ROWS)
        here = deep[span, :]
        above = jnp.where(top, low_row[plane : plane + 1, :], pltpu.roll(here, 1, 0))
        below = jnp.where(bottom, high_row[plane : plane + 1, :], pltpu.roll(here, ROWS - 1, 0))
        smooth[span, :] = 0.25 * (above + 2.0 * here + below)

    def resist(plane):
        return resistance(cells(smooth, plane + 1) - cells(smooth, plane))

    half = PLANES // 2
    one = jnp.ones((ROWS, COLS), F32)
    states = [
        (1.0 / resist(start), one, cells(vol, start + 1), one, cells(vol, start)) for start in (0, half)
    ]
    for step in range(1, half):
        final = step == half - 1
        for part in range(2):
            plane = part * half + step
            span = slice(plane * ROWS, (plane + 1) * ROWS)
            if final and part == 1:
                *state, saved = eliminate_last(*states[part], z_open / (TAU3 * resist(plane)))
            else:
                *state, saved = eliminate(*states[part], resist(plane))
            if not final:
                state[1] = state[1] + 1.0
                state[2] = state[2] + cells(vol, plane + 1)
            states[part] = state
            factor[span, :], back[span, :], rest[span, :] = saved
    joined, middle = join(*[(c, ng, fg, ns, fs) for c, fg, fs, ng, ns in states])
    for place, value in enumerate(joined):
        port[place] = value
    for place, value in enumerate(middle):
        mid[place] = value


def row_kernel(vol, near_side, far_side, port, factor, back, rest, inner, deep, mixed):
    below, above = faces(near_side, far_side)
    lane = lax.broadcasted_iota(jnp.int32, (ROWS, COLS), 1)
    first, last = lane == 0, lane == COLS - 1
    mixed[0] = smooth_lanes(below, first, last)
    for plane in range(PLANES):
        mixed[plane + 1] = smooth_lanes(cells(vol, plane), first, last)
    for plane in range(2):
        mixed[PLANES + 1 + plane] = smooth_lanes(above[plane * ROWS : (plane + 1) * ROWS, :], first, last)
    for plane in range(PLANES + 1):
        deep[plane * ROWS : (plane + 1) * ROWS, :] = 0.25 * (
            mixed[plane] + 2.0 * mixed[plane + 1] + mixed[plane + 2]
        )
    part = [strided(deep, row) for row in range(ROWS)]
    low_sum = 2.0 * part[0] + part[1]
    high_sum = part[ROWS - 2] + 2.0 * part[ROWS - 1]
    smooth = [None] + [0.25 * (part[r - 1] + 2.0 * part[r] + part[r + 1]) for r in range(1, ROWS - 1)]
    one = jnp.ones((PLANES, COLS), F32)
    state = (1.0 / resistance(smooth[2] - smooth[1]), one, strided(vol, 2), one, strided(vol, 1))
    for row in range(2, ROWS - 2):
        *state, saved = eliminate(*state, resistance(smooth[row + 1] - smooth[row]))
        state[1] = state[1] + 1.0
        state[2] = state[2] + strided(vol, row + 1)
        factor[row], back[row], rest[row] = saved
    coupling, far_ground, far_source, near_ground, near_source = state
    values = (
        coupling, near_ground, far_ground, near_source, far_source,
        part[0], part[ROWS - 1], low_sum, high_sum, smooth[1], smooth[ROWS - 2],
        strided(vol, 0), strided(vol, ROWS - 1),
    )
    for place, value in enumerate(values):
        port[pl.ds(place, PLANES, stride=PORT), :] = value
    for place in range(5):
        inner[place] = values[place]
    for place in range(len(values), PORT):
        port[pl.ds(place, PLANES, stride=PORT), :] = jnp.zeros((PLANES, COLS), F32)


def chain_solve(coupling, near_ground, far_ground, near_source, far_source, count):
    size = coupling.shape[0]
    right = coupling
    ground = near_ground + pltpu.roll(far_ground, 1, 0)
    source = near_source + pltpu.roll(far_source, 1, 0)
    step = 1
    while step < count:
        left = pltpu.roll(right, step, 0)
        inverse = 1.0 / (ground + left + right)
        ground_part = ground * inverse
        source_part = source * inverse
        ground = (
            ground
            + left * pltpu.roll(ground_part, step, 0)
            + right * pltpu.roll(ground_part, size - step, 0)
        )
        source = (
            source
            + left * pltpu.roll(source_part, step, 0)
            + right * pltpu.roll(source_part, size - step, 0)
        )
        right = right * pltpu.roll(right * inverse, size - step, 0)
        step *= 2
    return source / ground


def column_kernel(vol, smooth, solved_x, turned, turned_smooth, factor, back, rest):
    for group in range(4):
        span = slice(group * COLS, (group + 1) * COLS)
        turned[span, :] = vol[span, :].T
        turned_smooth[span, :] = smooth[span, :].T

    def resist(step):
        if step < 15:
            return resistance(strided(turned_smooth, step + 1) - strided(turned_smooth, step))
        return resistance(pltpu.roll(strided(turned_smooth, 0), 31, 0) - strided(turned_smooth, 15))

    chunk_last = (lax.broadcasted_iota(jnp.int32, (32, COLS), 0) & 7) == 7
    one = jnp.ones((32, COLS), F32)
    state = (1.0 / resist(0), one, strided(turned, 1), one, strided(turned, 0))
    for step in range(1, 16):
        if step == 15:
            *state, saved = eliminate_last(*state, jnp.where(chunk_last, 0.0, 1.0 / resist(step)))
        else:
            *state, saved = eliminate(*state, resist(step))
            state[1] = state[1] + 1.0
            state[2] = state[2] + strided(turned, step + 1)
        factor[step], back[step], rest[step] = saved
    coupling, far_ground, far_source, near_ground, near_source = state
    first = chain_solve(coupling, near_ground, far_ground, near_source, far_source, 8)
    turned[pl.ds(0, 32, stride=16), :] = first
    value = pltpu.roll(first, 31, 0)
    for step in range(15, 0, -1):
        value = factor[step] * value + (back[step] * first + rest[step])
        turned[pl.ds(step, 32, stride=16), :] = value
    for group in range(4):
        span = slice(group * COLS, (group + 1) * COLS)
        solved_x[span, :] = turned[span, :].T


def row_reduced_kernel(ports, out):
    (
        coupling, near_ground, far_ground, near_source, far_source,
        low, high, low_sum, high_sum, low_smooth, high_smooth, low_cell, high_cell,
    ) = (ports[pl.ds(place, BLOCKS, stride=PORT), :] for place in range(13))
    block = lax.broadcasted_iota(jnp.int32, (BLOCKS, COLS), 0)
    block_first, block_last = block == 0, block == BLOCKS - 1
    low_end = 0.25 * (jnp.where(block_first, 0.0, pltpu.roll(high, 1, 0)) + low_sum)
    high_end = 0.25 * (high_sum + jnp.where(block_last, 0.0, pltpu.roll(low, BLOCKS - 1, 0)))
    enter = 1.0 / resistance(low_smooth - low_end)
    leave = 1.0 / resistance(high_end - high_smooth)
    across = pltpu.roll(low_end, BLOCKS - 1, 0) - high_end
    across = jnp.where(block_last, 0.0, 1.0 / resistance(across))
    zero = jnp.zeros_like(coupling)
    one = jnp.ones_like(coupling)
    before, _ = join(
        (enter, one, zero, low_cell, zero), (coupling, near_ground, far_ground, near_source, far_source)
    )
    after, at_high = join((leave, zero, one, zero, high_cell), (across, zero, zero, zero, zero))
    whole, between = join(before, after)
    first = chain_solve(*whole, BLOCKS)
    later = pltpu.roll(first, BLOCKS - 1, 0)

    def middle(weights, left, right):
        return weights[0] * left + weights[1] * right + weights[2]

    out[:, 0, :] = first
    out[:, 1, :] = middle(at_high, middle(between, first, later), later)


def pick(flag, there, here):
    return tuple(jnp.where(flag, a, b) for a, b in zip(there, here))


def join_kernel(bit, own, other, out):
    upper = (lax.axis_index("depth") & bit) != 0
    mine = tuple(own[place] for place in range(5))
    theirs = tuple(other[place] for place in range(5))
    port, _ = join(pick(upper, theirs, mine), pick(upper, mine, theirs))
    for place, value in enumerate(port):
        out[place] = value


def finish_plane_kernel(
    own, near, pair, quad, factor, back, rest, mid, solved_x, inner, smooth, out, ends,
):
    index = lax.axis_index("depth")
    zero = jnp.zeros((ROWS, COLS), F32)
    left_ground, left_source, right_ground, right_source = zero, zero, zero, zero
    for bit, ref in ((4, quad), (2, pair), (1, near)):
        on_left = (index & bit) != 0
        c, ng, fg, ns, fs = (ref[place] for place in range(5))
        ground, source = ng + left_ground, ns + left_source
        share = c / (c + ground)
        left_ground = jnp.where(on_left, fg + share * ground, left_ground)
        left_source = jnp.where(on_left, fs + share * source, left_source)
        ground, source = fg + right_ground, fs + right_source
        total = c + ground
        share = jnp.where(total > 0.0, c / jnp.where(total > 0.0, total, 1.0), 0.0)
        right_ground = jnp.where(on_left, right_ground, ng + share * ground)
        right_source = jnp.where(on_left, right_source, ns + share * source)
    c, ng, fg, ns, fs = (own[place] for place in range(5))
    ground, source = fg + right_ground, fs + right_source
    total = c + ground
    inverse = jnp.where(total > 0.0, 1.0 / jnp.where(total > 0.0, total, 1.0), 0.0)
    share = c * inverse
    first = (left_source + ns + share * source) / (left_ground + ng + share * ground)
    after = share * first + source * inverse
    middle = mid[0] * first + mid[1] * after + mid[2]
    half = PLANES // 2
    for start, near_value, far_value in ((0, first, middle), (half, middle, after)):
        value = far_value
        for plane in range(start + half - 1, start, -1):
            span = slice(plane * ROWS, (plane + 1) * ROWS)
            value = factor[span, :] * value + (back[span, :] * near_value + rest[span, :])
            out[span, :] = solved_x[span, :] + value
        span = slice(start * ROWS, (start + 1) * ROWS)
        out[span, :] = solved_x[span, :] + near_value
    coupling, near_ground, far_ground, near_source, far_source = (inner[place] for place in range(5))
    enter = 1.0 / resistance(strided(smooth, 1) - strided(smooth, 0))
    leave = 1.0 / resistance(strided(smooth, ROWS - 1) - strided(smooth, ROWS - 2))
    inverse = 1.0 / (enter + near_ground + coupling)
    to_low, to_high, at_low = enter * inverse, coupling * inverse, near_source * inverse
    total = 1.0 / (leave + far_ground + to_high * (enter + near_ground))
    values = (
        to_low, to_high, at_low,
        coupling * to_low * total, leave * total, (far_source + coupling * at_low) * total,
    )
    for place, value in enumerate(values):
        ends[place] = value


def finish_row_kernel(solved, ends, factor, back, rest, others, out):
    third = 1.0 / 3.0

    def put(row, value):
        place = pl.ds(row, PLANES, stride=ROWS)
        out[place, :] = (others[place, :] + value) * third

    low, high = solved[:, 0, :], solved[:, 1, :]
    value = ends[3] * low + (ends[4] * high + ends[5])
    first = ends[0] * low + (ends[1] * value + ends[2])
    put(0, low)
    put(1, first)
    put(ROWS - 2, value)
    put(ROWS - 1, high)
    for row in range(ROWS - 3, 1, -1):
        value = factor[row] * value + (back[row] * first + rest[row])
        put(row, value)


def call(kernel, outs, scratch=(), flops=1000000, moved=500000, **options):
    return pl.pallas_call(
        kernel,
        out_shape=outs,
        scratch_shapes=scratch,
        compiler_params=pltpu.CompilerParams(vmem_limit_bytes=16 * 1024 * 1024),
        cost_estimate=pl.CostEstimate(flops=flops, bytes_accessed=moved, transcendentals=0),
        **options,
    )


def shaped(*shape):
    return jax.ShapeDtypeStruct(shape, F32)


def line_perm(axis, step):
    count = lax.axis_size(axis)
    if step > 0:
        return [(i, i + 1) for i in range(count - 1)]
    return [(i + 1, i) for i in range(count - 1)]


def swap_perm(axis, bit):
    return [(i, i ^ bit) for i in range(lax.axis_size(axis))]


def next_perm(axis):
    pairs = []
    for i in range(1, lax.axis_size(axis) - 1, 2):
        pairs += [(i, i + 1), (i + 1, i)]
    return pairs


def shards(volume):
    flat = volume.reshape(PLANES * ROWS, COLS)
    lines = shaped(ROWS, PLANES, COLS)
    whole = shaped(PLANES * ROWS, COLS)
    tall = shaped((PLANES + 1) * ROWS, COLS)
    port = shaped(5, ROWS, COLS)
    side = shaped(PLANES + 1, COLS)
    to_near, to_far = call(
        edge_kernel,
        (shaped(2 * ROWS, COLS), shaped(2 * ROWS, COLS)),
        (pltpu.SemaphoreType.DMA((2,)),),
        in_specs=[pl.BlockSpec(memory_space=pl.ANY)],
    )(flat)
    far_side = lax.ppermute(to_far, "depth", next_perm("depth"))
    near_side = lax.ppermute(to_near, "depth", swap_perm("depth", 1))
    to_pair, to_next = call(
        side_kernel, (side, side), (pltpu.VMEM((40, COLS), F32), pltpu.VMEM((40, COLS), F32))
    )(flat, near_side, far_side)
    next_row = lax.ppermute(to_next, "lat", next_perm("lat"))
    pair_row = lax.ppermute(to_pair, "lat", swap_perm("lat", 1))
    y_port, y_factor, y_back, y_rest, y_inner, deep = call(
        row_kernel,
        (shaped(PLANES * PORT, COLS), lines, lines, lines, shaped(5, PLANES, COLS), tall),
        (pltpu.VMEM((PLANES + 3, ROWS, COLS), F32),),
    )(flat, near_side, far_side)
    ports = lax.all_to_all(y_port, "lat", 0, 0, tiled=True)
    z_port, z_factor, z_back, z_rest, z_mid, smooth = call(
        plane_kernel, (port, whole, whole, whole, shaped(3, ROWS, COLS), tall)
    )(flat, deep, pair_row, next_row)
    near = lax.ppermute(z_port, "depth", swap_perm("depth", 1))
    solved_x = call(
        column_kernel,
        whole,
        (
            pltpu.VMEM((512, COLS), F32),
            pltpu.VMEM((512, COLS), F32),
            pltpu.VMEM((16, 32, COLS), F32),
            pltpu.VMEM((16, 32, COLS), F32),
            pltpu.VMEM((16, 32, COLS), F32),
        ),
    )(flat, smooth)
    pair_own = call(lambda *refs: join_kernel(1, *refs), port)(z_port, near)
    ports, pair_own, solved_x = lax.optimization_barrier((ports, pair_own, solved_x))
    ends = call(row_reduced_kernel, shaped(BLOCKS, 2, COLS))(ports)
    ends, pair_own = lax.optimization_barrier((ends, pair_own))
    pair = lax.ppermute(pair_own, "depth", swap_perm("depth", 2))
    quad_own = call(lambda *refs: join_kernel(2, *refs), port)(pair_own, pair)
    quad = lax.ppermute(quad_own, "depth", swap_perm("depth", 6))
    others, y_ends = call(finish_plane_kernel, (whole, shaped(6, PLANES, COLS)))(
        z_port, near, pair, quad, z_factor, z_back, z_rest, z_mid, solved_x, y_inner, smooth
    )
    ends_y = lax.all_to_all(ends, "lat", 0, 0, tiled=True)
    out = call(finish_row_kernel, whole)(ends_y, y_ends, y_factor, y_back, y_rest, others)
    return out.reshape(PLANES, ROWS, COLS)


def solution(mesh):
    placed = (P("depth", "lat", None),)
    return jax.shard_map(
        shards, mesh=mesh, in_specs=placed, out_specs=P("depth", "lat", None), check_vma=False
    )
```

```python
import jax
import jax.numpy as jnp
from jax import lax
from jax.experimental import pallas as pl
from jax.experimental.pallas import tpu as pltpu
from jax.sharding import PartitionSpec as P

TAU3 = 900.0
INV_LAMBDA_SQ = 4.0
PLANES = 32
ROWS = 16
COLS = 128
BLOCKS = 32
PORT = 16
F32 = jnp.float32


def resistance(diff):
    return (1.0 + INV_LAMBDA_SQ * (diff * diff)) * (1.0 / TAU3)


def smooth_lanes(field, first, last):
    before = jnp.where(first, 0.0, pltpu.roll(field, 1, field.ndim - 1))
    after = jnp.where(last, 0.0, pltpu.roll(field, COLS - 1, field.ndim - 1))
    return 0.25 * (before + 2.0 * field + after)


def eliminate(coupling, ground, source, near_ground, near_source, resist):
    factor = 1.0 / (1.0 + (coupling + ground) * resist)
    weight = factor * resist
    back = coupling * weight
    near_ground = near_ground + back * ground
    near_source = near_source + back * source
    saved = (factor, back, source * weight)
    return coupling * factor, ground * factor, source * factor, near_ground, near_source, saved


def eliminate_last(coupling, ground, source, near_ground, near_source, conduct):
    inverse = 1.0 / (coupling + ground + conduct)
    factor = conduct * inverse
    back = coupling * inverse
    near_ground = near_ground + back * ground
    near_source = near_source + back * source
    saved = (factor, back, source * inverse)
    return coupling * factor, ground * factor, source * factor, near_ground, near_source, saved


def join(left, right):
    lc, lg, lh, ls, lt = left
    rc, rg, rh, rs, rt = right
    ground = lh + rg
    source = lt + rs
    inverse = 1.0 / (lc + rc + ground)
    to_left = lc * inverse
    to_right = rc * inverse
    return (
        lc * to_right,
        lg + to_left * ground,
        rh + to_right * ground,
        ls + to_left * source,
        rt + to_right * source,
    ), (to_left, to_right, source * inverse)


def edge_kernel(vol, near_side, far_side, sems):
    odd = lax.axis_index("depth") & 1
    high = (PLANES - 2) * ROWS
    near_start = pl.multiple_of((1 - odd) * high, ROWS)
    far_start = pl.multiple_of(odd * high, ROWS)
    copies = (
        pltpu.make_async_copy(vol.at[pl.ds(near_start, 2 * ROWS), :], near_side, sems.at[0]),
        pltpu.make_async_copy(vol.at[pl.ds(far_start, 2 * ROWS), :], far_side, sems.at[1]),
    )
    for copy in copies:
        copy.start()
    for copy in copies:
        copy.wait()


def strided(ref, row):
    return ref[pl.ds(row, 32, stride=16), :]


def cells(ref, plane):
    return ref[plane * ROWS : (plane + 1) * ROWS, :]


def faces(near_side, far_side):
    odd = (lax.axis_index("depth") & 1) == 1
    near, far = near_side[...], far_side[...]
    return jnp.where(odd, near, far)[ROWS:, :], jnp.where(odd, far, near)


def side_kernel(vol, near_side, far_side, pair_row, next_row, low_side, high_side):
    odd_row = (lax.axis_index("lat") & 1) == 1
    below, above = faces(near_side, far_side)
    lane = lax.broadcasted_iota(jnp.int32, (PLANES + 3, COLS), 1)
    sides = []
    for row, ref in ((0, low_side), (ROWS - 1, high_side)):
        ref[0:1, :] = below[row : row + 1, :]
        ref[1 : PLANES + 1, :] = vol[pl.ds(row, PLANES, stride=ROWS), :]
        ref[PLANES + 1 : PLANES + 2, :] = above[row : row + 1, :]
        ref[PLANES + 2 : PLANES + 3, :] = above[ROWS + row : ROWS + row + 1, :]
        ref[0 : PLANES + 3, :] = smooth_lanes(ref[0 : PLANES + 3, :], lane == 0, lane == COLS - 1)
        sides.append(
            0.25 * (ref[0 : PLANES + 1, :] + 2.0 * ref[1 : PLANES + 2, :] + ref[2 : PLANES + 3, :])
        )
    pair_row[...] = jnp.where(odd_row, sides[0], sides[1])
    next_row[...] = jnp.where(odd_row, sides[1], sides[0])


def plane_kernel(vol, deep, pair_row, next_row, port, factor, back, rest, mid, smooth):
    odd_row = (lax.axis_index("lat") & 1) == 1
    low_row = jnp.where(odd_row, pair_row[...], next_row[...])
    high_row = jnp.where(odd_row, next_row[...], pair_row[...])
    depth_last = lax.axis_index("depth") == lax.axis_size("depth") - 1
    z_open = jnp.where(depth_last, 0.0, TAU3).astype(F32)
    row_index = lax.broadcasted_iota(jnp.int32, (ROWS, COLS), 0)
    top, bottom = row_index == 0, row_index == ROWS - 1
    for plane in range(PLANES + 1):
        span = slice(plane * ROWS, (plane + 1) * ROWS)
        here = deep[span, :]
        above = jnp.where(top, low_row[plane : plane + 1, :], pltpu.roll(here, 1, 0))
        below = jnp.where(bottom, high_row[plane : plane + 1, :], pltpu.roll(here, ROWS - 1, 0))
        smooth[span, :] = 0.25 * (above + 2.0 * here + below)

    def resist(plane):
        return resistance(cells(smooth, plane + 1) - cells(smooth, plane))

    half = PLANES // 2
    one = jnp.ones((ROWS, COLS), F32)
    states = [
        (1.0 / resist(start), one, cells(vol, start + 1), one, cells(vol, start)) for start in (0, half)
    ]
    for step in range(1, half):
        final = step == half - 1
        for part in range(2):
            plane = part * half + step
            span = slice(plane * ROWS, (plane + 1) * ROWS)
            if final and part == 1:
                *state, saved = eliminate_last(*states[part], z_open / (TAU3 * resist(plane)))
            else:
                *state, saved = eliminate(*states[part], resist(plane))
            if not final:
                state[1] = state[1] + 1.0
                state[2] = state[2] + cells(vol, plane + 1)
            states[part] = state
            factor[span, :], back[span, :], rest[span, :] = saved
    joined, middle = join(*[(c, ng, fg, ns, fs) for c, fg, fs, ng, ns in states])
    for place, value in enumerate(joined):
        port[place] = value
    for place, value in enumerate(middle):
        mid[place] = value


def row_kernel(vol, near_side, far_side, port, factor, back, rest, deep, mixed):
    below, above = faces(near_side, far_side)
    lane = lax.broadcasted_iota(jnp.int32, (ROWS, COLS), 1)
    first, last = lane == 0, lane == COLS - 1
    mixed[0] = smooth_lanes(below, first, last)
    for plane in range(PLANES):
        mixed[plane + 1] = smooth_lanes(cells(vol, plane), first, last)
    for plane in range(2):
        mixed[PLANES + 1 + plane] = smooth_lanes(above[plane * ROWS : (plane + 1) * ROWS, :], first, last)
    for plane in range(PLANES + 1):
        deep[plane * ROWS : (plane + 1) * ROWS, :] = 0.25 * (
            mixed[plane] + 2.0 * mixed[plane + 1] + mixed[plane + 2]
        )
    part = [strided(deep, row) for row in range(ROWS)]
    low_sum = 2.0 * part[0] + part[1]
    high_sum = part[ROWS - 2] + 2.0 * part[ROWS - 1]
    smooth = [None] + [0.25 * (part[r - 1] + 2.0 * part[r] + part[r + 1]) for r in range(1, ROWS - 1)]
    one = jnp.ones((PLANES, COLS), F32)
    state = (1.0 / resistance(smooth[2] - smooth[1]), one, strided(vol, 2), one, strided(vol, 1))
    for row in range(2, ROWS - 2):
        *state, saved = eliminate(*state, resistance(smooth[row + 1] - smooth[row]))
        state[1] = state[1] + 1.0
        state[2] = state[2] + strided(vol, row + 1)
        factor[row], back[row], rest[row] = saved
    coupling, far_ground, far_source, near_ground, near_source = state
    values = (
        coupling, near_ground, far_ground, near_source, far_source,
        part[0], part[ROWS - 1], low_sum, high_sum, smooth[1], smooth[ROWS - 2],
        strided(vol, 0), strided(vol, ROWS - 1),
    )
    for place, value in enumerate(values):
        port[pl.ds(place, PLANES, stride=PORT), :] = value
    for place in range(len(values), PORT):
        port[pl.ds(place, PLANES, stride=PORT), :] = jnp.zeros((PLANES, COLS), F32)


def chain_solve(coupling, near_ground, far_ground, near_source, far_source, count):
    size = coupling.shape[0]
    right = coupling
    ground = near_ground + pltpu.roll(far_ground, 1, 0)
    source = near_source + pltpu.roll(far_source, 1, 0)
    step = 1
    while step < count:
        left = pltpu.roll(right, step, 0)
        inverse = 1.0 / (ground + left + right)
        ground_part = ground * inverse
        source_part = source * inverse
        ground = (
            ground
            + left * pltpu.roll(ground_part, step, 0)
            + right * pltpu.roll(ground_part, size - step, 0)
        )
        source = (
            source
            + left * pltpu.roll(source_part, step, 0)
            + right * pltpu.roll(source_part, size - step, 0)
        )
        right = right * pltpu.roll(right * inverse, size - step, 0)
        step *= 2
    return source / ground


def column_kernel(vol, smooth, solved_x, turned, turned_smooth, factor, back, rest):
    for group in range(4):
        span = slice(group * COLS, (group + 1) * COLS)
        turned[span, :] = vol[span, :].T
        turned_smooth[span, :] = smooth[span, :].T

    def resist(step):
        if step < 15:
            return resistance(strided(turned_smooth, step + 1) - strided(turned_smooth, step))
        return resistance(pltpu.roll(strided(turned_smooth, 0), 31, 0) - strided(turned_smooth, 15))

    chunk_last = (lax.broadcasted_iota(jnp.int32, (32, COLS), 0) & 7) == 7
    one = jnp.ones((32, COLS), F32)
    state = (1.0 / resist(0), one, strided(turned, 1), one, strided(turned, 0))
    for step in range(1, 16):
        if step == 15:
            *state, saved = eliminate_last(*state, jnp.where(chunk_last, 0.0, 1.0 / resist(step)))
        else:
            *state, saved = eliminate(*state, resist(step))
            state[1] = state[1] + 1.0
            state[2] = state[2] + strided(turned, step + 1)
        factor[step], back[step], rest[step] = saved
    coupling, far_ground, far_source, near_ground, near_source = state
    first = chain_solve(coupling, near_ground, far_ground, near_source, far_source, 8)
    turned[pl.ds(0, 32, stride=16), :] = first
    value = pltpu.roll(first, 31, 0)
    for step in range(15, 0, -1):
        value = factor[step] * value + (back[step] * first + rest[step])
        turned[pl.ds(step, 32, stride=16), :] = value
    for group in range(4):
        span = slice(group * COLS, (group + 1) * COLS)
        solved_x[span, :] = turned[span, :].T


def row_reduced_kernel(ports, out):
    (
        coupling, near_ground, far_ground, near_source, far_source,
        low, high, low_sum, high_sum, low_smooth, high_smooth, low_cell, high_cell,
    ) = (ports[pl.ds(place, BLOCKS, stride=PORT), :] for place in range(13))
    block = lax.broadcasted_iota(jnp.int32, (BLOCKS, COLS), 0)
    block_first, block_last = block == 0, block == BLOCKS - 1
    low_end = 0.25 * (jnp.where(block_first, 0.0, pltpu.roll(high, 1, 0)) + low_sum)
    high_end = 0.25 * (high_sum + jnp.where(block_last, 0.0, pltpu.roll(low, BLOCKS - 1, 0)))
    enter = 1.0 / resistance(low_smooth - low_end)
    leave = 1.0 / resistance(high_end - high_smooth)
    across = pltpu.roll(low_end, BLOCKS - 1, 0) - high_end
    across = jnp.where(block_last, 0.0, 1.0 / resistance(across))
    zero = jnp.zeros_like(coupling)
    one = jnp.ones_like(coupling)
    before, at_low = join(
        (enter, one, zero, low_cell, zero), (coupling, near_ground, far_ground, near_source, far_source)
    )
    after, at_high = join((leave, zero, one, zero, high_cell), (across, zero, zero, zero, zero))
    whole, between = join(before, after)
    first = chain_solve(*whole, BLOCKS)
    later = pltpu.roll(first, BLOCKS - 1, 0)

    def middle(weights, left, right):
        return weights[0] * left + weights[1] * right + weights[2]

    out[:, 0, :] = first
    inner_high = middle(between, first, later)
    out[:, 1, :] = middle(at_low, first, inner_high)
    out[:, 2, :] = inner_high
    out[:, 3, :] = middle(at_high, inner_high, later)


def pick(flag, there, here):
    return tuple(jnp.where(flag, a, b) for a, b in zip(there, here))


def join_kernel(bit, own, other, out):
    upper = (lax.axis_index("depth") & bit) != 0
    mine = tuple(own[place] for place in range(5))
    theirs = tuple(other[place] for place in range(5))
    port, _ = join(pick(upper, theirs, mine), pick(upper, mine, theirs))
    for place, value in enumerate(port):
        out[place] = value


def finish_plane_kernel(
    own, near, pair, quad, factor, back, rest, mid, solved_x, out,
):
    index = lax.axis_index("depth")
    zero = jnp.zeros((ROWS, COLS), F32)
    left_ground, left_source, right_ground, right_source = zero, zero, zero, zero
    for bit, ref in ((4, quad), (2, pair), (1, near)):
        on_left = (index & bit) != 0
        c, ng, fg, ns, fs = (ref[place] for place in range(5))
        ground, source = ng + left_ground, ns + left_source
        share = c / (c + ground)
        left_ground = jnp.where(on_left, fg + share * ground, left_ground)
        left_source = jnp.where(on_left, fs + share * source, left_source)
        ground, source = fg + right_ground, fs + right_source
        total = c + ground
        share = jnp.where(total > 0.0, c / jnp.where(total > 0.0, total, 1.0), 0.0)
        right_ground = jnp.where(on_left, right_ground, ng + share * ground)
        right_source = jnp.where(on_left, right_source, ns + share * source)
    c, ng, fg, ns, fs = (own[place] for place in range(5))
    ground, source = fg + right_ground, fs + right_source
    total = c + ground
    inverse = jnp.where(total > 0.0, 1.0 / jnp.where(total > 0.0, total, 1.0), 0.0)
    share = c * inverse
    first = (left_source + ns + share * source) / (left_ground + ng + share * ground)
    after = share * first + source * inverse
    middle = mid[0] * first + mid[1] * after + mid[2]
    half = PLANES // 2
    for start, near_value, far_value in ((0, first, middle), (half, middle, after)):
        value = far_value
        for plane in range(start + half - 1, start, -1):
            span = slice(plane * ROWS, (plane + 1) * ROWS)
            value = factor[span, :] * value + (back[span, :] * near_value + rest[span, :])
            out[span, :] = solved_x[span, :] + value
        span = slice(start * ROWS, (start + 1) * ROWS)
        out[span, :] = solved_x[span, :] + near_value


def finish_row_kernel(solved, factor, back, rest, others, out):
    third = 1.0 / 3.0

    def put(row, value):
        place = pl.ds(row, PLANES, stride=ROWS)
        out[place, :] = (others[place, :] + value) * third

    for place, row in ((0, 0), (1, 1), (2, ROWS - 2), (3, ROWS - 1)):
        put(row, solved[:, place, :])
    first = solved[:, 1, :]
    value = solved[:, 2, :]
    for row in range(ROWS - 3, 1, -1):
        value = factor[row] * value + (back[row] * first + rest[row])
        put(row, value)


def call(kernel, outs, scratch=(), flops=1000000, moved=500000, **options):
    return pl.pallas_call(
        kernel,
        out_shape=outs,
        scratch_shapes=scratch,
        compiler_params=pltpu.CompilerParams(vmem_limit_bytes=16 * 1024 * 1024),
        cost_estimate=pl.CostEstimate(flops=flops, bytes_accessed=moved, transcendentals=0),
        **options,
    )


def shaped(*shape):
    return jax.ShapeDtypeStruct(shape, F32)


def line_perm(axis, step):
    count = lax.axis_size(axis)
    if step > 0:
        return [(i, i + 1) for i in range(count - 1)]
    return [(i + 1, i) for i in range(count - 1)]


def swap_perm(axis, bit):
    return [(i, i ^ bit) for i in range(lax.axis_size(axis))]


def next_perm(axis):
    pairs = []
    for i in range(1, lax.axis_size(axis) - 1, 2):
        pairs += [(i, i + 1), (i + 1, i)]
    return pairs


def shards(volume):
    flat = volume.reshape(PLANES * ROWS, COLS)
    lines = shaped(ROWS, PLANES, COLS)
    whole = shaped(PLANES * ROWS, COLS)
    tall = shaped((PLANES + 1) * ROWS, COLS)
    port = shaped(5, ROWS, COLS)
    side = shaped(PLANES + 1, COLS)
    to_near, to_far = call(
        edge_kernel,
        (shaped(2 * ROWS, COLS), shaped(2 * ROWS, COLS)),
        (pltpu.SemaphoreType.DMA((2,)),),
        in_specs=[pl.BlockSpec(memory_space=pl.ANY)],
    )(flat)
    far_side = lax.ppermute(to_far, "depth", next_perm("depth"))
    near_side = lax.ppermute(to_near, "depth", swap_perm("depth", 1))
    to_pair, to_next = call(
        side_kernel, (side, side), (pltpu.VMEM((40, COLS), F32), pltpu.VMEM((40, COLS), F32))
    )(flat, near_side, far_side)
    next_row = lax.ppermute(to_next, "lat", next_perm("lat"))
    pair_row = lax.ppermute(to_pair, "lat", swap_perm("lat", 1))
    y_port, y_factor, y_back, y_rest, deep = call(
        row_kernel,
        (shaped(PLANES * PORT, COLS), lines, lines, lines, tall),
        (pltpu.VMEM((PLANES + 3, ROWS, COLS), F32),),
    )(flat, near_side, far_side)
    ports = lax.all_to_all(y_port, "lat", 0, 0, tiled=True)
    z_port, z_factor, z_back, z_rest, z_mid, smooth = call(
        plane_kernel, (port, whole, whole, whole, shaped(3, ROWS, COLS), tall)
    )(flat, deep, pair_row, next_row)
    near = lax.ppermute(z_port, "depth", swap_perm("depth", 1))
    solved_x = call(
        column_kernel,
        whole,
        (
            pltpu.VMEM((512, COLS), F32),
            pltpu.VMEM((512, COLS), F32),
            pltpu.VMEM((16, 32, COLS), F32),
            pltpu.VMEM((16, 32, COLS), F32),
            pltpu.VMEM((16, 32, COLS), F32),
        ),
    )(flat, smooth)
    pair_own = call(lambda *refs: join_kernel(1, *refs), port)(z_port, near)
    ports, pair_own, solved_x = lax.optimization_barrier((ports, pair_own, solved_x))
    ends = call(row_reduced_kernel, shaped(BLOCKS, 4, COLS))(ports)
    ends, pair_own = lax.optimization_barrier((ends, pair_own))
    pair = lax.ppermute(pair_own, "depth", swap_perm("depth", 2))
    quad_own = call(lambda *refs: join_kernel(2, *refs), port)(pair_own, pair)
    quad = lax.ppermute(quad_own, "depth", swap_perm("depth", 6))
    others = call(finish_plane_kernel, whole)(
        z_port, near, pair, quad, z_factor, z_back, z_rest, z_mid, solved_x
    )
    ends_y = lax.all_to_all(ends, "lat", 0, 0, tiled=True)
    out = call(finish_row_kernel, whole)(ends_y, y_factor, y_back, y_rest, others)
    return out.reshape(PLANES, ROWS, COLS)


def solution(mesh):
    placed = (P("depth", "lat", None),)
    return jax.shard_map(
        shards, mesh=mesh, in_specs=placed, out_specs=P("depth", "lat", None), check_vma=False
    )
```

```python
import jax
import jax.numpy as jnp
from jax import lax
from jax.experimental import pallas as pl
from jax.experimental.pallas import tpu as pltpu
from jax.sharding import PartitionSpec as P

TAU3 = 900.0
INV_LAMBDA_SQ = 4.0
PLANES = 32
ROWS = 16
COLS = 128
BLOCKS = 32
PORT = 16
F32 = jnp.float32


def resistance(diff):
    return (1.0 + INV_LAMBDA_SQ * (diff * diff)) * (1.0 / TAU3)


def smooth_lanes(field, first, last):
    before = jnp.where(first, 0.0, pltpu.roll(field, 1, field.ndim - 1))
    after = jnp.where(last, 0.0, pltpu.roll(field, COLS - 1, field.ndim - 1))
    return 0.25 * (before + 2.0 * field + after)


def eliminate(coupling, ground, source, near_ground, near_source, resist):
    factor = 1.0 / (1.0 + (coupling + ground) * resist)
    weight = factor * resist
    back = coupling * weight
    near_ground = near_ground + back * ground
    near_source = near_source + back * source
    saved = (factor, back, source * weight)
    return coupling * factor, ground * factor, source * factor, near_ground, near_source, saved


def eliminate_last(coupling, ground, source, near_ground, near_source, conduct):
    inverse = 1.0 / (coupling + ground + conduct)
    factor = conduct * inverse
    back = coupling * inverse
    near_ground = near_ground + back * ground
    near_source = near_source + back * source
    saved = (factor, back, source * inverse)
    return coupling * factor, ground * factor, source * factor, near_ground, near_source, saved


def join(left, right):
    lc, lg, lh, ls, lt = left
    rc, rg, rh, rs, rt = right
    ground = lh + rg
    source = lt + rs
    inverse = 1.0 / (lc + rc + ground)
    to_left = lc * inverse
    to_right = rc * inverse
    return (
        lc * to_right,
        lg + to_left * ground,
        rh + to_right * ground,
        ls + to_left * source,
        rt + to_right * source,
    ), (to_left, to_right, source * inverse)


def edge_kernel(vol, near_side, far_side, sems):
    odd = lax.axis_index("depth") & 1
    high = (PLANES - 2) * ROWS
    near_start = pl.multiple_of((1 - odd) * high, ROWS)
    far_start = pl.multiple_of(odd * high, ROWS)
    copies = (
        pltpu.make_async_copy(vol.at[pl.ds(near_start, 2 * ROWS), :], near_side, sems.at[0]),
        pltpu.make_async_copy(vol.at[pl.ds(far_start, 2 * ROWS), :], far_side, sems.at[1]),
    )
    for copy in copies:
        copy.start()
    for copy in copies:
        copy.wait()


def strided(ref, row):
    return ref[pl.ds(row, 32, stride=16), :]


def cells(ref, plane):
    return ref[plane * ROWS : (plane + 1) * ROWS, :]


def faces(near_side, far_side):
    odd = (lax.axis_index("depth") & 1) == 1
    near, far = near_side[...], far_side[...]
    return jnp.where(odd, near, far)[ROWS:, :], jnp.where(odd, far, near)


def side_kernel(vol, near_side, far_side, pair_row, next_row, low_side, high_side):
    odd_row = (lax.axis_index("lat") & 1) == 1
    below, above = faces(near_side, far_side)
    lane = lax.broadcasted_iota(jnp.int32, (PLANES + 3, COLS), 1)
    sides = []
    for row, ref in ((0, low_side), (ROWS - 1, high_side)):
        ref[0:1, :] = below[row : row + 1, :]
        ref[1 : PLANES + 1, :] = vol[pl.ds(row, PLANES, stride=ROWS), :]
        ref[PLANES + 1 : PLANES + 2, :] = above[row : row + 1, :]
        ref[PLANES + 2 : PLANES + 3, :] = above[ROWS + row : ROWS + row + 1, :]
        ref[0 : PLANES + 3, :] = smooth_lanes(ref[0 : PLANES + 3, :], lane == 0, lane == COLS - 1)
        sides.append(
            0.25 * (ref[0 : PLANES + 1, :] + 2.0 * ref[1 : PLANES + 2, :] + ref[2 : PLANES + 3, :])
        )
    pair_row[...] = jnp.where(odd_row, sides[0], sides[1])
    next_row[...] = jnp.where(odd_row, sides[1], sides[0])


def plane_kernel(vol, deep, pair_row, next_row, port, factor, back, rest, mid, smooth):
    odd_row = (lax.axis_index("lat") & 1) == 1
    low_row = jnp.where(odd_row, pair_row[...], next_row[...])
    high_row = jnp.where(odd_row, next_row[...], pair_row[...])
    depth_last = lax.axis_index("depth") == lax.axis_size("depth") - 1
    z_open = jnp.where(depth_last, 0.0, TAU3).astype(F32)
    row_index = lax.broadcasted_iota(jnp.int32, (ROWS, COLS), 0)
    top, bottom = row_index == 0, row_index == ROWS - 1
    for plane in range(PLANES + 1):
        span = slice(plane * ROWS, (plane + 1) * ROWS)
        here = deep[span, :]
        above = jnp.where(top, low_row[plane : plane + 1, :], pltpu.roll(here, 1, 0))
        below = jnp.where(bottom, high_row[plane : plane + 1, :], pltpu.roll(here, ROWS - 1, 0))
        smooth[span, :] = 0.25 * (above + 2.0 * here + below)

    def resist(plane):
        return resistance(cells(smooth, plane + 1) - cells(smooth, plane))

    half = PLANES // 2
    one = jnp.ones((ROWS, COLS), F32)
    states = [
        (1.0 / resist(start), one, cells(vol, start + 1), one, cells(vol, start)) for start in (0, half)
    ]
    for step in range(1, half):
        final = step == half - 1
        for part in range(2):
            plane = part * half + step
            span = slice(plane * ROWS, (plane + 1) * ROWS)
            if final and part == 1:
                *state, saved = eliminate_last(*states[part], z_open / (TAU3 * resist(plane)))
            else:
                *state, saved = eliminate(*states[part], resist(plane))
            if not final:
                state[1] = state[1] + 1.0
                state[2] = state[2] + cells(vol, plane + 1)
            states[part] = state
            factor[span, :], back[span, :], rest[span, :] = saved
    joined, middle = join(*[(c, ng, fg, ns, fs) for c, fg, fs, ng, ns in states])
    for place, value in enumerate(joined):
        port[place] = value
    for place, value in enumerate(middle):
        mid[place] = value


def row_kernel(vol, near_side, far_side, port, factor, back, rest, deep, mixed):
    below, above = faces(near_side, far_side)
    lane = lax.broadcasted_iota(jnp.int32, (ROWS, COLS), 1)
    first, last = lane == 0, lane == COLS - 1
    mixed[0] = smooth_lanes(below, first, last)
    for plane in range(PLANES):
        mixed[plane + 1] = smooth_lanes(cells(vol, plane), first, last)
    for plane in range(2):
        mixed[PLANES + 1 + plane] = smooth_lanes(above[plane * ROWS : (plane + 1) * ROWS, :], first, last)
    for plane in range(PLANES + 1):
        deep[plane * ROWS : (plane + 1) * ROWS, :] = 0.25 * (
            mixed[plane] + 2.0 * mixed[plane + 1] + mixed[plane + 2]
        )
    part = [strided(deep, row) for row in range(ROWS)]
    low_sum = 2.0 * part[0] + part[1]
    high_sum = part[ROWS - 2] + 2.0 * part[ROWS - 1]
    smooth = [None] + [0.25 * (part[r - 1] + 2.0 * part[r] + part[r + 1]) for r in range(1, ROWS - 1)]
    one = jnp.ones((PLANES, COLS), F32)
    state = (1.0 / resistance(smooth[2] - smooth[1]), one, strided(vol, 2), one, strided(vol, 1))
    for row in range(2, ROWS - 2):
        *state, saved = eliminate(*state, resistance(smooth[row + 1] - smooth[row]))
        state[1] = state[1] + 1.0
        state[2] = state[2] + strided(vol, row + 1)
        factor[row], back[row], rest[row] = saved
    coupling, far_ground, far_source, near_ground, near_source = state
    values = (
        coupling, near_ground, far_ground, near_source, far_source,
        part[0], part[ROWS - 1], low_sum, high_sum, smooth[1], smooth[ROWS - 2],
        strided(vol, 0), strided(vol, ROWS - 1),
    )
    for place, value in enumerate(values):
        port[pl.ds(place, PLANES, stride=PORT), :] = value
    for place in range(len(values), PORT):
        port[pl.ds(place, PLANES, stride=PORT), :] = jnp.zeros((PLANES, COLS), F32)


def chain_solve(coupling, near_ground, far_ground, near_source, far_source, count):
    size = coupling.shape[0]
    right = coupling
    ground = near_ground + pltpu.roll(far_ground, 1, 0)
    source = near_source + pltpu.roll(far_source, 1, 0)
    step = 1
    while step < count:
        left = pltpu.roll(right, step, 0)
        inverse = 1.0 / (ground + left + right)
        ground_part = ground * inverse
        source_part = source * inverse
        ground = (
            ground
            + left * pltpu.roll(ground_part, step, 0)
            + right * pltpu.roll(ground_part, size - step, 0)
        )
        source = (
            source
            + left * pltpu.roll(source_part, step, 0)
            + right * pltpu.roll(source_part, size - step, 0)
        )
        right = right * pltpu.roll(right * inverse, size - step, 0)
        step *= 2
    return source / ground


def column_kernel(vol, smooth, solved_x, turned, turned_smooth, factor, back, rest):
    for group in range(4):
        span = slice(group * COLS, (group + 1) * COLS)
        turned[span, :] = vol[span, :].T
        turned_smooth[span, :] = smooth[span, :].T

    def resist(step):
        if step < 15:
            return resistance(strided(turned_smooth, step + 1) - strided(turned_smooth, step))
        return resistance(pltpu.roll(strided(turned_smooth, 0), 31, 0) - strided(turned_smooth, 15))

    chunk_last = (lax.broadcasted_iota(jnp.int32, (32, COLS), 0) & 7) == 7
    one = jnp.ones((32, COLS), F32)
    state = (1.0 / resist(0), one, strided(turned, 1), one, strided(turned, 0))
    for step in range(1, 16):
        if step == 15:
            *state, saved = eliminate_last(*state, jnp.where(chunk_last, 0.0, 1.0 / resist(step)))
        else:
            *state, saved = eliminate(*state, resist(step))
            state[1] = state[1] + 1.0
            state[2] = state[2] + strided(turned, step + 1)
        factor[step], back[step], rest[step] = saved
    coupling, far_ground, far_source, near_ground, near_source = state
    first = chain_solve(coupling, near_ground, far_ground, near_source, far_source, 8)
    turned[pl.ds(0, 32, stride=16), :] = first
    value = pltpu.roll(first, 31, 0)
    for step in range(15, 0, -1):
        value = factor[step] * value + (back[step] * first + rest[step])
        turned[pl.ds(step, 32, stride=16), :] = value
    for group in range(4):
        span = slice(group * COLS, (group + 1) * COLS)
        solved_x[span, :] = turned[span, :].T


def row_reduced_kernel(ports, out):
    (
        coupling, near_ground, far_ground, near_source, far_source,
        low, high, low_sum, high_sum, low_smooth, high_smooth, low_cell, high_cell,
    ) = (ports[pl.ds(place, BLOCKS, stride=PORT), :] for place in range(13))
    block = lax.broadcasted_iota(jnp.int32, (BLOCKS, COLS), 0)
    block_first, block_last = block == 0, block == BLOCKS - 1
    low_end = 0.25 * (jnp.where(block_first, 0.0, pltpu.roll(high, 1, 0)) + low_sum)
    high_end = 0.25 * (high_sum + jnp.where(block_last, 0.0, pltpu.roll(low, BLOCKS - 1, 0)))
    enter = 1.0 / resistance(low_smooth - low_end)
    leave = 1.0 / resistance(high_end - high_smooth)
    across = pltpu.roll(low_end, BLOCKS - 1, 0) - high_end
    across = jnp.where(block_last, 0.0, 1.0 / resistance(across))
    zero = jnp.zeros_like(coupling)
    one = jnp.ones_like(coupling)
    before, at_low = join(
        (enter, one, zero, low_cell, zero), (coupling, near_ground, far_ground, near_source, far_source)
    )
    after, at_high = join((leave, zero, one, zero, high_cell), (across, zero, zero, zero, zero))
    whole, between = join(before, after)
    first = chain_solve(*whole, BLOCKS)
    later = pltpu.roll(first, BLOCKS - 1, 0)

    def middle(weights, left, right):
        return weights[0] * left + weights[1] * right + weights[2]

    out[:, 0, :] = first
    inner_high = middle(between, first, later)
    out[:, 1, :] = middle(at_low, first, inner_high)
    out[:, 2, :] = inner_high
    out[:, 3, :] = middle(at_high, inner_high, later)


def pick(flag, there, here):
    return tuple(jnp.where(flag, a, b) for a, b in zip(there, here))


def join_kernel(bit, own, other, out):
    upper = (lax.axis_index("depth") & bit) != 0
    mine = tuple(own[place] for place in range(5))
    theirs = tuple(other[place] for place in range(5))
    port, _ = join(pick(upper, theirs, mine), pick(upper, mine, theirs))
    for place, value in enumerate(port):
        out[place] = value


def finish_plane_kernel(
    own, near, pair, quad, factor, back, rest, mid, solved_x, out,
):
    index = lax.axis_index("depth")
    zero = jnp.zeros((ROWS, COLS), F32)
    left_ground, left_source, right_ground, right_source = zero, zero, zero, zero
    for bit, ref in ((4, quad), (2, pair), (1, near)):
        on_left = (index & bit) != 0
        c, ng, fg, ns, fs = (ref[place] for place in range(5))
        ground, source = ng + left_ground, ns + left_source
        share = c / (c + ground)
        left_ground = jnp.where(on_left, fg + share * ground, left_ground)
        left_source = jnp.where(on_left, fs + share * source, left_source)
        ground, source = fg + right_ground, fs + right_source
        total = c + ground
        share = jnp.where(total > 0.0, c / jnp.where(total > 0.0, total, 1.0), 0.0)
        right_ground = jnp.where(on_left, right_ground, ng + share * ground)
        right_source = jnp.where(on_left, right_source, ns + share * source)
    c, ng, fg, ns, fs = (own[place] for place in range(5))
    ground, source = fg + right_ground, fs + right_source
    total = c + ground
    inverse = jnp.where(total > 0.0, 1.0 / jnp.where(total > 0.0, total, 1.0), 0.0)
    share = c * inverse
    first = (left_source + ns + share * source) / (left_ground + ng + share * ground)
    after = share * first + source * inverse
    middle = mid[0] * first + mid[1] * after + mid[2]
    half = PLANES // 2
    for start, near_value, far_value in ((0, first, middle), (half, middle, after)):
        value = far_value
        for plane in range(start + half - 1, start, -1):
            span = slice(plane * ROWS, (plane + 1) * ROWS)
            value = factor[span, :] * value + (back[span, :] * near_value + rest[span, :])
            out[span, :] = solved_x[span, :] + value
        span = slice(start * ROWS, (start + 1) * ROWS)
        out[span, :] = solved_x[span, :] + near_value


def finish_row_kernel(solved, factor, back, rest, others, out):
    third = 1.0 / 3.0

    def put(row, value):
        place = pl.ds(row, PLANES, stride=ROWS)
        out[place, :] = (others[place, :] + value) * third

    for place, row in ((0, 0), (1, 1), (2, ROWS - 2), (3, ROWS - 1)):
        put(row, solved[:, place, :])
    first = solved[:, 1, :]
    value = solved[:, 2, :]
    for row in range(ROWS - 3, 1, -1):
        value = factor[row] * value + (back[row] * first + rest[row])
        put(row, value)


def call(kernel, outs, scratch=(), flops=1000000, moved=500000, **options):
    return pl.pallas_call(
        kernel,
        out_shape=outs,
        scratch_shapes=scratch,
        compiler_params=pltpu.CompilerParams(vmem_limit_bytes=16 * 1024 * 1024),
        cost_estimate=pl.CostEstimate(flops=flops, bytes_accessed=moved, transcendentals=0),
        **options,
    )


def shaped(*shape):
    return jax.ShapeDtypeStruct(shape, F32)


def line_perm(axis, step):
    count = lax.axis_size(axis)
    if step > 0:
        return [(i, i + 1) for i in range(count - 1)]
    return [(i + 1, i) for i in range(count - 1)]


def swap_perm(axis, bit):
    return [(i, i ^ bit) for i in range(lax.axis_size(axis))]


def next_perm(axis):
    pairs = []
    for i in range(1, lax.axis_size(axis) - 1, 2):
        pairs += [(i, i + 1), (i + 1, i)]
    return pairs


def shards(volume):
    flat = volume.reshape(PLANES * ROWS, COLS)
    lines = shaped(ROWS, PLANES, COLS)
    whole = shaped(PLANES * ROWS, COLS)
    tall = shaped((PLANES + 1) * ROWS, COLS)
    port = shaped(5, ROWS, COLS)
    side = shaped(PLANES + 1, COLS)
    to_near, to_far = call(
        edge_kernel,
        (shaped(2 * ROWS, COLS), shaped(2 * ROWS, COLS)),
        (pltpu.SemaphoreType.DMA((2,)),),
        in_specs=[pl.BlockSpec(memory_space=pl.ANY)],
    )(flat)
    far_side = lax.ppermute(to_far, "depth", next_perm("depth"))
    near_side = lax.ppermute(to_near, "depth", swap_perm("depth", 1))
    to_pair, to_next = call(
        side_kernel, (side, side), (pltpu.VMEM((40, COLS), F32), pltpu.VMEM((40, COLS), F32))
    )(flat, near_side, far_side)
    next_row = lax.ppermute(to_next, "lat", next_perm("lat"))
    pair_row = lax.ppermute(to_pair, "lat", swap_perm("lat", 1))
    y_port, y_factor, y_back, y_rest, deep = call(
        row_kernel,
        (shaped(PLANES * PORT, COLS), lines, lines, lines, tall),
        (pltpu.VMEM((PLANES + 3, ROWS, COLS), F32),),
    )(flat, near_side, far_side)
    ports = lax.all_to_all(y_port, "lat", 0, 0, tiled=True)
    z_port, z_factor, z_back, z_rest, z_mid, smooth = call(
        plane_kernel, (port, whole, whole, whole, shaped(3, ROWS, COLS), tall)
    )(flat, deep, pair_row, next_row)
    near = lax.ppermute(z_port, "depth", swap_perm("depth", 1))
    solved_x = call(
        column_kernel,
        whole,
        (
            pltpu.VMEM((512, COLS), F32),
            pltpu.VMEM((512, COLS), F32),
            pltpu.VMEM((16, 32, COLS), F32),
            pltpu.VMEM((16, 32, COLS), F32),
            pltpu.VMEM((16, 32, COLS), F32),
        ),
    )(flat, smooth)
    pair_own = call(lambda *refs: join_kernel(1, *refs), port)(z_port, near)
    ports, pair_own, solved_x = lax.optimization_barrier((ports, pair_own, solved_x))
    ends = call(row_reduced_kernel, shaped(BLOCKS, 4, COLS))(ports)
    ends, pair_own = lax.optimization_barrier((ends, pair_own))
    pair = lax.ppermute(pair_own, "depth", swap_perm("depth", 2))
    quad_own = call(lambda *refs: join_kernel(2, *refs), port)(pair_own, pair)
    quad = lax.ppermute(quad_own, "depth", swap_perm("depth", 4))
    others = call(finish_plane_kernel, whole)(
        z_port, near, pair, quad, z_factor, z_back, z_rest, z_mid, solved_x
    )
    ends_y = lax.all_to_all(ends, "lat", 0, 0, tiled=True)
    out = call(finish_row_kernel, whole)(ends_y, y_factor, y_back, y_rest, others)
    return out.reshape(PLANES, ROWS, COLS)


def solution(mesh):
    placed = (P("depth", "lat", None),)
    return jax.shard_map(
        shards, mesh=mesh, in_specs=placed, out_specs=P("depth", "lat", None), check_vma=False
    )
```

```python
import jax
import jax.numpy as jnp
from jax import lax
from jax.experimental import pallas as pl
from jax.experimental.pallas import tpu as pltpu
from jax.sharding import PartitionSpec as P

TAU3 = 900.0
INV_LAMBDA_SQ = 4.0
PLANES = 32
ROWS = 16
COLS = 128
BLOCKS = 32
PORT = 16
F32 = jnp.float32


def resistance(diff):
    return (1.0 + INV_LAMBDA_SQ * (diff * diff)) * (1.0 / TAU3)


def smooth_lanes(field, first, last):
    before = jnp.where(first, 0.0, pltpu.roll(field, 1, field.ndim - 1))
    after = jnp.where(last, 0.0, pltpu.roll(field, COLS - 1, field.ndim - 1))
    return 0.25 * (before + 2.0 * field + after)


def eliminate(coupling, ground, source, near_ground, near_source, resist):
    factor = 1.0 / (1.0 + (coupling + ground) * resist)
    weight = factor * resist
    back = coupling * weight
    near_ground = near_ground + back * ground
    near_source = near_source + back * source
    saved = (factor, back, source * weight)
    return coupling * factor, ground * factor, source * factor, near_ground, near_source, saved


def eliminate_last(coupling, ground, source, near_ground, near_source, conduct):
    inverse = 1.0 / (coupling + ground + conduct)
    factor = conduct * inverse
    back = coupling * inverse
    near_ground = near_ground + back * ground
    near_source = near_source + back * source
    saved = (factor, back, source * inverse)
    return coupling * factor, ground * factor, source * factor, near_ground, near_source, saved


def join(left, right):
    lc, lg, lh, ls, lt = left
    rc, rg, rh, rs, rt = right
    ground = lh + rg
    source = lt + rs
    inverse = 1.0 / (lc + rc + ground)
    to_left = lc * inverse
    to_right = rc * inverse
    return (
        lc * to_right,
        lg + to_left * ground,
        rh + to_right * ground,
        ls + to_left * source,
        rt + to_right * source,
    ), (to_left, to_right, source * inverse)


def strided(ref, row):
    return ref[pl.ds(row, 32, stride=16), :]


def cells(ref, plane):
    return ref[plane * ROWS : (plane + 1) * ROWS, :]


def faces(near_side, far_side):
    odd = (lax.axis_index("depth") & 1) == 1
    near, far = near_side[...], far_side[...]
    return jnp.where(odd, near, far)[ROWS:, :], jnp.where(odd, far, near)


def side_kernel(vol, near_side, far_side, pair_row, next_row, low_side, high_side):
    odd_row = (lax.axis_index("lat") & 1) == 1
    below, above = faces(near_side, far_side)
    lane = lax.broadcasted_iota(jnp.int32, (PLANES + 3, COLS), 1)
    sides = []
    for row, ref in ((0, low_side), (ROWS - 1, high_side)):
        ref[0:1, :] = below[row : row + 1, :]
        ref[1 : PLANES + 1, :] = vol[pl.ds(row, PLANES, stride=ROWS), :]
        ref[PLANES + 1 : PLANES + 2, :] = above[row : row + 1, :]
        ref[PLANES + 2 : PLANES + 3, :] = above[ROWS + row : ROWS + row + 1, :]
        ref[0 : PLANES + 3, :] = smooth_lanes(ref[0 : PLANES + 3, :], lane == 0, lane == COLS - 1)
        sides.append(
            0.25 * (ref[0 : PLANES + 1, :] + 2.0 * ref[1 : PLANES + 2, :] + ref[2 : PLANES + 3, :])
        )
    pair_row[...] = jnp.where(odd_row, sides[0], sides[1])
    next_row[...] = jnp.where(odd_row, sides[1], sides[0])


def plane_kernel(vol, deep, pair_row, next_row, port, factor, back, rest, mid, smooth):
    odd_row = (lax.axis_index("lat") & 1) == 1
    low_row = jnp.where(odd_row, pair_row[...], next_row[...])
    high_row = jnp.where(odd_row, next_row[...], pair_row[...])
    depth_last = lax.axis_index("depth") == lax.axis_size("depth") - 1
    z_open = jnp.where(depth_last, 0.0, TAU3).astype(F32)
    row_index = lax.broadcasted_iota(jnp.int32, (ROWS, COLS), 0)
    top, bottom = row_index == 0, row_index == ROWS - 1
    for plane in range(PLANES + 1):
        span = slice(plane * ROWS, (plane + 1) * ROWS)
        here = deep[span, :]
        above = jnp.where(top, low_row[plane : plane + 1, :], pltpu.roll(here, 1, 0))
        below = jnp.where(bottom, high_row[plane : plane + 1, :], pltpu.roll(here, ROWS - 1, 0))
        smooth[span, :] = 0.25 * (above + 2.0 * here + below)

    def resist(plane):
        return resistance(cells(smooth, plane + 1) - cells(smooth, plane))

    half = PLANES // 2
    one = jnp.ones((ROWS, COLS), F32)
    states = [
        (1.0 / resist(start), one, cells(vol, start + 1), one, cells(vol, start)) for start in (0, half)
    ]
    for step in range(1, half):
        final = step == half - 1
        for part in range(2):
            plane = part * half + step
            span = slice(plane * ROWS, (plane + 1) * ROWS)
            if final and part == 1:
                *state, saved = eliminate_last(*states[part], z_open / (TAU3 * resist(plane)))
            else:
                *state, saved = eliminate(*states[part], resist(plane))
            if not final:
                state[1] = state[1] + 1.0
                state[2] = state[2] + cells(vol, plane + 1)
            states[part] = state
            factor[span, :], back[span, :], rest[span, :] = saved
    joined, middle = join(*[(c, ng, fg, ns, fs) for c, fg, fs, ng, ns in states])
    for place, value in enumerate(joined):
        port[place] = value
    for place, value in enumerate(middle):
        mid[place] = value


def row_kernel(vol, near_side, far_side, port, factor, back, rest, deep, mixed):
    below, above = faces(near_side, far_side)
    lane = lax.broadcasted_iota(jnp.int32, (ROWS, COLS), 1)
    first, last = lane == 0, lane == COLS - 1
    mixed[0] = smooth_lanes(below, first, last)
    for plane in range(PLANES):
        mixed[plane + 1] = smooth_lanes(cells(vol, plane), first, last)
    for plane in range(2):
        mixed[PLANES + 1 + plane] = smooth_lanes(above[plane * ROWS : (plane + 1) * ROWS, :], first, last)
    for plane in range(PLANES + 1):
        deep[plane * ROWS : (plane + 1) * ROWS, :] = 0.25 * (
            mixed[plane] + 2.0 * mixed[plane + 1] + mixed[plane + 2]
        )
    part = [strided(deep, row) for row in range(ROWS)]
    low_sum = 2.0 * part[0] + part[1]
    high_sum = part[ROWS - 2] + 2.0 * part[ROWS - 1]
    smooth = [None] + [0.25 * (part[r - 1] + 2.0 * part[r] + part[r + 1]) for r in range(1, ROWS - 1)]
    one = jnp.ones((PLANES, COLS), F32)
    state = (1.0 / resistance(smooth[2] - smooth[1]), one, strided(vol, 2), one, strided(vol, 1))
    for row in range(2, ROWS - 2):
        *state, saved = eliminate(*state, resistance(smooth[row + 1] - smooth[row]))
        state[1] = state[1] + 1.0
        state[2] = state[2] + strided(vol, row + 1)
        factor[row], back[row], rest[row] = saved
    coupling, far_ground, far_source, near_ground, near_source = state
    values = (
        coupling, near_ground, far_ground, near_source, far_source,
        part[0], part[ROWS - 1], low_sum, high_sum, smooth[1], smooth[ROWS - 2],
        strided(vol, 0), strided(vol, ROWS - 1),
    )
    for place, value in enumerate(values):
        port[pl.ds(place, PLANES, stride=PORT), :] = value
    for place in range(len(values), PORT):
        port[pl.ds(place, PLANES, stride=PORT), :] = jnp.zeros((PLANES, COLS), F32)


def chain_solve(coupling, near_ground, far_ground, near_source, far_source, count):
    size = coupling.shape[0]
    right = coupling
    ground = near_ground + pltpu.roll(far_ground, 1, 0)
    source = near_source + pltpu.roll(far_source, 1, 0)
    step = 1
    while step < count:
        left = pltpu.roll(right, step, 0)
        inverse = 1.0 / (ground + left + right)
        ground_part = ground * inverse
        source_part = source * inverse
        ground = (
            ground
            + left * pltpu.roll(ground_part, step, 0)
            + right * pltpu.roll(ground_part, size - step, 0)
        )
        source = (
            source
            + left * pltpu.roll(source_part, step, 0)
            + right * pltpu.roll(source_part, size - step, 0)
        )
        right = right * pltpu.roll(right * inverse, size - step, 0)
        step *= 2
    return source / ground


def column_kernel(vol, smooth, solved_x, turned, turned_smooth, factor, back, rest):
    for group in range(4):
        span = slice(group * COLS, (group + 1) * COLS)
        turned[span, :] = vol[span, :].T
        turned_smooth[span, :] = smooth[span, :].T

    def resist(step):
        if step < 15:
            return resistance(strided(turned_smooth, step + 1) - strided(turned_smooth, step))
        return resistance(pltpu.roll(strided(turned_smooth, 0), 31, 0) - strided(turned_smooth, 15))

    chunk_last = (lax.broadcasted_iota(jnp.int32, (32, COLS), 0) & 7) == 7
    one = jnp.ones((32, COLS), F32)
    state = (1.0 / resist(0), one, strided(turned, 1), one, strided(turned, 0))
    for step in range(1, 16):
        if step == 15:
            *state, saved = eliminate_last(*state, jnp.where(chunk_last, 0.0, 1.0 / resist(step)))
        else:
            *state, saved = eliminate(*state, resist(step))
            state[1] = state[1] + 1.0
            state[2] = state[2] + strided(turned, step + 1)
        factor[step], back[step], rest[step] = saved
    coupling, far_ground, far_source, near_ground, near_source = state
    first = chain_solve(coupling, near_ground, far_ground, near_source, far_source, 8)
    turned[pl.ds(0, 32, stride=16), :] = first
    value = pltpu.roll(first, 31, 0)
    for step in range(15, 0, -1):
        value = factor[step] * value + (back[step] * first + rest[step])
        turned[pl.ds(step, 32, stride=16), :] = value
    for group in range(4):
        span = slice(group * COLS, (group + 1) * COLS)
        solved_x[span, :] = turned[span, :].T


def row_reduced_kernel(ports, out):
    (
        coupling, near_ground, far_ground, near_source, far_source,
        low, high, low_sum, high_sum, low_smooth, high_smooth, low_cell, high_cell,
    ) = (ports[pl.ds(place, BLOCKS, stride=PORT), :] for place in range(13))
    block = lax.broadcasted_iota(jnp.int32, (BLOCKS, COLS), 0)
    block_first, block_last = block == 0, block == BLOCKS - 1
    low_end = 0.25 * (jnp.where(block_first, 0.0, pltpu.roll(high, 1, 0)) + low_sum)
    high_end = 0.25 * (high_sum + jnp.where(block_last, 0.0, pltpu.roll(low, BLOCKS - 1, 0)))
    enter = 1.0 / resistance(low_smooth - low_end)
    leave = 1.0 / resistance(high_end - high_smooth)
    across = pltpu.roll(low_end, BLOCKS - 1, 0) - high_end
    across = jnp.where(block_last, 0.0, 1.0 / resistance(across))
    zero = jnp.zeros_like(coupling)
    one = jnp.ones_like(coupling)
    before, at_low = join(
        (enter, one, zero, low_cell, zero), (coupling, near_ground, far_ground, near_source, far_source)
    )
    after, at_high = join((leave, zero, one, zero, high_cell), (across, zero, zero, zero, zero))
    whole, between = join(before, after)
    first = chain_solve(*whole, BLOCKS)
    later = pltpu.roll(first, BLOCKS - 1, 0)

    def middle(weights, left, right):
        return weights[0] * left + weights[1] * right + weights[2]

    out[:, 0, :] = first
    inner_high = middle(between, first, later)
    out[:, 1, :] = middle(at_low, first, inner_high)
    out[:, 2, :] = inner_high
    out[:, 3, :] = middle(at_high, inner_high, later)


def pick(flag, there, here):
    return tuple(jnp.where(flag, a, b) for a, b in zip(there, here))


def join_kernel(bit, own, other, out):
    upper = (lax.axis_index("depth") & bit) != 0
    mine = tuple(own[place] for place in range(5))
    theirs = tuple(other[place] for place in range(5))
    port, _ = join(pick(upper, theirs, mine), pick(upper, mine, theirs))
    for place, value in enumerate(port):
        out[place] = value


def finish_plane_kernel(
    own, near, pair, quad, factor, back, rest, mid, solved_x, out,
):
    index = lax.axis_index("depth")
    zero = jnp.zeros((ROWS, COLS), F32)
    left_ground, left_source, right_ground, right_source = zero, zero, zero, zero
    for bit, ref in ((4, quad), (2, pair), (1, near)):
        on_left = (index & bit) != 0
        c, ng, fg, ns, fs = (ref[place] for place in range(5))
        ground, source = ng + left_ground, ns + left_source
        share = c / (c + ground)
        left_ground = jnp.where(on_left, fg + share * ground, left_ground)
        left_source = jnp.where(on_left, fs + share * source, left_source)
        ground, source = fg + right_ground, fs + right_source
        total = c + ground
        share = jnp.where(total > 0.0, c / jnp.where(total > 0.0, total, 1.0), 0.0)
        right_ground = jnp.where(on_left, right_ground, ng + share * ground)
        right_source = jnp.where(on_left, right_source, ns + share * source)
    c, ng, fg, ns, fs = (own[place] for place in range(5))
    ground, source = fg + right_ground, fs + right_source
    total = c + ground
    inverse = jnp.where(total > 0.0, 1.0 / jnp.where(total > 0.0, total, 1.0), 0.0)
    share = c * inverse
    first = (left_source + ns + share * source) / (left_ground + ng + share * ground)
    after = share * first + source * inverse
    middle = mid[0] * first + mid[1] * after + mid[2]
    half = PLANES // 2
    for start, near_value, far_value in ((0, first, middle), (half, middle, after)):
        value = far_value
        for plane in range(start + half - 1, start, -1):
            span = slice(plane * ROWS, (plane + 1) * ROWS)
            value = factor[span, :] * value + (back[span, :] * near_value + rest[span, :])
            out[span, :] = solved_x[span, :] + value
        span = slice(start * ROWS, (start + 1) * ROWS)
        out[span, :] = solved_x[span, :] + near_value


def finish_row_kernel(solved, factor, back, rest, others, out):
    third = 1.0 / 3.0

    def put(row, value):
        place = pl.ds(row, PLANES, stride=ROWS)
        out[place, :] = (others[place, :] + value) * third

    for place, row in ((0, 0), (1, 1), (2, ROWS - 2), (3, ROWS - 1)):
        put(row, solved[:, place, :])
    first = solved[:, 1, :]
    value = solved[:, 2, :]
    for row in range(ROWS - 3, 1, -1):
        value = factor[row] * value + (back[row] * first + rest[row])
        put(row, value)


def call(kernel, outs, scratch=(), flops=1000000, moved=500000, **options):
    return pl.pallas_call(
        kernel,
        out_shape=outs,
        scratch_shapes=scratch,
        compiler_params=pltpu.CompilerParams(vmem_limit_bytes=16 * 1024 * 1024),
        cost_estimate=pl.CostEstimate(flops=flops, bytes_accessed=moved, transcendentals=0),
        **options,
    )


def shaped(*shape):
    return jax.ShapeDtypeStruct(shape, F32)


def line_perm(axis, step):
    count = lax.axis_size(axis)
    if step > 0:
        return [(i, i + 1) for i in range(count - 1)]
    return [(i + 1, i) for i in range(count - 1)]


def swap_perm(axis, bit):
    return [(i, i ^ bit) for i in range(lax.axis_size(axis))]


def next_perm(axis):
    pairs = []
    for i in range(1, lax.axis_size(axis) - 1, 2):
        pairs += [(i, i + 1), (i + 1, i)]
    return pairs


def shards(volume):
    flat = volume.reshape(PLANES * ROWS, COLS)
    lines = shaped(ROWS, PLANES, COLS)
    whole = shaped(PLANES * ROWS, COLS)
    tall = shaped((PLANES + 1) * ROWS, COLS)
    port = shaped(5, ROWS, COLS)
    side = shaped(PLANES + 1, COLS)
    odd = (lax.axis_index("depth") & 1) == 1
    low_planes, high_planes = flat[: 2 * ROWS], flat[(PLANES - 2) * ROWS :]
    to_near = jnp.where(odd, low_planes, high_planes)
    to_far = jnp.where(odd, high_planes, low_planes)
    far_side = lax.ppermute(to_far, "depth", next_perm("depth"))
    near_side = lax.ppermute(to_near, "depth", swap_perm("depth", 1))
    to_pair, to_next = call(
        side_kernel, (side, side), (pltpu.VMEM((40, COLS), F32), pltpu.VMEM((40, COLS), F32))
    )(flat, near_side, far_side)
    next_row = lax.ppermute(to_next, "lat", next_perm("lat"))
    pair_row = lax.ppermute(to_pair, "lat", swap_perm("lat", 1))
    y_port, y_factor, y_back, y_rest, deep = call(
        row_kernel,
        (shaped(PLANES * PORT, COLS), lines, lines, lines, tall),
        (pltpu.VMEM((PLANES + 3, ROWS, COLS), F32),),
    )(flat, near_side, far_side)
    ports = lax.all_to_all(y_port, "lat", 0, 0, tiled=True)
    z_port, z_factor, z_back, z_rest, z_mid, smooth = call(
        plane_kernel, (port, whole, whole, whole, shaped(3, ROWS, COLS), tall)
    )(flat, deep, pair_row, next_row)
    near = lax.ppermute(z_port, "depth", swap_perm("depth", 1))
    solved_x = call(
        column_kernel,
        whole,
        (
            pltpu.VMEM((512, COLS), F32),
            pltpu.VMEM((512, COLS), F32),
            pltpu.VMEM((16, 32, COLS), F32),
            pltpu.VMEM((16, 32, COLS), F32),
            pltpu.VMEM((16, 32, COLS), F32),
        ),
    )(flat, smooth)
    pair_own = call(lambda *refs: join_kernel(1, *refs), port)(z_port, near)
    ports, pair_own, solved_x = lax.optimization_barrier((ports, pair_own, solved_x))
    ends = call(row_reduced_kernel, shaped(BLOCKS, 4, COLS))(ports)
    ends, pair_own = lax.optimization_barrier((ends, pair_own))
    pair = lax.ppermute(pair_own, "depth", swap_perm("depth", 2))
    quad_own = call(lambda *refs: join_kernel(2, *refs), port)(pair_own, pair)
    quad = lax.ppermute(quad_own, "depth", swap_perm("depth", 6))
    others = call(finish_plane_kernel, whole)(
        z_port, near, pair, quad, z_factor, z_back, z_rest, z_mid, solved_x
    )
    ends_y = lax.all_to_all(ends, "lat", 0, 0, tiled=True)
    out = call(finish_row_kernel, whole)(ends_y, y_factor, y_back, y_rest, others)
    return out.reshape(PLANES, ROWS, COLS)


def solution(mesh):
    placed = (P("depth", "lat", None),)
    return jax.shard_map(
        shards, mesh=mesh, in_specs=placed, out_specs=P("depth", "lat", None), check_vma=False
    )
```
